128 devices in a mesh: rows: 16 (over z_lo, x, core), cols: 8 (over z_hi, y).
Axes of the slice: x: 4, y: 4, z: 4 (z_hi: 2, z_lo: 2; z = z_hi * 2 + z_lo), core: 2. Of those that a mesh axis runs over, the one named last changes fastest.
Arguments:
- spectrum: bfloat16 [2, 4096, 4096], P(None, 'rows', 'cols'), may hold values from -6 to 6
- diffraction: bfloat16 [2, 32, 3, 128, 128], P(None, 'rows'), may hold values from -0.21875 to 0.21875
- order_mask: int32 [32, 3], P('rows'), may hold values from 0 to 1, as said below
- phases: float32 [2, 4096, 4096], P(None, 'rows', 'cols'), may hold values from -3.140625 to 3.140625
- transmission: float32 [4096, 4096], P('rows', 'cols'), may hold values from 0.2 to 1
- shifts: int32 [2], replicated, may hold values from 128 to 256, as said below
Outputs:
- outgoing: float32 [2, 4096, 4096], P(None, 'rows', 'cols')
The draws below stay inside these ranges and needn't reach their ends.
Inputs may be any that keep to these rules, and one draw needn't show every extreme that they name: Each bounce's shift lies between 128 and 256; one bounce shifts by exactly 256. `order_mask`: every block carries the orders -1 and +1; the order 0 is off in some blocks.
All inputs are finite; a program needn't handle non-finite values.
Results may differ from the reference program's by a relative error of at most 0.018.
Values may be sent and summed in bfloat16 or wider, within the bound.
A program may use at most 128 MiB of HBM per device.

```python
import math
import jax
import jax.numpy as jnp
from jax import lax

NX = 4096
NY = 4096
BLOCK = 128
BASE = 256
BOUNCES = 2
NBLK = 32
GMAX = 256


def draw_shifts(key, part):
    first_key = jax.random.fold_in(key, 11)
    second_key = jax.random.fold_in(key, 23)
    drawn = jax.random.randint(first_key, (BOUNCES,), GMAX // 2, GMAX + 1)
    chosen = jax.random.randint(second_key, (), 0, BOUNCES)
    return jnp.where(jnp.arange(BOUNCES) == chosen, GMAX, drawn).astype(jnp.int32)


def draw_order_mask(key, part):
    first_key = jax.random.fold_in(key, 37)
    second_key = jax.random.fold_in(key, 41)
    middle = jax.random.randint(first_key, (NBLK,), 0, 2)
    chosen = jax.random.randint(second_key, (), 0, NBLK)
    middle = jnp.where(jnp.arange(NBLK) == chosen, 0, middle)
    sides = jnp.ones((NBLK,), jnp.int32)
    return jnp.stack([sides, middle, sides], axis=1).astype(jnp.int32)


def block_levels(own_key, shape, cuts, least, top_value):
    factor_of, own = 1.0, jax.random.fold_in(own_key, 6)
    for dim, blocks in cuts:
        steps = jnp.exp(jax.random.uniform(jax.random.fold_in(own, dim), (blocks,), jnp.float32, least / len(cuts), top_value / len(cuts)))
        factor_of = factor_of * jnp.repeat(steps, shape[dim] // blocks).reshape([-1 if axis == dim else 1 for axis in range(len(shape))])
    return factor_of


def normal_values(stream_key, dims, spread, most, split=(), kind=jnp.bfloat16):
    values = jax.random.normal(stream_key, dims, jnp.float32) * spread
    if len(split) > 0:
        values = block_levels(stream_key, dims, split, -0.22, 0.18) * values
    return jnp.clip(values, min=-most, max=most).astype(kind)


def setup_inputs(seed: int = 0) -> dict:
    key_list = jax.random.split(jax.random.key(seed), 7)
    spectrum = normal_values(key_list[0], (2, NX, NY), 1.0, 6.0, ((1, 16), (2, 8)))
    diffraction = normal_values(key_list[1], (2, NBLK, 3, BLOCK, BLOCK), (6 * BLOCK) ** -0.5, 0.21875, ((1, 16),))
    order_mask = draw_order_mask(jax.random.fold_in(key_list[6], 71), 0)
    phases = jnp.clip(jax.random.uniform(key_list[3], (BOUNCES, NX, NY), jnp.float32, -3.140625, 3.140625), -3.140625, 3.140625)
    transmission = jnp.clip(0.2 + 0.8 * jax.random.uniform(key_list[4], (NX, NY), jnp.float32) ** block_levels(key_list[4], (NX, NY), ((0, 16), (1, 8)), -0.2, 0.2), 0.2, 1.0)
    shifts = draw_shifts(jax.random.fold_in(key_list[6], 71), 0)
    return dict(spectrum=spectrum, diffraction=diffraction, order_mask=order_mask, phases=phases, transmission=transmission, shifts=shifts)


def rounded(values):
    return lax.optimization_barrier(values.astype(jnp.bfloat16))

def twiddles(extent, sign_value, left_index, right_index):
    wrapped = left_index[:, None] * right_index[None, :] % extent
    angles = wrapped.astype(jnp.float32) * (2.0 * math.pi / extent)
    return (jnp.cos(angles), sign_value * jnp.sin(angles))

def product(left_side, right_side):
    return jnp.dot(left_side, right_side, precision=lax.Precision.HIGHEST, preferred_element_type=jnp.float32)

def transform_first(values, sign_value):
    extent = values.shape[1]
    others = values.shape[2]
    target = jnp.arange(extent, dtype=jnp.int32)
    base_real, base_imag = twiddles(extent, sign_value, jnp.arange(BASE, dtype=jnp.int32), target)
    factor = 1.0 / math.sqrt(extent)
    base_real = rounded(base_real * factor).astype(jnp.float32).T
    base_imag = rounded(base_imag * factor).astype(jnp.float32).T
    blocked = values.astype(jnp.float32).reshape(2, extent // BASE, BASE, others).transpose(1, 0, 2, 3)

    def advance(running, element):
        number, segment = element
        inner_real = product(base_real, segment[0]) - product(base_imag, segment[1])
        inner_imag = product(base_imag, segment[0]) + product(base_real, segment[1])
        turn_real, turn_imag = twiddles(extent, sign_value, (number * BASE)[None], target)
        turn_real = turn_real[0][:, None]
        turn_imag = turn_imag[0][:, None]
        next_real = running[0] + turn_real * inner_real - turn_imag * inner_imag
        next_imag = running[1] + turn_real * inner_imag + turn_imag * inner_real
        return ((next_real, next_imag), number)
    initial = (jnp.zeros((extent, others), jnp.float32), jnp.zeros((extent, others), jnp.float32))
    numbers = jnp.arange(extent // BASE, dtype=jnp.int32)
    finished, ignored = lax.scan(advance, initial, (numbers, blocked))
    return jnp.stack([finished[0], finished[1]])

def transform_second(values, sign_value):
    return jnp.swapaxes(transform_first(jnp.swapaxes(values, 1, 2), sign_value), 1, 2)

def apply_blocks(left_side, right_side):
    return jnp.einsum('bjk,bkq->bjq', left_side, right_side, precision=lax.Precision.HIGHEST, preferred_element_type=jnp.float32)

def diffract(current, matrices, weights, offset_step):
    padded = jnp.pad(current, ((0, 0), (NX, NX), (0, 0)))
    result_real = jnp.zeros((NBLK, BLOCK, NY), jnp.float32)
    result_imag = jnp.zeros((NBLK, BLOCK, NY), jnp.float32)
    for order_at in range(3):
        start_row = NX + (order_at - 1) * offset_step
        source = lax.dynamic_slice_in_dim(padded, start_row, NX, 1).astype(jnp.float32).reshape(2, NBLK, BLOCK, NY)
        kernel = matrices[:, :, order_at].astype(jnp.float32)
        weight_now = weights[:, order_at][:, None, None]
        result_real = result_real + weight_now * (apply_blocks(kernel[0], source[0]) - apply_blocks(kernel[1], source[1]))
        result_imag = result_imag + weight_now * (apply_blocks(kernel[0], source[1]) + apply_blocks(kernel[1], source[0]))
    return (result_real.reshape(NX, NY), result_imag.reshape(NX, NY))

def reference(spectrum, diffraction, order_mask, phases, transmission, shifts):
    weights = order_mask.astype(jnp.float32)
    current = spectrum
    outgoing = None
    for bounce in range(BOUNCES):
        diff_real, diff_imag = diffract(current, diffraction, weights, shifts[bounce])
        cosine = jnp.cos(phases[bounce])
        sine_part = jnp.sin(phases[bounce])
        wave_k = rounded(jnp.stack([diff_real * cosine - diff_imag * sine_part, diff_real * sine_part + diff_imag * cosine]))
        rows_space = rounded(transform_first(wave_k, 1.0))
        space = transform_second(rows_space, 1.0) * transmission[None]
        if bounce == BOUNCES - 1:
            outgoing = space
        else:
            columns_k = rounded(transform_second(rounded(space), -1.0))
            current = rounded(transform_first(columns_k, -1.0))
    return outgoing
```

```python
import math

import jax
import jax.numpy as jnp
import numpy as np
from jax import lax
from jax.experimental import pallas as pl
from jax.experimental.pallas import tpu as pltpu
from jax.sharding import PartitionSpec as P

F32 = jnp.float32
BF16 = jnp.bfloat16
NR = 16
NC = 8
FULL = 4096


def tables():
    def circle(count, rows, columns):
        angle = 2.0 * np.pi * ((np.arange(rows)[:, None] * np.arange(columns)[None, :]) % count) / count
        return np.cos(angle), np.sin(angle)

    c256, s256 = circle(256, 256, 256)
    c512, s512 = circle(512, 512, 512)
    base_rows = np.stack([c256, s256]) / 64.0
    base_cols = np.stack([c512, s512]) / 64.0
    turn_rows = np.stack(circle(FULL, NR, 256))[:, :, None, :]
    turn_cols = np.stack(circle(FULL, NC, 512))[:, :, None, :]
    return (
        jnp.asarray(base_rows, BF16),
        jnp.asarray(base_cols, BF16),
        jnp.asarray(turn_rows, F32),
        jnp.asarray(turn_cols, F32),
    )


def times_unit(value, numerator, count, sign):
    real, imag = value
    step = (numerator * 8) % (count * 8)
    eighth, rest = divmod(step, count)
    if rest == 0 and eighth % 2 == 0:
        quarter = (eighth // 2) % 4
        if quarter == 0:
            return real, imag
        if quarter == 2:
            return -real, -imag
        if (quarter == 1) == (sign > 0):
            return -imag, real
        return imag, -real
    angle = 2.0 * math.pi * numerator / count
    cosine, sine = math.cos(angle), sign * math.sin(angle)
    if rest == 0:
        half = abs(cosine)
        a = (real - imag) if cosine * sine > 0 else (real + imag)
        b = (real + imag) if cosine * sine > 0 else (imag - real)
        if cosine < 0:
            return a * (-half), b * (-half)
        return a * half, b * half
    return real * cosine - imag * sine, real * sine + imag * cosine


def butterfly(values, sign):
    count = len(values)
    if count == 1:
        return values
    even = butterfly(values[0::2], sign)
    odd = butterfly(values[1::2], sign)
    low, high = [], []
    for at in range(count // 2):
        er, ei = even[at]
        tr, ti = times_unit(odd[at], at, count, sign)
        low.append((er + tr, ei + ti))
        high.append((er - tr, ei - ti))
    return low + high


def cos_sin(angle):
    half = angle * 0.5
    square = half * half
    sine = -2.5052108e-08
    for factor in (2.7557319e-06, -1.9841270e-04, 8.3333333e-03, -1.6666667e-01, 1.0):
        sine = sine * square + factor
    sine = sine * half
    cosine = 2.0876757e-09
    for factor in (-2.7557319e-07, 2.4801587e-05, -1.3888889e-03, 4.1666667e-02, -0.5, 1.0):
        cosine = cosine * square + factor
    return 1.0 - 2.0 * (sine * sine), 2.0 * (sine * cosine)


def dot(a, b):
    return jnp.dot(a, b, preferred_element_type=F32)


def dot_nt(a, b):
    return lax.dot_general(a, b, (((1,), (1,)), ((), ())), preferred_element_type=F32)


def kernel(
    shifts, mask, spec, diff, phases, trans, base_rows, base_cols, turn_rows, turn_cols,
    out,
    low0, high0, dw, trig0, trig1, wr, wc, pick_cols, pick_rows, back_rows, tspace, work,
    sa1, rb1, sb1, ra1, sd1, rd1, sd2, ra2, sa2, rb2, sb2, ra3, low1, high1,
    sa3, rb3, sb3, ra4, sd3, rd3, fs, rf, ts, tr,
    send_sem, recv_sem, halo_sem,
):
    rp = lax.axis_index("rows")
    cp = lax.axis_index("cols")

    def row_peer(step):
        return lax.rem(rp + step, NR)

    def col_peer(step):
        return lax.rem(cp + step, NC)

    barrier = pltpu.get_barrier_semaphore()
    for step in range(1, NR):
        pl.semaphore_signal(barrier, inc=1, device_id={"rows": row_peer(step)})
    for step in range(1, NC):
        pl.semaphore_signal(barrier, inc=1, device_id={"cols": col_peer(step)})
    half_row = lax.div(rp, 2)
    own_pair = half_row == cp
    for h in range(2):
        for step in range(NC):
            peer = col_peer(step)
            target = 2 * cp + h

            @pl.when(jnp.logical_or(peer != cp, target != rp))
            def _():
                pl.semaphore_signal(barrier, inc=1, device_id={"rows": target, "cols": peer})
    for step in range(NR):
        peer = row_peer(step)

        @pl.when(jnp.logical_or(peer != rp, half_row != cp))
        def _():
            pl.semaphore_signal(barrier, inc=1, device_id={"rows": peer, "cols": half_row})

    @pl.when(own_pair)
    def _():
        pl.semaphore_wait(barrier, NR - 1 + NC - 1 + 30)

    @pl.when(jnp.logical_not(own_pair))
    def _():
        pl.semaphore_wait(barrier, NR - 1 + NC - 1 + 32)

    def remote(src, dst, at, device):
        return pltpu.make_async_remote_copy(
            src_ref=src, dst_ref=dst, send_sem=send_sem.at[at], recv_sem=recv_sem.at[at], device_id=device
        )

    def rows_exchange(src, dst, at):
        for step in range(1, NR):
            peer = row_peer(step)
            remote(src.at[peer], dst.at[rp], at, {"rows": peer}).start()
        pltpu.make_async_copy(src.at[rp], dst.at[rp], recv_sem.at[at]).start()

    def cols_exchange(src, dst, at):
        for step in range(1, NC):
            peer = col_peer(step)
            remote(src.at[peer], dst.at[cp], at, {"cols": peer}).start()
        pltpu.make_async_copy(src.at[cp], dst.at[cp], recv_sem.at[at]).start()

    def arrived(dst, at):
        pltpu.make_async_copy(dst, dst, recv_sem.at[at]).wait()

    def halo_start(src, low, high, at):
        @pl.when(rp < NR - 1)
        def _():
            pltpu.make_async_remote_copy(
                src_ref=src, dst_ref=low, send_sem=halo_sem.at[at, 0], recv_sem=halo_sem.at[at, 1],
                device_id={"rows": rp + 1},
            ).start()

        @pl.when(rp > 0)
        def _():
            pltpu.make_async_remote_copy(
                src_ref=src, dst_ref=high, send_sem=halo_sem.at[at, 2], recv_sem=halo_sem.at[at, 3],
                device_id={"rows": rp - 1},
            ).start()

    def halo_wait(src, low, high, at):
        @pl.when(rp < NR - 1)
        def _():
            pltpu.make_async_copy(high, high, halo_sem.at[at, 3]).wait()
            pltpu.make_async_copy(src, src, halo_sem.at[at, 0]).wait()

        @pl.when(rp > 0)
        def _():
            pltpu.make_async_copy(low, low, halo_sem.at[at, 1]).wait()
            pltpu.make_async_copy(src, src, halo_sem.at[at, 2]).wait()

    halo_start(spec, low0, high0, 0)

    @pl.when(rp == 0)
    def _():
        low0[...] = jnp.zeros_like(low0)
        low1[...] = jnp.zeros_like(low1)

    @pl.when(rp == NR - 1)
    def _():
        high0[...] = jnp.zeros_like(high0)
        high1[...] = jnp.zeros_like(high1)

    def iota(shape, axis):
        return lax.broadcasted_iota(jnp.int32, shape, axis)

    def one_hot(test):
        return jnp.where(test, 1.0, 0.0).astype(BF16)

    lane = iota((512, 512), 1)
    pick_cols[...] = one_hot(iota((512, 512), 0) == (lane & 63) * 8 + (lane >> 6))
    a, b = iota((256, 256), 0), iota((256, 256), 1)
    pick_rows[...] = one_hot(b == (a & 15) * 16 + (a >> 4))
    back_rows[...] = one_hot(a == (b & 15) * 16 + (b >> 4))

    for half in range(2):
        cols = pl.ds(half * 256, 256)
        picked = dot(trans[...].astype(BF16), pick_cols[:, cols]).astype(BF16)
        ts[:, :, cols] = dot(pick_rows[...], picked).astype(BF16).reshape(NR, 16, 256)
    for step in range(NR):
        peer = row_peer(step)
        slot = tr.at[cp, lax.rem(rp, 2)]
        here = jnp.logical_and(peer == rp, half_row == cp)

        @pl.when(here)
        def _():
            pltpu.make_async_copy(ts.at[peer], slot, recv_sem.at[0]).start()

        @pl.when(jnp.logical_not(here))
        def _():
            remote(ts.at[peer], slot, 0, {"rows": peer, "cols": half_row}).start()

    c, s = base_rows[0], base_rows[1]
    for sign in range(2):
        t = s if sign == 0 else -s
        wr[sign, 0:256, 0:256] = c
        wr[sign, 256:512, 256:512] = c
        wr[sign, 0:256, 256:512] = t
        wr[sign, 256:512, 0:256] = -t
    c, s = base_cols[0], base_cols[1]
    for sign in range(2):
        t = s if sign == 0 else -s
        wc[sign, 0:512, 0:512] = c
        wc[sign, 512:1024, 512:1024] = c
        wc[sign, 0:512, 512:1024] = t
        wc[sign, 512:1024, 0:512] = -t

    at_j, to_j = iota((128, 256), 0), iota((128, 256), 1)
    for bounce in range(2):
        g = shifts[bounce]
        below = one_hot(to_j == at_j + 256 - g)
        above = one_hot(to_j == at_j + g - 128)
        for block in range(2):
            weights = [mask[block, m].astype(F32) for m in range(3)]
            for plane in range(2):
                left = (dot(diff[plane, block, 0], below) * weights[0]).astype(BF16)
                own = (diff[plane, block, 1].astype(F32) * weights[1]).astype(BF16)
                right = (dot(diff[plane, block, 2], above) * weights[2]).astype(BF16)
                nothing = jnp.zeros((128, 128), BF16)
                units = [left[:, :128], left[:, 128:], own, right[:, :128], right[:, 128:]]
                units = units + [nothing] if block == 0 else [nothing] + units
                for at, unit in enumerate(units):
                    which, col = at // 2, 128 * (at % 2)
                    row = 128 * block
                    if plane == 0:
                        dw[bounce, which, row:row + 128, col:col + 128] = unit
                        dw[bounce, which, 256 + row:384 + row, 256 + col:384 + col] = unit
                    else:
                        dw[bounce, which, 256 + row:384 + row, col:col + 128] = unit
                        dw[bounce, which, row:row + 128, 256 + col:384 + col] = -unit

    def phase0(at, _):
        rows = pl.ds(pl.multiple_of(at * 32, 32), 32)
        cosine, sine = cos_sin(phases[0, rows, :])
        trig0[0, rows, :] = cosine
        trig0[1, rows, :] = sine
        return 0

    lax.fori_loop(0, 8, phase0, 0)

    halo_wait(spec, low0, high0, 0)

    def diffract0(at, _):
        cols = pl.ds(pl.multiple_of(at * 128, 128), 128)
        total = None
        for which, ref in enumerate((low0, spec, high0)):
            block = ref[:, :, cols].reshape(512, 128)
            term = dot(dw[0, which], block)
            total = term if total is None else total + term
        cosine, sine = trig0[0, :, cols], trig0[1, :, cols]
        real, imag = total[:256], total[256:]
        wave_re = (real * cosine - imag * sine).astype(BF16)
        wave_im = (real * sine + imag * cosine).astype(BF16)
        sa1[pl.ds(at * 4, 4), :, 0:256] = wave_re.T.reshape(4, 32, 256)
        sa1[pl.ds(at * 4, 4), :, 256:512] = wave_im.T.reshape(4, 32, 256)
        return 0

    lax.fori_loop(0, 4, diffract0, 0)
    rows_exchange(sa1, rb1, 1)

    def phase1(at, _):
        cols = pl.ds(pl.multiple_of(at * 128, 128), 128)
        cosine, sine = cos_sin(phases[1, :, cols])
        trig1[0, cols, :] = cosine.T
        trig1[1, cols, :] = sine.T
        return 0

    lax.fori_loop(0, 4, phase1, 0)

    arrived(tr, 0)
    low_lane = iota((32, 128), 1) < 64

    def swap_halves(first, second):
        return (
            jnp.where(low_lane, first, pltpu.roll(second, 64, 1)),
            jnp.where(low_lane, pltpu.roll(first, 64, 1), second),
        )

    for e in range(4):
        for q in range(4):
            src = slice(128 * q, 128 * q + 128)
            first = tr[2 * e, :, :, src].reshape(32, 128).astype(F32)
            second = tr[2 * e + 1, :, :, src].reshape(32, 128).astype(F32)
            one, two = swap_halves(first, second)
            tspace[2 * q, :, 128 * e:128 * e + 128] = one
            tspace[2 * q + 1, :, 128 * e:128 * e + 128] = two

    def forward_rows(src, dst):
        def first(at, _):
            crow = pl.ds(pl.multiple_of(lax.div(at, 2) * 16, 16), 16)
            half = pl.multiple_of(lax.rem(at, 2) * 128, 128)
            re, im = pl.ds(half, 128), pl.ds(half + 256, 128)
            values = [(src[p, crow, re].astype(F32), src[p, crow, im].astype(F32)) for p in range(NR)]
            values = butterfly(values, 1)
            for r in range(NR):
                real, imag = values[r]
                cosine, sine = turn_rows[0, r, :, re], turn_rows[1, r, :, re]
                work[r, crow, re] = (real * cosine - imag * sine).astype(BF16)
                work[r, crow, im] = (real * sine + imag * cosine).astype(BF16)
            return 0

        lax.fori_loop(0, 4, first, 0)

        def second(at, _):
            block = pl.ds(at * 4, 4)
            got = dot(work[block].reshape(128, 512), wr[0])
            dst[block] = got.astype(BF16).reshape(4, 32, 512)
            return 0

        lax.fori_loop(0, 4, second, 0)

    def to_natural(src, dst):
        def part(at, _):
            cols = pl.ds(pl.multiple_of(at * 128, 128), 128)
            cols2 = pl.ds(pl.multiple_of(at * 128 + 512, 128), 128)
            block = src[pl.ds(at * 4, 4)].reshape(128, 512)
            dst[:, :, cols] = block[:, :256].T.reshape(8, 32, 128)
            dst[:, :, cols2] = block[:, 256:].T.reshape(8, 32, 128)
            return 0

        lax.fori_loop(0, 4, part, 0)

    def to_turned(src, dst):
        def part(at, _):
            cols = pl.ds(pl.multiple_of(at * 128, 128), 128)
            cols2 = pl.ds(pl.multiple_of(at * 128 + 512, 128), 128)
            dst[pl.ds(at * 4, 4), :, 0:256] = src[:, :, cols].reshape(256, 128).T.reshape(4, 32, 256)
            dst[pl.ds(at * 4, 4), :, 256:512] = src[:, :, cols2].reshape(256, 128).T.reshape(4, 32, 256)
            return 0

        lax.fori_loop(0, 4, part, 0)

    def forward_cols(src, dst):
        def first(at, _):
            crow = pl.ds(pl.multiple_of(lax.div(at, 4) * 16, 16), 16)
            quarter = pl.multiple_of(lax.rem(at, 4) * 128, 128)
            re, im = pl.ds(quarter, 128), pl.ds(quarter + 512, 128)
            values = [(src[p, crow, re].astype(F32), src[p, crow, im].astype(F32)) for p in range(NC)]
            values = butterfly(values, 1)
            for r in range(NC):
                real, imag = values[r]
                cosine, sine = turn_cols[0, r, :, re], turn_cols[1, r, :, re]
                dst[r, crow, re] = (real * cosine - imag * sine).astype(BF16)
                dst[r, crow, im] = (real * sine + imag * cosine).astype(BF16)
            return 0

        lax.fori_loop(0, 8, first, 0)

    def run_cols_pair(src, temp, work_f, dst):
        forward_cols(src, temp)

        def middle(at, _):
            block = pl.ds(at * 2, 2)
            space = dot(temp[block].reshape(64, 1024), wc[0])
            kept = tspace[block].reshape(64, 512)
            kept = jnp.concatenate([kept, kept], axis=1)
            back = dot((space * kept).astype(BF16), wc[1])
            work_f[block] = back.reshape(2, 32, 1024)
            return 0

        lax.fori_loop(0, 4, middle, 0)

        def last(at, _):
            crow = pl.ds(pl.multiple_of(lax.div(at, 4) * 16, 16), 16)
            quarter = pl.multiple_of(lax.rem(at, 4) * 128, 128)
            re, im = pl.ds(quarter, 128), pl.ds(quarter + 512, 128)
            values = []
            for r in range(NC):
                real, imag = work_f[r, crow, re], work_f[r, crow, im]
                cosine, sine = turn_cols[0, r, :, re], turn_cols[1, r, :, re]
                values.append((real * cosine + imag * sine, imag * cosine - real * sine))
            values = butterfly(values, -1)
            for r in range(NC):
                dst[r, crow, re] = values[r][0].astype(BF16)
                dst[r, crow, im] = values[r][1].astype(BF16)
            return 0

        lax.fori_loop(0, 8, last, 0)

    def with_scratch(temp_d, work_d, work_r):
        arrived(rb1, 1)
        forward_rows(rb1, sb1)
        rows_exchange(sb1, ra1, 2)
        arrived(ra1, 2)
        to_natural(ra1, sd1)
        cols_exchange(sd1, rd1, 3)
        arrived(rd1, 3)
        run_cols_pair(rd1, temp_d, work_d, sd2)
        cols_exchange(sd2, ra2, 4)
        arrived(ra2, 4)
        to_turned(ra2, sa2)
        rows_exchange(sa2, rb2, 5)
        arrived(rb2, 5)

        def lanes(at, _):
            block = pl.ds(at * 4, 4)
            work_r[block] = dot(rb2[block].reshape(128, 512), wr[1]).reshape(4, 32, 512)
            return 0

        lax.fori_loop(0, 4, lanes, 0)

        def sources(at, _):
            crow = pl.ds(pl.multiple_of(lax.div(at, 2) * 16, 16), 16)
            half = pl.multiple_of(lax.rem(at, 2) * 128, 128)
            re, im = pl.ds(half, 128), pl.ds(half + 256, 128)
            values = []
            for r in range(NR):
                real, imag = work_r[r, crow, re], work_r[r, crow, im]
                cosine, sine = turn_rows[0, r, :, re], turn_rows[1, r, :, re]
                values.append((real * cosine + imag * sine, imag * cosine - real * sine))
            values = butterfly(values, -1)
            for r in range(NR):
                sb2[r, crow, re] = values[r][0].astype(BF16)
                sb2[r, crow, im] = values[r][1].astype(BF16)
            return 0

        lax.fori_loop(0, 4, sources, 0)
        rows_exchange(sb2, ra3, 6)
        arrived(ra3, 6)
        halo_start(ra3, low1, high1, 1)
        halo_wait(ra3, low1, high1, 1)

        def diffract1(at, _):
            block = pl.ds(at * 4, 4)
            rows = pl.ds(pl.multiple_of(at * 128, 128), 128)
            total = None
            for which, ref in enumerate((low1, ra3, high1)):
                term = dot_nt(ref[block].reshape(128, 512), dw[1, which])
                total = term if total is None else total + term
            cosine, sine = trig1[0, rows, :], trig1[1, rows, :]
            real, imag = total[:, :256], total[:, 256:]
            sa3[block, :, 0:256] = (real * cosine - imag * sine).astype(BF16).reshape(4, 32, 256)
            sa3[block, :, 256:512] = (real * sine + imag * cosine).astype(BF16).reshape(4, 32, 256)
            return 0

        lax.fori_loop(0, 4, diffract1, 0)
        rows_exchange(sa3, rb3, 7)
        arrived(rb3, 7)
        forward_rows(rb3, sb3)
        rows_exchange(sb3, ra4, 8)
        arrived(ra4, 8)
        to_natural(ra4, sd3)
        cols_exchange(sd3, rd3, 9)
        arrived(rd3, 9)
        forward_cols(rd3, temp_d)

        def final_lanes(at, _):
            block = pl.ds(at * 2, 2)
            work_d[block] = dot(temp_d[block].reshape(64, 1024), wc[0]).reshape(2, 32, 1024)
            return 0

        lax.fori_loop(0, 4, final_lanes, 0)
        for plane in range(2):
            for q in range(4):
                for e in range(4):
                    src = slice(512 * plane + 128 * e, 512 * plane + 128 * e + 128)
                    lanes_to = slice(512 * plane + 128 * q, 512 * plane + 128 * q + 128)
                    one, two = swap_halves(work_d[2 * q, :, src], work_d[2 * q + 1, :, src])
                    fs[2 * e, :, lanes_to] = one.astype(BF16)
                    fs[2 * e + 1, :, lanes_to] = two.astype(BF16)
        for h in range(2):
            for step in range(NC):
                peer = col_peer(step)
                target = 2 * cp + h
                here = jnp.logical_and(peer == cp, target == rp)
                src = fs.at[peer, pl.ds(16 * h, 16)]

                @pl.when(here)
                def _():
                    pltpu.make_async_copy(src, rf.at[rp], recv_sem.at[10]).start()

                @pl.when(jnp.logical_not(here))
                def _():
                    remote(src, rf.at[rp], 10, {"rows": target, "cols": peer}).start()
        arrived(rf, 10)
        for plane in range(2):
            ordered = dot_nt(rf[:, :, 512 * plane:512 * plane + 512].reshape(256, 512), pick_cols[...])
            space = dot(back_rows[...], ordered.astype(BF16))
            out[plane] = space * trans[...]

    pl.run_scoped(
        with_scratch,
        pltpu.VMEM((NC, 32, 1024), BF16),
        pltpu.VMEM((NC, 32, 1024), F32),
        pltpu.VMEM((NR, 32, 512), F32),
    )

    def sent(src, at):
        pltpu.make_async_copy(src, src, send_sem.at[at]).wait()

    for at, src in ((1, sa1), (2, sb1), (5, sa2), (6, sb2), (7, sa3), (8, sb3)):
        sent(src.at[pl.ds(0, NR - 1)], at)
    for at, src in ((3, sd1), (4, sd2), (9, sd3)):
        sent(src.at[pl.ds(0, NC - 1)], at)

    @pl.when(own_pair)
    def _():
        sent(ts.at[pl.ds(0, 15)], 0)
        sent(rf.at[pl.ds(0, 15)], 10)

    @pl.when(jnp.logical_not(own_pair))
    def _():
        sent(ts, 0)
        sent(rf, 10)


def on_device(spectrum, diffraction, order_mask, phases, transmission, shifts):
    vmem = pl.BlockSpec(memory_space=pltpu.VMEM)
    smem = pl.BlockSpec(memory_space=pltpu.SMEM)
    rows_buf = pltpu.VMEM((NR, 32, 512), BF16)
    cols_buf = pltpu.VMEM((NC, 32, 1024), BF16)
    halo0 = pltpu.VMEM((2, 256, 512), BF16)
    return pl.pallas_call(
        kernel,
        out_shape=jax.ShapeDtypeStruct((2, 256, 512), F32),
        in_specs=[smem, smem] + [vmem] * 8,
        out_specs=vmem,
        scratch_shapes=[
            halo0, halo0,
            pltpu.VMEM((2, 3, 512, 512), BF16),
            pltpu.VMEM((2, 256, 512), F32),
            pltpu.VMEM((2, 512, 256), F32),
            pltpu.VMEM((2, 512, 512), BF16),
            pltpu.VMEM((2, 1024, 1024), BF16),
            pltpu.VMEM((512, 512), BF16),
            pltpu.VMEM((256, 256), BF16),
            pltpu.VMEM((256, 256), BF16),
            pltpu.VMEM((NC, 32, 512), F32),
            rows_buf,
            rows_buf, rows_buf, rows_buf, rows_buf,
            cols_buf, cols_buf, cols_buf, cols_buf,
            rows_buf, rows_buf, rows_buf, rows_buf,
            rows_buf, rows_buf,
            rows_buf, rows_buf, rows_buf, rows_buf,
            cols_buf, cols_buf, cols_buf,
            pltpu.VMEM((NR, 16, 1024), BF16),
            pltpu.VMEM((NR, 16, 512), BF16),
            pltpu.VMEM((NC, 2, 16, 512), BF16),
            pltpu.SemaphoreType.DMA((11,)),
            pltpu.SemaphoreType.DMA((11,)),
            pltpu.SemaphoreType.DMA((2, 4)),
        ],
        compiler_params=pltpu.CompilerParams(
            collective_id=0, has_side_effects=True, vmem_limit_bytes=60 * 1024 * 1024
        ),
    )(shifts, order_mask, spectrum, diffraction, phases, transmission, *tables())


def solution(mesh):
    placed = (
        P(None, "rows", "cols"),
        P(None, "rows", None, None, None),
        P("rows", None),
        P(None, "rows", "cols"),
        P("rows", "cols"),
        P(),
    )
    return jax.shard_map(
        on_device, mesh=mesh, in_specs=placed, out_specs=P(None, "rows", "cols"), check_vma=False
    )
```

```python
import math

import jax
import jax.numpy as jnp
import numpy as np
from jax import lax
from jax.experimental import pallas as pl
from jax.experimental.pallas import tpu as pltpu
from jax.sharding import PartitionSpec as P

F32 = jnp.float32
BF16 = jnp.bfloat16
NR = 16
NC = 8
FULL = 4096


def tables():
    def circle(count, left, right):
        angle = 2.0 * np.pi * ((left[:, None] * right[None, :]) % count) / count
        return np.cos(angle), np.sin(angle)

    at = np.arange(512)
    row = 32 * (at // 16 % 8) + 8 * (at // 128) + at % 8
    imaginary = at // 8 % 2 == 1
    c, s = circle(256, np.arange(256), row)
    base_rows = np.concatenate([np.where(imaginary, s, c), np.where(imaginary, c, -s)]) / 64.0
    at = np.arange(512)
    col = 256 * (at // 16 % 2) + 16 * (at // 32) + at % 16
    base_cols = np.stack(circle(512, col, np.arange(512))) / 64.0
    turn_rows = np.stack(circle(FULL, np.arange(NR), np.arange(256)))[:, :, None, :]
    turn_cols = np.stack(circle(FULL, np.arange(NC), col))
    by_source = turn_cols.reshape(2, NC, NR, 1, 32)
    by_source = np.tile(by_source, (1, 1, 1, 1, 4))
    by_lane = turn_cols.reshape(2, NC, 4, 1, 128)
    return (
        jnp.asarray(base_rows, BF16),
        jnp.asarray(base_cols, BF16),
        jnp.asarray(turn_rows, F32),
        jnp.asarray(by_source, F32),
        jnp.asarray(by_lane, F32),
    )


def times_unit(value, numerator, count, sign):
    real, imag = value
    step = (numerator * 8) % (count * 8)
    eighth, rest = divmod(step, count)
    if rest == 0 and eighth % 2 == 0:
        quarter = (eighth // 2) % 4
        if quarter == 0:
            return real, imag
        if quarter == 2:
            return -real, -imag
        if (quarter == 1) == (sign > 0):
            return -imag, real
        return imag, -real
    angle = 2.0 * math.pi * numerator / count
    cosine, sine = math.cos(angle), sign * math.sin(angle)
    if rest == 0:
        half = abs(cosine)
        a = (real - imag) if cosine * sine > 0 else (real + imag)
        b = (real + imag) if cosine * sine > 0 else (imag - real)
        if cosine < 0:
            return a * (-half), b * (-half)
        return a * half, b * half
    return real * cosine - imag * sine, real * sine + imag * cosine


def butterfly(values, sign):
    count = len(values)
    if count == 1:
        return values
    even = butterfly(values[0::2], sign)
    odd = butterfly(values[1::2], sign)
    low, high = [], []
    for at in range(count // 2):
        er, ei = even[at]
        tr, ti = times_unit(odd[at], at, count, sign)
        low.append((er + tr, ei + ti))
        high.append((er - tr, ei - ti))
    return low + high


def cos_sin(angle):
    half = angle * 0.5
    square = half * half
    sine = -2.5052108e-08
    for factor in (2.7557319e-06, -1.9841270e-04, 8.3333333e-03, -1.6666667e-01, 1.0):
        sine = sine * square + factor
    sine = sine * half
    cosine = 2.0876757e-09
    for factor in (-2.7557319e-07, 2.4801587e-05, -1.3888889e-03, 4.1666667e-02, -0.5, 1.0):
        cosine = cosine * square + factor
    return 1.0 - 2.0 * (sine * sine), 2.0 * (sine * cosine)


def dot(a, b):
    return jnp.dot(a, b, preferred_element_type=F32)


def dot_nt(a, b):
    return lax.dot_general(a, b, (((1,), (1,)), ((), ())), preferred_element_type=F32)


def kernel(
    shifts, mask, spec_h, diff_h, phases_h, trans_h, base_rows_h, base_cols_h, turn_rows_h, turn_source_h,
    turn_lane_h, out_h,
    spec, diff, phases, trans, wr, base_cols, turn_rows, turn_source, turn_lane, out,
    low0, high0, dw, trig0, trig1, wc, pick_cols, pick_rows, back_rows, tspace,
    work_b, work_z, work_r, work_d, work_s, work_f,
    sa1, rb1, sm1, rd1, sm2, rb2, sb2, ra3, low1, high1, sa3, rb3, sm3, rd3, fs, rf, ts, tr,
    in_sem, send_sem, recv_sem, halo_sem, ready_sem,
):
    rp = lax.axis_index("rows")
    cp = lax.axis_index("cols")

    def row_peer(step):
        return lax.rem(rp + step, NR)

    def col_peer(step):
        return lax.rem(cp + step, NC)

    barrier = pltpu.get_barrier_semaphore()
    for step in range(1, NR):
        pl.semaphore_signal(barrier, inc=1, device_id={"rows": row_peer(step)})
    for step in range(1, NC):
        pl.semaphore_signal(barrier, inc=1, device_id={"cols": col_peer(step)})

    loads = {}
    for at, (name, src, dst) in enumerate((
        ("diff", diff_h, diff), ("phases", phases_h, phases), ("spec", spec_h, spec),
        ("wr", base_rows_h, wr), ("turn_rows", turn_rows_h, turn_rows), ("trans", trans_h, trans),
        ("base_cols", base_cols_h, base_cols), ("turn_source", turn_source_h, turn_source),
        ("turn_lane", turn_lane_h, turn_lane),
    )):
        loads[name] = pltpu.make_async_copy(src, dst, in_sem.at[at])
        loads[name].start()

    def remote(src, dst, at, device):
        return pltpu.make_async_remote_copy(
            src_ref=src, dst_ref=dst, send_sem=send_sem.at[at], recv_sem=recv_sem.at[at], device_id=device
        )

    def rows_exchange(src, dst, at):
        for step in range(1, NR):
            peer = row_peer(step)
            remote(src.at[peer], dst.at[rp], at, {"rows": peer}).start()
        pltpu.make_async_copy(src.at[rp], dst.at[rp], recv_sem.at[at]).start()

    def arrived(dst, at):
        pltpu.make_async_copy(dst, dst, recv_sem.at[at]).wait()

    def sent(src, at):
        pltpu.make_async_copy(src, src, send_sem.at[at]).wait()

    def halo_start(src, low, high, at):
        @pl.when(rp < NR - 1)
        def _():
            pltpu.make_async_remote_copy(
                src_ref=src, dst_ref=low, send_sem=halo_sem.at[at, 0], recv_sem=halo_sem.at[at, 1],
                device_id={"rows": rp + 1},
            ).start()

        @pl.when(rp > 0)
        def _():
            pltpu.make_async_remote_copy(
                src_ref=src, dst_ref=high, send_sem=halo_sem.at[at, 2], recv_sem=halo_sem.at[at, 3],
                device_id={"rows": rp - 1},
            ).start()

    def halo_wait(low, high, at):
        @pl.when(rp < NR - 1)
        def _():
            pltpu.make_async_copy(high, high, halo_sem.at[at, 3]).wait()

        @pl.when(rp > 0)
        def _():
            pltpu.make_async_copy(low, low, halo_sem.at[at, 1]).wait()

    def halo_sent(src, at):
        @pl.when(rp < NR - 1)
        def _():
            pltpu.make_async_copy(src, src, halo_sem.at[at, 0]).wait()

        @pl.when(rp > 0)
        def _():
            pltpu.make_async_copy(src, src, halo_sem.at[at, 2]).wait()

    def iota(shape, axis):
        return lax.broadcasted_iota(jnp.int32, shape, axis)

    def one_hot(test):
        return jnp.where(test, 1.0, 0.0).astype(BF16)

    at_j, to_j = iota((128, 256), 0), iota((128, 256), 1)

    def banded(bounce):
        g = shifts[bounce]
        below = one_hot(to_j == at_j + 256 - g)
        above = one_hot(to_j == at_j + g - 128)
        for block in range(2):
            weights = [mask[block, m].astype(F32) for m in range(3)]
            for plane in range(2):
                left = (dot(diff[plane, block, 0], below) * weights[0]).astype(BF16)
                own = (diff[plane, block, 1].astype(F32) * weights[1]).astype(BF16)
                right = (dot(diff[plane, block, 2], above) * weights[2]).astype(BF16)
                nothing = jnp.zeros((128, 128), BF16)
                units = [left[:, :128], left[:, 128:], own, right[:, :128], right[:, 128:]]
                units = units + [nothing] if block == 0 else [nothing] + units
                for at, unit in enumerate(units):
                    which, col = at // 2, 128 * (at % 2)
                    row = 128 * block
                    if plane == 0:
                        dw[bounce, which, row:row + 128, col:col + 128] = unit
                        dw[bounce, which, 256 + row:384 + row, 256 + col:384 + col] = unit
                    else:
                        dw[bounce, which, 256 + row:384 + row, col:col + 128] = unit
                        dw[bounce, which, row:row + 128, 256 + col:384 + col] = -unit

    loads["diff"].wait()
    banded(0)

    @pl.when(rp == 0)
    def _():
        low0[...] = jnp.zeros_like(low0)
        low1[...] = jnp.zeros_like(low1)

    @pl.when(rp == NR - 1)
    def _():
        high0[...] = jnp.zeros_like(high0)
        high1[...] = jnp.zeros_like(high1)

    pl.semaphore_wait(barrier, NR - 1 + NC - 1)
    for h in range(2):
        halo_start(spec_h.at[:, :, pl.ds(256 * h, 256)], low0.at[h], high0.at[h], h)
    for step in range(1, NC):
        pl.semaphore_signal(ready_sem, inc=1, device_id={"cols": col_peer(step)})

    loads["phases"].wait()

    def phase0(at, _):
        rows = pl.ds(pl.multiple_of(at * 32, 32), 32)
        cosine, sine = cos_sin(phases[0, rows, :])
        trig0[0, rows, :] = cosine
        trig0[1, rows, :] = sine
        return 0

    lax.fori_loop(0, 8, phase0, 0)
    loads["spec"].wait()

    for h in range(2):
        halo_wait(low0.at[h], high0.at[h], h)
        for part in range(2):
            cols = slice(256 * h + 128 * part, 256 * h + 128 * part + 128)
            here = slice(128 * part, 128 * part + 128)
            total = dot(dw[0, 1], spec[:, :, cols].reshape(512, 128))
            total = total + dot(dw[0, 0], low0[h, :, :, here].reshape(512, 128))
            total = total + dot(dw[0, 2], high0[h, :, :, here].reshape(512, 128))
            cosine, sine = trig0[0, :, cols], trig0[1, :, cols]
            real, imag = total[:256], total[256:]
            wave_re = (real * cosine - imag * sine).astype(BF16)
            wave_im = (real * sine + imag * cosine).astype(BF16)
            sa1[h, 8 * part:8 * part + 8, :, 0:256] = wave_re.T.reshape(8, 16, 256)
            sa1[h, 8 * part:8 * part + 8, :, 256:512] = wave_im.T.reshape(8, 16, 256)
        rows_exchange(sa1.at[h], rb1.at[h], 1 + h)

    pl.semaphore_wait(ready_sem, NC - 1)

    lane = iota((512, 512), 1)
    pick_cols[...] = one_hot(iota((512, 512), 0) == (lane & 63) * 8 + (lane >> 6))
    a, b = iota((256, 256), 0), iota((256, 256), 1)
    pick_rows[...] = one_hot(b == (a & 15) * 16 + (a >> 4))
    back_rows[...] = one_hot(a == (b & 15) * 16 + (b >> 4))

    half_row = lax.div(rp, 2)
    own_pair = half_row == cp
    loads["trans"].wait()
    for half in range(2):
        cols = pl.ds(half * 256, 256)
        picked = dot(trans[...].astype(BF16), pick_cols[:, cols]).astype(BF16)
        ts[:, :, cols] = dot(pick_rows[...], picked).astype(BF16).reshape(NR, 16, 256)
    for step in range(NR):
        peer = row_peer(step)
        slot = tr.at[cp, lax.rem(rp, 2)]
        here = jnp.logical_and(peer == rp, own_pair)

        @pl.when(here)
        def _():
            pltpu.make_async_copy(ts.at[peer], slot, recv_sem.at[0]).start()

        @pl.when(jnp.logical_not(here))
        def _():
            remote(ts.at[peer], slot, 0, {"rows": peer, "cols": half_row}).start()

    loads["base_cols"].wait()
    c, s = base_cols[0], base_cols[1]
    wc[0:512, 0:512] = c
    wc[512:1024, 512:1024] = c
    wc[0:512, 512:1024] = s
    wc[512:1024, 0:512] = -s
    for name in ("wr", "turn_rows", "turn_source", "turn_lane"):
        loads[name].wait()

    lane128 = iota((1, 128), 1)
    low_half = lane128 < 64
    even_group = (lane128 & 32) == 0

    def swap_halves(first, second):
        return (
            jnp.where(low_half, first, pltpu.roll(second, 64, 1)),
            jnp.where(low_half, pltpu.roll(first, 64, 1), second),
        )

    def swap_groups(first, second):
        return (
            jnp.where(even_group, first, pltpu.roll(second, 32, 1)),
            jnp.where(even_group, pltpu.roll(first, 96, 1), second),
        )

    def quad(values):
        p0, p2 = swap_halves(values[0], values[2])
        p1, p3 = swap_halves(values[1], values[3])
        b0, b1 = swap_groups(p0, p1)
        b2, b3 = swap_groups(p2, p3)
        return [b0, b1, b2, b3]

    def forward_rows(src, h):
        def first(at, _):
            half = pl.multiple_of(at * 128, 128)
            re, im = pl.ds(half, 128), pl.ds(half + 256, 128)
            values = [(src[p, :, re].astype(F32), src[p, :, im].astype(F32)) for p in range(NR)]
            values = butterfly(values, 1)
            for r in range(NR):
                real, imag = values[r]
                cosine, sine = turn_rows[0, r, :, re], turn_rows[1, r, :, re]
                work_b[r, :, re] = (real * cosine - imag * sine).astype(BF16)
                work_b[r, :, im] = (real * sine + imag * cosine).astype(BF16)
            return 0

        lax.fori_loop(0, 2, first, 0)
        for part in range(2):
            lanes = slice(256 * part, 256 * part + 256)
            got = dot(work_b[...].reshape(256, 512), wr[:, lanes])
            work_z[:, 16 * h:16 * h + 16, lanes] = got.astype(BF16).reshape(NR, 16, 256)

    def mesh_send(src, dst, slot, at, r, g):
        remote(src.at[r, g], dst.at[slot], at, {"rows": r, "cols": g}).start()

    def to_cols(send, recv, at):
        def turn(step):
            r = row_peer(step)
            block = work_z[r]
            block = jnp.concatenate([block[:, 128 * u:128 * u + 128] for u in range(4)], axis=0)
            send[r] = block.T.reshape(NC, 16, 128)
            return r

        def others(step, _):
            r = turn(step)
            for away in range(NC):
                g = col_peer(away)
                remote(send.at[r, g], recv.at[cp, rp], at, {"rows": r, "cols": g}).start()
            return 0

        lax.fori_loop(1, NR, others, 0)
        turn(0)
        for away in range(1, NC):
            g = col_peer(away)
            remote(send.at[rp, g], recv.at[cp, rp], at, {"rows": rp, "cols": g}).start()
        pltpu.make_async_copy(send.at[rp, cp], recv.at[cp, rp], recv_sem.at[at]).start()

    def forward_cols(src):
        def first(at, _):
            turned = []
            for low in range(4):
                t = at * 4 + low
                values = []
                for p in range(NC):
                    tile = src[p, t].astype(F32)
                    values.append((tile[:8], tile[8:]))
                values = butterfly(values, 1)
                for r in range(NC):
                    real, imag = values[r]
                    cosine, sine = turn_source[0, r, t], turn_source[1, r, t]
                    values[r] = (real * cosine - imag * sine, real * sine + imag * cosine)
                turned.append(values)
            for r in range(NC):
                for plane in range(2):
                    lanes = pl.ds(pl.multiple_of(at * 128 + 512 * plane, 128), 128)
                    rows = quad([turned[low][r][plane] for low in range(4)])
                    work_d[r, :, lanes] = jnp.concatenate(rows, axis=0).astype(BF16)
            return 0

        lax.fori_loop(0, 4, first, 0)

    def phase1(at, _):
        cols = pl.ds(pl.multiple_of(at * 128, 128), 128)
        cosine, sine = cos_sin(phases[1, :, cols])
        trig1[0, cols, :] = cosine.T
        trig1[1, cols, :] = sine.T
        return 0

    for h in range(2):
        arrived(rb1.at[h], 1 + h)
        forward_rows(rb1.at[h], h)
    to_cols(sm1, rd1, 3)

    lax.fori_loop(0, 4, phase1, 0)
    banded(1)

    arrived(tr, 0)
    for e in range(4):
        for q in range(4):
            src = slice(128 * q, 128 * q + 128)
            first = tr[2 * e, :, :, src].reshape(32, 128).astype(F32)
            second = tr[2 * e + 1, :, :, src].reshape(32, 128).astype(F32)
            one, two = swap_halves(first, second)
            tspace[2 * q, :, 128 * e:128 * e + 128] = one
            tspace[2 * q + 1, :, 128 * e:128 * e + 128] = two

    arrived(rd1, 3)
    forward_cols(rd1)
    for part in range(4):
        lanes = slice(256 * part, 256 * part + 256)
        kept = slice(256 * (part % 2), 256 * (part % 2) + 256)
        space = dot(work_d[...].reshape(256, 1024), wc[:, lanes])
        work_s[:, lanes] = (space * tspace[:, :, kept].reshape(256, 256)).astype(BF16)
    for part in range(4):
        lanes = slice(256 * part, 256 * part + 256)
        work_f[:, :, lanes] = dot_nt(work_s[...], wc[lanes, :]).reshape(NC, 32, 256)

    def last_cols(at, _):
        re = pl.ds(pl.multiple_of(at * 128, 128), 128)
        im = pl.ds(pl.multiple_of(at * 128 + 512, 128), 128)
        parts = []
        for u in range(4):
            values = []
            for r in range(NC):
                real, imag = work_f[r, 8 * u:8 * u + 8, re], work_f[r, 8 * u:8 * u + 8, im]
                cosine, sine = turn_lane[0, r, at], turn_lane[1, r, at]
                values.append((real * cosine + imag * sine, imag * cosine - real * sine))
            parts.append(butterfly(values, -1))
        for q in range(NC):
            reals = quad([parts[u][q][0] for u in range(4)])
            imags = quad([parts[u][q][1] for u in range(4)])
            for low in range(4):
                sm2[at * 4 + low, q] = jnp.concatenate([reals[low], imags[low]], axis=0).astype(BF16)
        return 0

    lax.fori_loop(0, 4, last_cols, 0)

    def send_back(step, _):
        t = row_peer(step)
        for away in range(NC):
            g = col_peer(away)
            remote(sm2.at[t, g], rb2.at[rp, cp], 4, {"rows": t, "cols": g}).start()
        return 0

    lax.fori_loop(1, NR, send_back, 0)
    for away in range(1, NC):
        g = col_peer(away)
        remote(sm2.at[rp, g], rb2.at[rp, cp], 4, {"rows": rp, "cols": g}).start()
    pltpu.make_async_copy(sm2.at[rp, cp], rb2.at[rp, cp], recv_sem.at[4]).start()
    arrived(rb2, 4)

    def untile(s, _):
        block = rb2[s].reshape(128, 128).T
        for u in range(4):
            work_z[s, :, 128 * u:128 * u + 128] = block[32 * u:32 * u + 32]
        return 0

    lax.fori_loop(0, NR, untile, 0)
    for h in range(2):
        for part in range(2):
            lanes = slice(256 * part, 256 * part + 256)
            rows = work_z[:, 16 * h:16 * h + 16, :].reshape(256, 512)
            work_r[:, :, lanes] = dot_nt(rows, wr[lanes, :]).reshape(NR, 16, 256)

        def sources(at, _):
            half = pl.multiple_of(at * 128, 128)
            re, im = pl.ds(half, 128), pl.ds(half + 256, 128)
            values = []
            for r in range(NR):
                real, imag = work_r[r, :, re], work_r[r, :, im]
                cosine, sine = turn_rows[0, r, :, re], turn_rows[1, r, :, re]
                values.append((real * cosine + imag * sine, imag * cosine - real * sine))
            values = butterfly(values, -1)
            for r in range(NR):
                sb2[h, r, :, re] = values[r][0].astype(BF16)
                sb2[h, r, :, im] = values[r][1].astype(BF16)
            return 0

        lax.fori_loop(0, 2, sources, 0)
        rows_exchange(sb2.at[h], ra3.at[h], 5 + h)

    for h in range(2):
        arrived(ra3.at[h], 5 + h)
        halo_start(ra3.at[h], low1.at[h], high1.at[h], 2 + h)

    for h in range(2):
        halo_wait(low1.at[h], high1.at[h], 2 + h)
        total = dot_nt(ra3[h].reshape(256, 512), dw[1, 1])
        total = total + dot_nt(low1[h].reshape(256, 512), dw[1, 0])
        total = total + dot_nt(high1[h].reshape(256, 512), dw[1, 2])
        rows = slice(256 * h, 256 * h + 256)
        cosine, sine = trig1[0, rows, :], trig1[1, rows, :]
        real, imag = total[:, :256], total[:, 256:]
        sa3[h, :, :, 0:256] = (real * cosine - imag * sine).astype(BF16).reshape(NR, 16, 256)
        sa3[h, :, :, 256:512] = (real * sine + imag * cosine).astype(BF16).reshape(NR, 16, 256)
        rows_exchange(sa3.at[h], rb3.at[h], 7 + h)
    for h in range(2):
        arrived(rb3.at[h], 7 + h)
        forward_rows(rb3.at[h], h)
    to_cols(sm3, rd3, 9)
    arrived(rd3, 9)
    forward_cols(rd3)
    for part in range(4):
        lanes = slice(256 * part, 256 * part + 256)
        work_f[:, :, lanes] = dot(work_d[...].reshape(256, 1024), wc[:, lanes]).reshape(NC, 32, 256)
    for plane in range(2):
        for q in range(4):
            for e in range(4):
                src = slice(512 * plane + 128 * e, 512 * plane + 128 * e + 128)
                lanes_to = slice(512 * plane + 128 * q, 512 * plane + 128 * q + 128)
                one, two = swap_halves(work_f[2 * q, :, src], work_f[2 * q + 1, :, src])
                fs[2 * e, :, lanes_to] = one.astype(BF16)
                fs[2 * e + 1, :, lanes_to] = two.astype(BF16)
    for h in range(2):
        for step in range(NC):
            peer = col_peer(step)
            target = 2 * cp + h
            here = jnp.logical_and(peer == cp, target == rp)
            src = fs.at[peer, pl.ds(16 * h, 16)]

            @pl.when(here)
            def _():
                pltpu.make_async_copy(src, rf.at[rp], recv_sem.at[10]).start()

            @pl.when(jnp.logical_not(here))
            def _():
                remote(src, rf.at[rp], 10, {"rows": target, "cols": peer}).start()
    arrived(rf, 10)
    for plane in range(2):
        ordered = dot_nt(rf[:, :, 512 * plane:512 * plane + 512].reshape(256, 512), pick_cols[...])
        space = dot(back_rows[...], ordered.astype(BF16))
        out[plane] = space * trans[...]
        pltpu.make_async_copy(out.at[plane], out_h.at[plane], in_sem.at[9 + plane]).start()

    for h in range(2):
        halo_sent(spec_h.at[:, :, pl.ds(256 * h, 256)], h)
        halo_sent(ra3.at[h], 2 + h)
        for at, src in ((1, sa1), (5, sb2), (7, sa3)):
            sent(src.at[h, pl.ds(0, NR - 1)], at + h)
    for at, src in ((3, sm1), (4, sm2), (9, sm3)):
        sent(src.at[pl.ds(0, NR - 1)], at)
        sent(src.at[0, pl.ds(0, NC - 1)], at)

    @pl.when(own_pair)
    def _():
        sent(ts.at[pl.ds(0, 15)], 0)
        sent(rf.at[pl.ds(0, 15)], 10)

    @pl.when(jnp.logical_not(own_pair))
    def _():
        sent(ts, 0)
        sent(rf, 10)

    for plane in range(2):
        pltpu.make_async_copy(out.at[plane], out_h.at[plane], in_sem.at[9 + plane]).wait()


def on_device(spectrum, diffraction, order_mask, phases, transmission, shifts):
    anywhere = pl.BlockSpec(memory_space=pl.ANY)
    smem = pl.BlockSpec(memory_space=pltpu.SMEM)
    constants = tables()
    operands = (spectrum, diffraction, phases, transmission) + constants

    def vmem(kind, *shape):
        return pltpu.VMEM(shape, kind)

    halves = (2, NR, 16, 512)
    return pl.pallas_call(
        kernel,
        out_shape=jax.ShapeDtypeStruct((2, 256, 512), F32),
        in_specs=[smem, smem] + [anywhere] * len(operands),
        out_specs=anywhere,
        scratch_shapes=[pltpu.VMEM(x.shape, x.dtype) for x in operands] + [
            vmem(F32, 2, 256, 512),
            vmem(BF16, 2, 2, 256, 256), vmem(BF16, 2, 2, 256, 256),
            vmem(BF16, 2, 3, 512, 512),
            vmem(F32, 2, 256, 512),
            vmem(F32, 2, 512, 256),
            vmem(BF16, 1024, 1024),
            vmem(BF16, 512, 512), vmem(BF16, 256, 256), vmem(BF16, 256, 256),
            vmem(F32, NC, 32, 512),
            vmem(BF16, NR, 16, 512),
            vmem(BF16, NR, 32, 512),
            vmem(F32, NR, 16, 512),
            vmem(BF16, NC, 32, 1024),
            vmem(BF16, 256, 1024),
            vmem(F32, NC, 32, 1024),
            vmem(BF16, *halves), vmem(BF16, *halves),
            vmem(BF16, NR, NC, 16, 128), vmem(BF16, NC, NR, 16, 128),
            vmem(BF16, NR, NC, 16, 128), vmem(BF16, NR, NC, 16, 128),
            vmem(BF16, *halves), vmem(BF16, *halves),
            vmem(BF16, *halves), vmem(BF16, *halves),
            vmem(BF16, *halves), vmem(BF16, *halves),
            vmem(BF16, NR, NC, 16, 128), vmem(BF16, NC, NR, 16, 128),
            vmem(BF16, NC, 32, 1024), vmem(BF16, NR, 16, 1024),
            vmem(BF16, NR, 16, 512), vmem(BF16, NC, 2, 16, 512),
            pltpu.SemaphoreType.DMA((11,)),
            pltpu.SemaphoreType.DMA((11,)),
            pltpu.SemaphoreType.DMA((11,)),
            pltpu.SemaphoreType.DMA((4, 4)),
            pltpu.SemaphoreType.REGULAR,
        ],
        compiler_params=pltpu.CompilerParams(
            collective_id=0, has_side_effects=True, vmem_limit_bytes=60 * 1024 * 1024
        ),
    )(shifts, order_mask, *operands)


def solution(mesh):
    placed = (
        P(None, "rows", "cols"),
        P(None, "rows", None, None, None),
        P("rows", None),
        P(None, "rows", "cols"),
        P("rows", "cols"),
        P(),
    )
    return jax.shard_map(
        on_device, mesh=mesh, in_specs=placed, out_specs=P(None, "rows", "cols"), check_vma=False
    )
```

```python
import math

import jax
import jax.numpy as jnp
import numpy as np
from jax import lax
from jax.experimental import pallas as pl
from jax.experimental.pallas import tpu as pltpu
from jax.sharding import PartitionSpec as P

F32 = jnp.float32
BF16 = jnp.bfloat16
NR = 16
NC = 8
FULL = 4096


def tables():
    def circle(count, left, right):
        angle = 2.0 * np.pi * ((left[:, None] * right[None, :]) % count) / count
        return np.cos(angle), np.sin(angle)

    at = np.arange(512)
    row = 16 * (at // 8 % 16) + 8 * (at // 256) + at % 8
    imaginary = at // 128 % 2 == 1
    c, s = circle(256, np.arange(256), row)
    base_rows = np.concatenate([np.where(imaginary, s, c), np.where(imaginary, c, -s)]) / 64.0
    col = 256 * (at // 16 % 2) + 16 * (at // 32) + at % 16
    base_cols = np.stack(circle(512, col, np.arange(512))) / 64.0
    turn_rows = np.stack(circle(FULL, np.arange(NR), np.arange(256)))[:, :, None, :]
    turn_cols = np.stack(circle(FULL, np.arange(NC), col)).reshape(2, NC, 4, 1, 128)
    return (
        jnp.asarray(base_rows, BF16),
        jnp.asarray(base_cols, BF16),
        jnp.asarray(turn_rows, F32),
        jnp.asarray(turn_cols, F32),
    )


def times_unit(value, numerator, count, sign):
    real, imag = value
    step = (numerator * 8) % (count * 8)
    eighth, rest = divmod(step, count)
    if rest == 0 and eighth % 2 == 0:
        quarter = (eighth // 2) % 4
        if quarter == 0:
            return real, imag
        if quarter == 2:
            return -real, -imag
        if (quarter == 1) == (sign > 0):
            return -imag, real
        return imag, -real
    angle = 2.0 * math.pi * numerator / count
    cosine, sine = math.cos(angle), sign * math.sin(angle)
    if rest == 0:
        half = abs(cosine)
        a = (real - imag) if cosine * sine > 0 else (real + imag)
        b = (real + imag) if cosine * sine > 0 else (imag - real)
        if cosine < 0:
            return a * (-half), b * (-half)
        return a * half, b * half
    return real * cosine - imag * sine, real * sine + imag * cosine


def butterfly(values, sign):
    count = len(values)
    if count == 1:
        return values
    even = butterfly(values[0::2], sign)
    odd = butterfly(values[1::2], sign)
    low, high = [], []
    for at in range(count // 2):
        er, ei = even[at]
        tr, ti = times_unit(odd[at], at, count, sign)
        low.append((er + tr, ei + ti))
        high.append((er - tr, ei - ti))
    return low + high


def cos_sin(angle):
    half = angle * 0.5
    square = half * half
    sine = -2.5052108e-08
    for factor in (2.7557319e-06, -1.9841270e-04, 8.3333333e-03, -1.6666667e-01, 1.0):
        sine = sine * square + factor
    sine = sine * half
    cosine = 2.0876757e-09
    for factor in (-2.7557319e-07, 2.4801587e-05, -1.3888889e-03, 4.1666667e-02, -0.5, 1.0):
        cosine = cosine * square + factor
    return 1.0 - 2.0 * (sine * sine), 2.0 * (sine * cosine)


def dot(a, b):
    return jnp.dot(a, b, preferred_element_type=F32)


def dot_nt(a, b):
    return lax.dot_general(a, b, (((1,), (1,)), ((), ())), preferred_element_type=F32)


def kernel(
    shifts, mask, spec_h, diff_h, phases_h, trans_h, base_rows_h, base_cols_h, turn_rows_h, turn_cols_h, out_h,
    spec, diff, phases, trans, wr, base_cols, turn_rows, turn_cols, out,
    low0, high0, dw, trig0, trig1, wc, pick_cols, pick_rows, back_rows, tspace,
    work_b, work_z, work_y, work_r, work_d, work_s, work_f, work_o,
    sa1, rb1, sm1, rd1, sm2, rb2, sb2, ra3, low1, high1, sa3, rb3, sm3, rd3, fs, rf, ts, tr,
    in_sem, send_sem, recv_sem, halo_sem, ready_sem,
):
    rp = lax.axis_index("rows")
    cp = lax.axis_index("cols")

    def row_peer(step):
        return lax.rem(rp + step, NR)

    def col_peer(step):
        return lax.rem(cp + step, NC)

    waits = []

    def finish():
        for wait in waits:
            wait()

    barrier = pltpu.get_barrier_semaphore()
    for step in range(1, NR):
        pl.semaphore_signal(barrier, inc=1, device_id={"rows": row_peer(step)})
    for step in range(1, NC):
        pl.semaphore_signal(barrier, inc=1, device_id={"cols": col_peer(step)})

    loads = {}
    for at, (name, src, dst) in enumerate((
        ("diff", diff_h, diff), ("phases", phases_h, phases), ("spec", spec_h, spec),
        ("wr", base_rows_h, wr), ("turn_rows", turn_rows_h, turn_rows), ("trans", trans_h, trans),
        ("base_cols", base_cols_h, base_cols), ("turn_cols", turn_cols_h, turn_cols),
    )):
        loads[name] = pltpu.make_async_copy(src, dst, in_sem.at[at])
        loads[name].start()

    def remote(src, dst, at, device):
        return pltpu.make_async_remote_copy(
            src_ref=src, dst_ref=dst, send_sem=send_sem.at[at], recv_sem=recv_sem.at[at], device_id=device
        )

    def rows_exchange(src, dst, at):
        for step in range(1, NR):
            peer = row_peer(step)
            remote(src.at[peer], dst.at[rp], at, {"rows": peer}).start()
        pltpu.make_async_copy(src.at[rp], dst.at[rp], recv_sem.at[at]).start()
        waits.append(lambda: sent(src.at[pl.ds(0, NR - 1)], at))

    def cols_exchange(src, dst, at):
        for step in range(1, NC):
            peer = col_peer(step)
            remote(src.at[peer], dst.at[cp], at, {"cols": peer}).start()
        pltpu.make_async_copy(src.at[cp], dst.at[cp], recv_sem.at[at]).start()
        waits.append(lambda: sent(src.at[pl.ds(0, NC - 1)], at))

    def arrived(dst, at):
        pltpu.make_async_copy(dst, dst, recv_sem.at[at]).wait()

    def sent(src, at):
        pltpu.make_async_copy(src, src, send_sem.at[at]).wait()

    def halo_start(src, low, high, at):
        @pl.when(rp < NR - 1)
        def _():
            pltpu.make_async_remote_copy(
                src_ref=src, dst_ref=low, send_sem=halo_sem.at[at, 0], recv_sem=halo_sem.at[at, 1],
                device_id={"rows": rp + 1},
            ).start()

        @pl.when(rp > 0)
        def _():
            pltpu.make_async_remote_copy(
                src_ref=src, dst_ref=high, send_sem=halo_sem.at[at, 2], recv_sem=halo_sem.at[at, 3],
                device_id={"rows": rp - 1},
            ).start()

        waits.append(lambda: halo_sent(src, at))

    def halo_wait(low, high, at):
        @pl.when(rp < NR - 1)
        def _():
            pltpu.make_async_copy(high, high, halo_sem.at[at, 3]).wait()

        @pl.when(rp > 0)
        def _():
            pltpu.make_async_copy(low, low, halo_sem.at[at, 1]).wait()

    def halo_sent(src, at):
        @pl.when(rp < NR - 1)
        def _():
            pltpu.make_async_copy(src, src, halo_sem.at[at, 0]).wait()

        @pl.when(rp > 0)
        def _():
            pltpu.make_async_copy(src, src, halo_sem.at[at, 2]).wait()

    def iota(shape, axis):
        return lax.broadcasted_iota(jnp.int32, shape, axis)

    def one_hot(test):
        return jnp.where(test, 1.0, 0.0).astype(BF16)

    at_j, to_j = iota((128, 256), 0), iota((128, 256), 1)

    def banded(bounce):
        g = shifts[bounce]
        below = one_hot(to_j == at_j + 256 - g)
        above = one_hot(to_j == at_j + g - 128)
        for block in range(2):
            weights = [mask[block, m].astype(F32) for m in range(3)]
            for plane in range(2):
                left = (dot(diff[plane, block, 0], below) * weights[0]).astype(BF16)
                own = (diff[plane, block, 1].astype(F32) * weights[1]).astype(BF16)
                right = (dot(diff[plane, block, 2], above) * weights[2]).astype(BF16)
                nothing = jnp.zeros((128, 128), BF16)
                units = [left[:, :128], left[:, 128:], own, right[:, :128], right[:, 128:]]
                units = units + [nothing] if block == 0 else [nothing] + units
                for at, unit in enumerate(units):
                    which, col = at // 2, 128 * (at % 2)
                    row = 128 * block
                    if plane == 0:
                        dw[bounce, which, row:row + 128, col:col + 128] = unit
                        dw[bounce, which, 256 + row:384 + row, 256 + col:384 + col] = unit
                    else:
                        dw[bounce, which, 256 + row:384 + row, col:col + 128] = unit
                        dw[bounce, which, row:row + 128, 256 + col:384 + col] = -unit

    loads["diff"].wait()
    banded(0)

    @pl.when(rp == 0)
    def _():
        low0[...] = jnp.zeros_like(low0)
        low1[...] = jnp.zeros_like(low1)

    @pl.when(rp == NR - 1)
    def _():
        high0[...] = jnp.zeros_like(high0)
        high1[...] = jnp.zeros_like(high1)

    pl.semaphore_wait(barrier, NR - 1 + NC - 1)
    for h in range(2):
        halo_start(spec_h.at[:, :, pl.ds(256 * h, 256)], low0.at[h], high0.at[h], h)
    for step in range(1, NC):
        pl.semaphore_signal(ready_sem, inc=1, device_id={"cols": col_peer(step)})

    loads["phases"].wait()

    def phase0(at, _):
        rows = pl.ds(pl.multiple_of(at * 32, 32), 32)
        cosine, sine = cos_sin(phases[0, rows, :])
        trig0[0, rows, :] = cosine
        trig0[1, rows, :] = sine
        return 0

    lax.fori_loop(0, 8, phase0, 0)
    loads["spec"].wait()

    for h in range(2):
        halo_wait(low0.at[h], high0.at[h], h)
        for part in range(2):
            cols = slice(256 * h + 128 * part, 256 * h + 128 * part + 128)
            here = slice(128 * part, 128 * part + 128)
            total = dot(dw[0, 1], spec[:, :, cols].reshape(512, 128))
            total = total + dot(dw[0, 0], low0[h, :, :, here].reshape(512, 128))
            total = total + dot(dw[0, 2], high0[h, :, :, here].reshape(512, 128))
            cosine, sine = trig0[0, :, cols], trig0[1, :, cols]
            real, imag = total[:256], total[256:]
            wave_re = (real * cosine - imag * sine).astype(BF16)
            wave_im = (real * sine + imag * cosine).astype(BF16)
            sa1[h, 8 * part:8 * part + 8, :, 0:256] = wave_re.T.reshape(8, 16, 256)
            sa1[h, 8 * part:8 * part + 8, :, 256:512] = wave_im.T.reshape(8, 16, 256)
        rows_exchange(sa1.at[h], rb1.at[h], 1 + h)

    pl.semaphore_wait(ready_sem, NC - 1)

    lane = iota((512, 512), 1)
    pick_cols[...] = one_hot(iota((512, 512), 0) == (lane & 63) * 8 + (lane >> 6))
    a, b = iota((256, 256), 0), iota((256, 256), 1)
    pick_rows[...] = one_hot(b == (a & 15) * 16 + (a >> 4))
    back_rows[...] = one_hot(b == (a & 1) * 128 + ((a & 15) >> 1) * 16 + (a >> 4))

    loads["trans"].wait()
    for half in range(2):
        cols = pl.ds(half * 256, 256)
        picked = dot(trans[...].astype(BF16), pick_cols[:, cols]).astype(BF16)
        ts[:, :, :, cols] = dot(pick_rows[...], picked).astype(BF16).reshape(NC, 2, 16, 256)
    cols_exchange(ts, tr, 0)

    loads["base_cols"].wait()
    c, s = base_cols[0], base_cols[1]
    wc[0:512, 0:512] = c
    wc[512:1024, 512:1024] = c
    wc[0:512, 512:1024] = s
    wc[512:1024, 0:512] = -s
    for name in ("wr", "turn_rows", "turn_cols"):
        loads[name].wait()

    lane128 = iota((1, 128), 1)
    low_half = lane128 < 64
    even_group = (lane128 & 32) == 0

    def swap_halves(first, second):
        return (
            jnp.where(low_half, first, pltpu.roll(second, 64, 1)),
            jnp.where(low_half, pltpu.roll(first, 64, 1), second),
        )

    def swap_groups(first, second):
        return (
            jnp.where(even_group, first, pltpu.roll(second, 32, 1)),
            jnp.where(even_group, pltpu.roll(first, 96, 1), second),
        )

    def quad(values):
        p0, p2 = swap_halves(values[0], values[2])
        p1, p3 = swap_halves(values[1], values[3])
        b0, b1 = swap_groups(p0, p1)
        b2, b3 = swap_groups(p2, p3)
        return [b0, b1, b2, b3]

    def forward_rows(src, h):
        def first(at, _):
            half = pl.multiple_of(at * 128, 128)
            re, im = pl.ds(half, 128), pl.ds(half + 256, 128)
            values = [(src[p, :, re].astype(F32), src[p, :, im].astype(F32)) for p in range(NR)]
            values = butterfly(values, 1)
            for r in range(NR):
                real, imag = values[r]
                cosine, sine = turn_rows[0, r, :, re], turn_rows[1, r, :, re]
                work_b[r, :, re] = (real * cosine - imag * sine).astype(BF16)
                work_b[r, :, im] = (real * sine + imag * cosine).astype(BF16)
            return 0

        lax.fori_loop(0, 2, first, 0)
        for part in range(2):
            lanes = slice(256 * part, 256 * part + 256)
            got = dot(work_b[...].reshape(256, 512), wr[:, lanes])
            work_z[:, 16 * h:16 * h + 16, lanes] = got.astype(BF16).reshape(NR, 16, 256)

    def to_cols(send, recv, at):
        for half in range(2):
            def turn(step):
                g = col_peer(step)
                r = 2 * g + half
                block = work_z[r]
                block = jnp.concatenate([block[:, 128 * u:128 * u + 128] for u in range(4)], axis=0)
                send[half, g] = block.T.reshape(NR, 8, 128)
                return g

            def others(step, _):
                g = turn(step)
                for away in range(NR):
                    d = row_peer(away)
                    remote(send.at[half, g, d], recv.at[half, cp, rp], at + half, {"rows": d, "cols": g}).start()
                return 0

            lax.fori_loop(1, NC, others, 0)
            turn(0)
            for away in range(1, NR):
                d = row_peer(away)
                remote(send.at[half, cp, d], recv.at[half, cp, rp], at + half, {"rows": d}).start()
            tiles_kept(send.at[half, cp, rp], recv.at[half, cp, rp], send.at[half], at + half)

    def tiles_kept(src, dst, send, at):
        pltpu.make_async_copy(src, dst, recv_sem.at[at]).start()
        first, second = send.shape[:2]
        waits.append(lambda: sent(send.at[pl.ds(0, first - 1)], at))
        waits.append(lambda: sent(send.at[0, pl.ds(0, second - 1)], at))

    def forward_cols(src):
        def first(at, _):
            parts = []
            for p in range(NC):
                parts.append(quad([src[p, at * 4 + low].astype(F32) for low in range(4)]))
            halves = []
            for u in range(2):
                values = butterfly([(parts[p][2 * u], parts[p][2 * u + 1]) for p in range(NC)], 1)
                for r in range(NC):
                    real, imag = values[r]
                    cosine, sine = turn_cols[0, r, at], turn_cols[1, r, at]
                    values[r] = (real * cosine - imag * sine, real * sine + imag * cosine)
                halves.append(values)
            for r in range(NC):
                for plane in range(2):
                    lanes = pl.ds(pl.multiple_of(at * 128 + 512 * plane, 128), 128)
                    rows = [halves[u][r][plane] for u in range(2)]
                    work_d[r, :, lanes] = jnp.concatenate(rows, axis=0).astype(BF16)
            return 0

        lax.fori_loop(0, 4, first, 0)

    def phase1(at, _):
        cols = pl.ds(pl.multiple_of(at * 128, 128), 128)
        cosine, sine = cos_sin(phases[1, :, cols])
        trig1[0, cols, :] = cosine.T
        trig1[1, cols, :] = sine.T
        return 0

    for h in range(2):
        arrived(rb1.at[h], 1 + h)
        forward_rows(rb1.at[h], h)
    to_cols(sm1, rd1, 3)

    lax.fori_loop(0, 4, phase1, 0)
    banded(1)

    arrived(tr, 0)
    for e in range(4):
        for q in range(4):
            src = slice(128 * q, 128 * q + 128)
            first = tr[2 * e, :, :, src].reshape(32, 128).astype(F32)
            second = tr[2 * e + 1, :, :, src].reshape(32, 128).astype(F32)
            one, two = swap_halves(first, second)
            tspace[:, 2 * q, :, 128 * e:128 * e + 128] = one.reshape(2, 16, 128)
            tspace[:, 2 * q + 1, :, 128 * e:128 * e + 128] = two.reshape(2, 16, 128)

    for half in range(2):
        arrived(rd1.at[half], 3 + half)
        forward_cols(rd1.at[half])
        for part in range(4):
            lanes = slice(256 * part, 256 * part + 256)
            kept = slice(256 * (part % 2), 256 * (part % 2) + 256)
            space = dot(work_d[...].reshape(128, 1024), wc[:, lanes])
            work_s[:, lanes] = (space * tspace[half, :, :, kept].reshape(128, 256)).astype(BF16)
        for part in range(4):
            lanes = slice(256 * part, 256 * part + 256)
            work_f[:, :, lanes] = dot_nt(work_s[...], wc[lanes, :]).reshape(NC, 16, 256)

        def last_cols(at, _):
            re = pl.ds(pl.multiple_of(at * 128, 128), 128)
            im = pl.ds(pl.multiple_of(at * 128 + 512, 128), 128)
            parts = []
            for u in range(2):
                values = []
                for r in range(NC):
                    real, imag = work_f[r, 8 * u:8 * u + 8, re], work_f[r, 8 * u:8 * u + 8, im]
                    cosine, sine = turn_cols[0, r, at], turn_cols[1, r, at]
                    values.append((real * cosine + imag * sine, imag * cosine - real * sine))
                parts.append(butterfly(values, -1))
            for q in range(NC):
                tiles = quad([parts[0][q][0], parts[0][q][1], parts[1][q][0], parts[1][q][1]])
                for low in range(4):
                    sm2[half, at * 4 + low, q] = tiles[low].astype(BF16)
            return 0

        lax.fori_loop(0, 4, last_cols, 0)

        def send_back(step, _):
            t = row_peer(step)
            for away in range(NC):
                g = col_peer(away)
                remote(sm2.at[half, t, g], rb2.at[half, cp, rp], 11 + half, {"rows": t, "cols": g}).start()
            return 0

        lax.fori_loop(1, NR, send_back, 0)
        for away in range(1, NC):
            g = col_peer(away)
            remote(sm2.at[half, rp, g], rb2.at[half, cp, rp], 11 + half, {"cols": g}).start()
        tiles_kept(sm2.at[half, rp, cp], rb2.at[half, cp, rp], sm2.at[half], 11 + half)

    for half in range(2):
        arrived(rb2.at[half], 11 + half)

        def untile(g, _):
            block = rb2[half, g].reshape(128, 128).T
            for u in range(4):
                work_y[g, :, 128 * u:128 * u + 128] = block[32 * u:32 * u + 32]
            return 0

        lax.fori_loop(0, NC, untile, 0)
        for part in range(2):
            lanes = slice(256 * part, 256 * part + 256)
            got = dot_nt(work_y[...].reshape(256, 512), wr[lanes, :])
            work_r[half, :, :, lanes] = got.reshape(NC, 32, 256)
    for h in range(2):
        crow = slice(16 * h, 16 * h + 16)

        def sources(at, _):
            half = pl.multiple_of(at * 128, 128)
            re, im = pl.ds(half, 128), pl.ds(half + 256, 128)
            values = []
            for r in range(NR):
                real, imag = work_r[r % 2, r // 2, crow, re], work_r[r % 2, r // 2, crow, im]
                cosine, sine = turn_rows[0, r, :, re], turn_rows[1, r, :, re]
                values.append((real * cosine + imag * sine, imag * cosine - real * sine))
            values = butterfly(values, -1)
            for r in range(NR):
                sb2[h, r, :, re] = values[r][0].astype(BF16)
                sb2[h, r, :, im] = values[r][1].astype(BF16)
            return 0

        lax.fori_loop(0, 2, sources, 0)
        rows_exchange(sb2.at[h], ra3.at[h], 5 + h)

    for h in range(2):
        arrived(ra3.at[h], 5 + h)
        halo_start(ra3.at[h], low1.at[h], high1.at[h], 2 + h)

    for h in range(2):
        halo_wait(low1.at[h], high1.at[h], 2 + h)
        total = dot_nt(ra3[h].reshape(256, 512), dw[1, 1])
        total = total + dot_nt(low1[h].reshape(256, 512), dw[1, 0])
        total = total + dot_nt(high1[h].reshape(256, 512), dw[1, 2])
        rows = slice(256 * h, 256 * h + 256)
        cosine, sine = trig1[0, rows, :], trig1[1, rows, :]
        real, imag = total[:, :256], total[:, 256:]
        sa3[h, :, :, 0:256] = (real * cosine - imag * sine).astype(BF16).reshape(NR, 16, 256)
        sa3[h, :, :, 256:512] = (real * sine + imag * cosine).astype(BF16).reshape(NR, 16, 256)
        rows_exchange(sa3.at[h], rb3.at[h], 7 + h)
    for h in range(2):
        arrived(rb3.at[h], 7 + h)
        forward_rows(rb3.at[h], h)
    to_cols(sm3, rd3, 9)
    for half in range(2):
        arrived(rd3.at[half], 9 + half)
        forward_cols(rd3.at[half])
        for part in range(4):
            lanes = slice(256 * part, 256 * part + 256)
            work_f[:, :, lanes] = dot(work_d[...].reshape(128, 1024), wc[:, lanes]).reshape(NC, 16, 256)
        for plane in range(2):
            for q in range(4):
                for e in range(4):
                    src = slice(512 * plane + 128 * e, 512 * plane + 128 * e + 128)
                    lanes_to = slice(512 * plane + 128 * q, 512 * plane + 128 * q + 128)
                    one, two = swap_halves(work_f[2 * q, :, src], work_f[2 * q + 1, :, src])
                    fs[half, 2 * e, :, lanes_to] = one.astype(BF16)
                    fs[half, 2 * e + 1, :, lanes_to] = two.astype(BF16)
        cols_exchange(fs.at[half], rf.at[half], 13 + half)
    for half in range(2):
        arrived(rf.at[half], 13 + half)
        for plane in range(2):
            lanes = slice(512 * plane, 512 * plane + 512)
            ordered = dot_nt(rf[half, :, :, lanes].reshape(128, 512), pick_cols[...])
            work_o[plane, 128 * half:128 * half + 128, :] = ordered.astype(BF16)
    for plane in range(2):
        out[plane] = dot(back_rows[...], work_o[plane]) * trans[...]
        result = pltpu.make_async_copy(out.at[plane], out_h.at[plane], in_sem.at[9 + plane])
        result.start()
        waits.append(result.wait)

    finish()


def on_device(spectrum, diffraction, order_mask, phases, transmission, shifts):
    anywhere = pl.BlockSpec(memory_space=pl.ANY)
    smem = pl.BlockSpec(memory_space=pltpu.SMEM)
    constants = tables()
    operands = (spectrum, diffraction, phases, transmission) + constants

    def vmem(kind, *shape):
        return pltpu.VMEM(shape, kind)

    halves = (2, NR, 16, 512)
    return pl.pallas_call(
        kernel,
        out_shape=jax.ShapeDtypeStruct((2, 256, 512), F32),
        in_specs=[smem, smem] + [anywhere] * len(operands),
        out_specs=anywhere,
        scratch_shapes=[pltpu.VMEM(x.shape, x.dtype) for x in operands] + [
            vmem(F32, 2, 256, 512),
            vmem(BF16, 2, 2, 256, 256), vmem(BF16, 2, 2, 256, 256),
            vmem(BF16, 2, 3, 512, 512),
            vmem(F32, 2, 256, 512),
            vmem(F32, 2, 512, 256),
            vmem(BF16, 1024, 1024),
            vmem(BF16, 512, 512), vmem(BF16, 256, 256), vmem(BF16, 256, 256),
            vmem(F32, 2, NC, 16, 512),
            vmem(BF16, NR, 16, 512),
            vmem(BF16, NR, 32, 512),
            vmem(BF16, NC, 32, 512),
            vmem(F32, 2, NC, 32, 512),
            vmem(BF16, NC, 16, 1024),
            vmem(BF16, 128, 1024),
            vmem(F32, NC, 16, 1024),
            vmem(BF16, 2, 256, 512),
            vmem(BF16, *halves), vmem(BF16, *halves),
            vmem(BF16, 2, NC, NR, 8, 128), vmem(BF16, 2, NC, NR, 8, 128),
            vmem(BF16, 2, NR, NC, 8, 128), vmem(BF16, 2, NC, NR, 8, 128),
            vmem(BF16, *halves), vmem(BF16, *halves),
            vmem(BF16, *halves), vmem(BF16, *halves),
            vmem(BF16, *halves), vmem(BF16, *halves),
            vmem(BF16, 2, NC, NR, 8, 128), vmem(BF16, 2, NC, NR, 8, 128),
            vmem(BF16, 2, NC, 16, 1024), vmem(BF16, 2, NC, 16, 1024),
            vmem(BF16, NC, 2, 16, 512), vmem(BF16, NC, 2, 16, 512),
            pltpu.SemaphoreType.DMA((11,)),
            pltpu.SemaphoreType.DMA((15,)),
            pltpu.SemaphoreType.DMA((15,)),
            pltpu.SemaphoreType.DMA((4, 4)),
            pltpu.SemaphoreType.REGULAR,
        ],
        compiler_params=pltpu.CompilerParams(
            collective_id=0, has_side_effects=True, vmem_limit_bytes=60 * 1024 * 1024
        ),
    )(shifts, order_mask, *operands)


def solution(mesh):
    placed = (
        P(None, "rows", "cols"),
        P(None, "rows", None, None, None),
        P("rows", None),
        P(None, "rows", "cols"),
        P("rows", "cols"),
        P(),
    )
    return jax.shard_map(
        on_device, mesh=mesh, in_specs=placed, out_specs=P(None, "rows", "cols"), check_vma=False
    )
```

```python
import math

import jax
import jax.numpy as jnp
import numpy as np
from jax import lax
from jax.experimental import pallas as pl
from jax.experimental.pallas import tpu as pltpu
from jax.sharding import PartitionSpec as P

F32 = jnp.float32
BF16 = jnp.bfloat16
NR = 16
NC = 8
FULL = 4096


def ring(step):
    return min(step, 4 - step)


def depth(high, low):
    return (0, 1, 2, 1)[2 * high + low]


ROW_STEPS = sorted(
    ((z, x, c) for z in range(2) for x in range(4) for c in range(2)),
    key=lambda o: -(8 * (o[0] + ring(o[1])) + o[2]),
)
COL_STEPS = sorted(
    ((z, y) for z in range(2) for y in range(4)), key=lambda o: -(2 * o[0] + ring(o[1]))
)
PAIR_STEPS = sorted(
    ((r, c) for r in ROW_STEPS for c in COL_STEPS),
    key=lambda p: -(8 * (depth(p[1][0], p[0][0]) + ring(p[0][1]) + ring(p[1][1])) + p[0][2]),
)


def tables():
    def circle(count, left, right):
        angle = 2.0 * np.pi * ((left[:, None] * right[None, :]) % count) / count
        return np.cos(angle), np.sin(angle)

    at = np.arange(512)
    row = 16 * (at // 8 % 16) + 8 * (at // 256) + at % 8
    imaginary = at // 128 % 2 == 1
    c, s = circle(256, np.arange(256), row)
    base_rows = np.concatenate([np.where(imaginary, s, c), np.where(imaginary, c, -s)]) / 64.0
    col = 256 * (at // 16 % 2) + 16 * (at // 32) + at % 16
    base_cols = np.stack(circle(512, col, np.arange(512))) / 64.0
    turn_rows = np.stack(circle(FULL, np.arange(NR), np.arange(256)))[:, :, None, :]
    turn_cols = np.stack(circle(FULL, np.arange(NC), col)).reshape(2, NC, 4, 1, 128)
    return (
        jnp.asarray(base_rows, BF16),
        jnp.asarray(base_cols, BF16),
        jnp.asarray(turn_rows, F32),
        jnp.asarray(turn_cols, F32),
    )


def times_unit(value, numerator, count, sign):
    real, imag = value
    step = (numerator * 8) % (count * 8)
    eighth, rest = divmod(step, count)
    if rest == 0 and eighth % 2 == 0:
        quarter = (eighth // 2) % 4
        if quarter == 0:
            return real, imag
        if quarter == 2:
            return -real, -imag
        if (quarter == 1) == (sign > 0):
            return -imag, real
        return imag, -real
    angle = 2.0 * math.pi * numerator / count
    cosine, sine = math.cos(angle), sign * math.sin(angle)
    if rest == 0:
        half = abs(cosine)
        a = (real - imag) if cosine * sine > 0 else (real + imag)
        b = (real + imag) if cosine * sine > 0 else (imag - real)
        if cosine < 0:
            return a * (-half), b * (-half)
        return a * half, b * half
    return real * cosine - imag * sine, real * sine + imag * cosine


def butterfly(values, sign):
    count = len(values)
    if count == 1:
        return values
    even = butterfly(values[0::2], sign)
    odd = butterfly(values[1::2], sign)
    low, high = [], []
    for at in range(count // 2):
        er, ei = even[at]
        tr, ti = times_unit(odd[at], at, count, sign)
        low.append((er + tr, ei + ti))
        high.append((er - tr, ei - ti))
    return low + high


def cos_sin(angle):
    half = angle * 0.5
    square = half * half
    sine = -2.5052108e-08
    for factor in (2.7557319e-06, -1.9841270e-04, 8.3333333e-03, -1.6666667e-01, 1.0):
        sine = sine * square + factor
    sine = sine * half
    cosine = 2.0876757e-09
    for factor in (-2.7557319e-07, 2.4801587e-05, -1.3888889e-03, 4.1666667e-02, -0.5, 1.0):
        cosine = cosine * square + factor
    return 1.0 - 2.0 * (sine * sine), 2.0 * (sine * cosine)


def dot(a, b):
    return jnp.dot(a, b, preferred_element_type=F32)


def dot_nt(a, b):
    return lax.dot_general(a, b, (((1,), (1,)), ((), ())), preferred_element_type=F32)


def kernel(
    shifts, mask, spec_h, diff_h, phases_h, trans_h, base_rows_h, base_cols_h, turn_rows_h, turn_cols_h, out_h,
    spec, diff, phases, trans, wr, base_cols, turn_rows, turn_cols, out,
    low0, high0, dw, trig0, trig1, wc, pick_cols, pick_rows, back_rows, tspace,
    work_b, work_z, work_y, work_r, work_d, work_s, work_f, work_o,
    sa1, rb1, sm1, rd1, sm2, rb2, sb2, ra3, low1, high1, sa3, rb3, sm3, rd3, fs, rf, ts, tr,
    in_sem, send_sem, recv_sem, halo_sem, ready_sem,
):
    rp = lax.axis_index("rows")
    cp = lax.axis_index("cols")

    z_lo, x, core = lax.div(rp, 8), lax.rem(lax.div(rp, 2), 4), lax.rem(rp, 2)
    z_hi, y = lax.div(cp, 4), lax.rem(cp, 4)

    def row_at(step):
        return lax.rem(rp + step, NR)

    def col_at(step):
        return lax.rem(cp + step, NC)

    row_peer = {
        o: lax.rem(z_lo + o[0], 2) * 8 + lax.rem(x + o[1], 4) * 2 + lax.rem(core + o[2], 2) for o in ROW_STEPS
    }
    col_peer = {o: lax.rem(z_hi + o[0], 2) * 4 + lax.rem(y + o[1], 4) for o in COL_STEPS}

    waits = []

    def finish():
        for wait in waits:
            wait()

    barrier = pltpu.get_barrier_semaphore()
    for step in (1, NR - 1):
        pl.semaphore_signal(barrier, inc=1, device_id={"rows": row_at(step)})
    for step in (1, NC - 1):
        pl.semaphore_signal(barrier, inc=1, device_id={"cols": col_at(step)})

    rounds = (("rows", 1), ("rows", 2), ("rows", 4), ("cols", 1), ("cols", 2), ("cols", 4))

    def tell(which):
        axis, reach = rounds[which]
        count, at = (NR, row_at) if axis == "rows" else (NC, col_at)
        for step in sorted({reach, count - reach}):
            pl.semaphore_signal(ready_sem.at[which], inc=1, device_id={axis: at(step)})

    def told(which):
        axis, reach = rounds[which]
        pl.semaphore_wait(ready_sem.at[which], 1 if 2 * reach == NC and axis == "cols" else 2)

    loads = {}
    for at, (name, src, dst) in enumerate((
        ("diff", diff_h, diff), ("phases", phases_h, phases), ("spec", spec_h, spec),
        ("wr", base_rows_h, wr), ("turn_rows", turn_rows_h, turn_rows), ("trans", trans_h, trans),
        ("base_cols", base_cols_h, base_cols), ("turn_cols", turn_cols_h, turn_cols),
    )):
        loads[name] = pltpu.make_async_copy(src, dst, in_sem.at[at])
        loads[name].start()

    def remote(src, dst, at, device):
        return pltpu.make_async_remote_copy(
            src_ref=src, dst_ref=dst, send_sem=send_sem.at[at], recv_sem=recv_sem.at[at], device_id=device
        )

    def rows_exchange(src, dst, at):
        for step in ROW_STEPS[:-1]:
            peer = row_peer[step]
            remote(src.at[peer], dst.at[rp], at, {"rows": peer}).start()
        pltpu.make_async_copy(src.at[rp], dst.at[rp], recv_sem.at[at]).start()
        waits.append(lambda: sent(src.at[pl.ds(0, NR - 1)], at))

    def cols_exchange(src, dst, at):
        for step in COL_STEPS[:-1]:
            peer = col_peer[step]
            remote(src.at[peer], dst.at[cp], at, {"cols": peer}).start()
        pltpu.make_async_copy(src.at[cp], dst.at[cp], recv_sem.at[at]).start()
        waits.append(lambda: sent(src.at[pl.ds(0, NC - 1)], at))

    def tiles_exchange(src, dst, at):
        for row_step, col_step in PAIR_STEPS[:-1]:
            d, g = row_peer[row_step], col_peer[col_step]
            remote(src.at[g, d], dst.at[cp, rp], at, {"rows": d, "cols": g}).start()
        pltpu.make_async_copy(src.at[cp, rp], dst.at[cp, rp], recv_sem.at[at]).start()
        waits.append(lambda: sent(src.at[pl.ds(0, NC - 1)], at))
        waits.append(lambda: sent(src.at[0, pl.ds(0, NR - 1)], at))

    def arrived(dst, at):
        pltpu.make_async_copy(dst, dst, recv_sem.at[at]).wait()

    def sent(src, at):
        pltpu.make_async_copy(src, src, send_sem.at[at]).wait()

    def halo_start(src, low, high, at):
        @pl.when(rp < NR - 1)
        def _():
            pltpu.make_async_remote_copy(
                src_ref=src, dst_ref=low, send_sem=halo_sem.at[at, 0], recv_sem=halo_sem.at[at, 1],
                device_id={"rows": rp + 1},
            ).start()

        @pl.when(rp > 0)
        def _():
            pltpu.make_async_remote_copy(
                src_ref=src, dst_ref=high, send_sem=halo_sem.at[at, 2], recv_sem=halo_sem.at[at, 3],
                device_id={"rows": rp - 1},
            ).start()

        waits.append(lambda: halo_sent(src, at))

    def halo_wait(low, high, at):
        @pl.when(rp < NR - 1)
        def _():
            pltpu.make_async_copy(high, high, halo_sem.at[at, 3]).wait()

        @pl.when(rp > 0)
        def _():
            pltpu.make_async_copy(low, low, halo_sem.at[at, 1]).wait()

    def halo_sent(src, at):
        @pl.when(rp < NR - 1)
        def _():
            pltpu.make_async_copy(src, src, halo_sem.at[at, 0]).wait()

        @pl.when(rp > 0)
        def _():
            pltpu.make_async_copy(src, src, halo_sem.at[at, 2]).wait()

    def iota(shape, axis):
        return lax.broadcasted_iota(jnp.int32, shape, axis)

    def one_hot(test):
        return jnp.where(test, 1.0, 0.0).astype(BF16)

    at_j, to_j = iota((128, 256), 0), iota((128, 256), 1)

    def banded(bounce):
        g = shifts[bounce]
        below = one_hot(to_j == at_j + 256 - g)
        above = one_hot(to_j == at_j + g - 128)
        for block in range(2):
            weights = [mask[block, m].astype(F32) for m in range(3)]
            for plane in range(2):
                left = (dot(diff[plane, block, 0], below) * weights[0]).astype(BF16)
                own = (diff[plane, block, 1].astype(F32) * weights[1]).astype(BF16)
                right = (dot(diff[plane, block, 2], above) * weights[2]).astype(BF16)
                nothing = jnp.zeros((128, 128), BF16)
                units = [left[:, :128], left[:, 128:], own, right[:, :128], right[:, 128:]]
                units = units + [nothing] if block == 0 else [nothing] + units
                for at, unit in enumerate(units):
                    which, col = at // 2, 128 * (at % 2)
                    row = 128 * block
                    if plane == 0:
                        dw[bounce, which, row:row + 128, col:col + 128] = unit
                        dw[bounce, which, 256 + row:384 + row, 256 + col:384 + col] = unit
                    else:
                        dw[bounce, which, 256 + row:384 + row, col:col + 128] = unit
                        dw[bounce, which, row:row + 128, 256 + col:384 + col] = -unit

    loads["diff"].wait()
    banded(0)

    @pl.when(rp == 0)
    def _():
        low0[...] = jnp.zeros_like(low0)
        low1[...] = jnp.zeros_like(low1)

    @pl.when(rp == NR - 1)
    def _():
        high0[...] = jnp.zeros_like(high0)
        high1[...] = jnp.zeros_like(high1)

    pl.semaphore_wait(barrier, 4)
    for h in range(2):
        halo_start(spec_h.at[:, :, pl.ds(256 * h, 256)], low0.at[h], high0.at[h], h)
    tell(0)
    loads["phases"].wait()

    def phase0(at, _):
        rows = pl.ds(pl.multiple_of(at * 32, 32), 32)
        cosine, sine = cos_sin(phases[0, rows, :])
        trig0[0, rows, :] = cosine
        trig0[1, rows, :] = sine
        return 0

    lax.fori_loop(0, 3, phase0, 0)
    told(0)
    tell(1)
    lax.fori_loop(3, 6, phase0, 0)
    told(1)
    tell(2)
    lax.fori_loop(6, 8, phase0, 0)
    loads["spec"].wait()

    for h in range(2):
        halo_wait(low0.at[h], high0.at[h], h)
        for part in range(2):
            cols = slice(256 * h + 128 * part, 256 * h + 128 * part + 128)
            here = slice(128 * part, 128 * part + 128)
            total = dot(dw[0, 1], spec[:, :, cols].reshape(512, 128))
            total = total + dot(dw[0, 0], low0[h, :, :, here].reshape(512, 128))
            total = total + dot(dw[0, 2], high0[h, :, :, here].reshape(512, 128))
            cosine, sine = trig0[0, :, cols], trig0[1, :, cols]
            real, imag = total[:256], total[256:]
            wave_re = (real * cosine - imag * sine).astype(BF16)
            wave_im = (real * sine + imag * cosine).astype(BF16)
            sa1[h, 8 * part:8 * part + 8, :, 0:256] = wave_re.T.reshape(8, 16, 256)
            sa1[h, 8 * part:8 * part + 8, :, 256:512] = wave_im.T.reshape(8, 16, 256)
        if h == 0:
            told(2)
            tell(3)
        rows_exchange(sa1.at[h], rb1.at[h], 1 + h)

    told(3)
    tell(4)

    lane = iota((512, 512), 1)
    pick_cols[...] = one_hot(iota((512, 512), 0) == (lane & 63) * 8 + (lane >> 6))
    a, b = iota((256, 256), 0), iota((256, 256), 1)
    pick_rows[...] = one_hot(b == (a & 15) * 16 + (a >> 4))
    back_rows[...] = one_hot(b == (a & 1) * 128 + ((a & 15) >> 1) * 16 + (a >> 4))

    told(4)
    tell(5)
    loads["trans"].wait()
    for half in range(2):
        cols = pl.ds(half * 256, 256)
        picked = dot(trans[...].astype(BF16), pick_cols[:, cols]).astype(BF16)
        ts[:, :, :, cols] = dot(pick_rows[...], picked).astype(BF16).reshape(NC, 2, 16, 256)
    told(5)
    cols_exchange(ts, tr, 0)

    loads["base_cols"].wait()
    c, s = base_cols[0], base_cols[1]
    wc[0:512, 0:512] = c
    wc[512:1024, 512:1024] = c
    wc[0:512, 512:1024] = s
    wc[512:1024, 0:512] = -s
    for name in ("wr", "turn_rows", "turn_cols"):
        loads[name].wait()

    lane128 = iota((1, 128), 1)
    low_half = lane128 < 64
    even_group = (lane128 & 32) == 0

    def swap_halves(first, second):
        return (
            jnp.where(low_half, first, pltpu.roll(second, 64, 1)),
            jnp.where(low_half, pltpu.roll(first, 64, 1), second),
        )

    def swap_groups(first, second):
        return (
            jnp.where(even_group, first, pltpu.roll(second, 32, 1)),
            jnp.where(even_group, pltpu.roll(first, 96, 1), second),
        )

    def quad(values):
        p0, p2 = swap_halves(values[0], values[2])
        p1, p3 = swap_halves(values[1], values[3])
        b0, b1 = swap_groups(p0, p1)
        b2, b3 = swap_groups(p2, p3)
        return [b0, b1, b2, b3]

    def forward_rows(src, h):
        def first(at, _):
            half = pl.multiple_of(at * 128, 128)
            re, im = pl.ds(half, 128), pl.ds(half + 256, 128)
            values = [(src[p, :, re].astype(F32), src[p, :, im].astype(F32)) for p in range(NR)]
            values = butterfly(values, 1)
            for r in range(NR):
                real, imag = values[r]
                cosine, sine = turn_rows[0, r, :, re], turn_rows[1, r, :, re]
                work_b[r, :, re] = (real * cosine - imag * sine).astype(BF16)
                work_b[r, :, im] = (real * sine + imag * cosine).astype(BF16)
            return 0

        lax.fori_loop(0, 2, first, 0)
        for part in range(2):
            lanes = slice(256 * part, 256 * part + 256)
            got = dot(work_b[...].reshape(256, 512), wr[:, lanes])
            work_z[:, 16 * h:16 * h + 16, lanes] = got.astype(BF16).reshape(NR, 16, 256)

    def to_cols(send, recv, at):
        for half in range(2):
            def turn(g, _):
                block = work_z[2 * g + half]
                block = jnp.concatenate([block[:, 128 * u:128 * u + 128] for u in range(4)], axis=0)
                send[half, g] = block.T.reshape(NR, 8, 128)
                return 0

            lax.fori_loop(0, NC, turn, 0)
            tiles_exchange(send.at[half], recv.at[half], at + half)

    def forward_cols(src):
        def first(at, _):
            parts = []
            for p in range(NC):
                parts.append(quad([src[p, at * 4 + low].astype(F32) for low in range(4)]))
            halves = []
            for u in range(2):
                values = butterfly([(parts[p][2 * u], parts[p][2 * u + 1]) for p in range(NC)], 1)
                for r in range(NC):
                    real, imag = values[r]
                    cosine, sine = turn_cols[0, r, at], turn_cols[1, r, at]
                    values[r] = (real * cosine - imag * sine, real * sine + imag * cosine)
                halves.append(values)
            for r in range(NC):
                for plane in range(2):
                    lanes = pl.ds(pl.multiple_of(at * 128 + 512 * plane, 128), 128)
                    rows = [halves[u][r][plane] for u in range(2)]
                    work_d[r, :, lanes] = jnp.concatenate(rows, axis=0).astype(BF16)
            return 0

        lax.fori_loop(0, 4, first, 0)

    def phase1(at, _):
        cols = pl.ds(pl.multiple_of(at * 128, 128), 128)
        cosine, sine = cos_sin(phases[1, :, cols])
        trig1[0, cols, :] = cosine.T
        trig1[1, cols, :] = sine.T
        return 0

    for h in range(2):
        arrived(rb1.at[h], 1 + h)
        forward_rows(rb1.at[h], h)
    to_cols(sm1, rd1, 3)

    lax.fori_loop(0, 4, phase1, 0)
    banded(1)

    arrived(tr, 0)
    for e in range(4):
        for q in range(4):
            src = slice(128 * q, 128 * q + 128)
            first = tr[2 * e, :, :, src].reshape(32, 128).astype(F32)
            second = tr[2 * e + 1, :, :, src].reshape(32, 128).astype(F32)
            one, two = swap_halves(first, second)
            tspace[:, 2 * q, :, 128 * e:128 * e + 128] = one.reshape(2, 16, 128)
            tspace[:, 2 * q + 1, :, 128 * e:128 * e + 128] = two.reshape(2, 16, 128)

    for half in range(2):
        arrived(rd1.at[half], 3 + half)
        forward_cols(rd1.at[half])
        for part in range(4):
            lanes = slice(256 * part, 256 * part + 256)
            kept = slice(256 * (part % 2), 256 * (part % 2) + 256)
            space = dot(work_d[...].reshape(128, 1024), wc[:, lanes])
            work_s[:, lanes] = (space * tspace[half, :, :, kept].reshape(128, 256)).astype(BF16)
        for part in range(4):
            lanes = slice(256 * part, 256 * part + 256)
            work_f[:, :, lanes] = dot_nt(work_s[...], wc[lanes, :]).reshape(NC, 16, 256)

        def last_cols(at, _):
            re = pl.ds(pl.multiple_of(at * 128, 128), 128)
            im = pl.ds(pl.multiple_of(at * 128 + 512, 128), 128)
            parts = []
            for u in range(2):
                values = []
                for r in range(NC):
                    real, imag = work_f[r, 8 * u:8 * u + 8, re], work_f[r, 8 * u:8 * u + 8, im]
                    cosine, sine = turn_cols[0, r, at], turn_cols[1, r, at]
                    values.append((real * cosine + imag * sine, imag * cosine - real * sine))
                parts.append(butterfly(values, -1))
            for q in range(NC):
                tiles = quad([parts[0][q][0], parts[0][q][1], parts[1][q][0], parts[1][q][1]])
                for low in range(4):
                    sm2[half, q, at * 4 + low] = tiles[low].astype(BF16)
            return 0

        lax.fori_loop(0, 4, last_cols, 0)

        tiles_exchange(sm2.at[half], rb2.at[half], 11 + half)

    for half in range(2):
        arrived(rb2.at[half], 11 + half)

        def untile(g, _):
            block = rb2[half, g].reshape(128, 128).T
            for u in range(4):
                work_y[g, :, 128 * u:128 * u + 128] = block[32 * u:32 * u + 32]
            return 0

        lax.fori_loop(0, NC, untile, 0)
        for part in range(2):
            lanes = slice(256 * part, 256 * part + 256)
            got = dot_nt(work_y[...].reshape(256, 512), wr[lanes, :])
            work_r[half, :, :, lanes] = got.reshape(NC, 32, 256)
    for h in range(2):
        crow = slice(16 * h, 16 * h + 16)

        def sources(at, _):
            half = pl.multiple_of(at * 128, 128)
            re, im = pl.ds(half, 128), pl.ds(half + 256, 128)
            values = []
            for r in range(NR):
                real, imag = work_r[r % 2, r // 2, crow, re], work_r[r % 2, r // 2, crow, im]
                cosine, sine = turn_rows[0, r, :, re], turn_rows[1, r, :, re]
                values.append((real * cosine + imag * sine, imag * cosine - real * sine))
            values = butterfly(values, -1)
            for r in range(NR):
                sb2[h, r, :, re] = values[r][0].astype(BF16)
                sb2[h, r, :, im] = values[r][1].astype(BF16)
            return 0

        lax.fori_loop(0, 2, sources, 0)
        rows_exchange(sb2.at[h], ra3.at[h], 5 + h)

    for h in range(2):
        arrived(ra3.at[h], 5 + h)
        halo_start(ra3.at[h], low1.at[h], high1.at[h], 2 + h)

    for h in range(2):
        halo_wait(low1.at[h], high1.at[h], 2 + h)
        total = dot_nt(ra3[h].reshape(256, 512), dw[1, 1])
        total = total + dot_nt(low1[h].reshape(256, 512), dw[1, 0])
        total = total + dot_nt(high1[h].reshape(256, 512), dw[1, 2])
        rows = slice(256 * h, 256 * h + 256)
        cosine, sine = trig1[0, rows, :], trig1[1, rows, :]
        real, imag = total[:, :256], total[:, 256:]
        sa3[h, :, :, 0:256] = (real * cosine - imag * sine).astype(BF16).reshape(NR, 16, 256)
        sa3[h, :, :, 256:512] = (real * sine + imag * cosine).astype(BF16).reshape(NR, 16, 256)
        rows_exchange(sa3.at[h], rb3.at[h], 7 + h)
    for h in range(2):
        arrived(rb3.at[h], 7 + h)
        forward_rows(rb3.at[h], h)
    to_cols(sm3, rd3, 9)
    for half in range(2):
        arrived(rd3.at[half], 9 + half)
        forward_cols(rd3.at[half])
        for part in range(4):
            lanes = slice(256 * part, 256 * part + 256)
            work_f[:, :, lanes] = dot(work_d[...].reshape(128, 1024), wc[:, lanes]).reshape(NC, 16, 256)
        for plane in range(2):
            for q in range(4):
                for e in range(4):
                    src = slice(512 * plane + 128 * e, 512 * plane + 128 * e + 128)
                    lanes_to = slice(512 * plane + 128 * q, 512 * plane + 128 * q + 128)
                    one, two = swap_halves(work_f[2 * q, :, src], work_f[2 * q + 1, :, src])
                    fs[half, 2 * e, :, lanes_to] = one.astype(BF16)
                    fs[half, 2 * e + 1, :, lanes_to] = two.astype(BF16)
        cols_exchange(fs.at[half], rf.at[half], 13 + half)
    for half in range(2):
        arrived(rf.at[half], 13 + half)
        for plane in range(2):
            lanes = slice(512 * plane, 512 * plane + 512)
            ordered = dot_nt(rf[half, :, :, lanes].reshape(128, 512), pick_cols[...])
            work_o[plane, 128 * half:128 * half + 128, :] = ordered.astype(BF16)
    for plane in range(2):
        out[plane] = dot(back_rows[...], work_o[plane]).astype(BF16)
        result = pltpu.make_async_copy(out.at[plane], out_h.at[plane], in_sem.at[9 + plane])
        result.start()
        waits.append(result.wait)

    finish()


def on_device(spectrum, diffraction, order_mask, phases, transmission, shifts):
    anywhere = pl.BlockSpec(memory_space=pl.ANY)
    smem = pl.BlockSpec(memory_space=pltpu.SMEM)
    constants = tables()
    operands = (spectrum, diffraction, phases, transmission) + constants

    def vmem(kind, *shape):
        return pltpu.VMEM(shape, kind)

    halves = (2, NR, 16, 512)
    space = pl.pallas_call(
        kernel,
        out_shape=jax.ShapeDtypeStruct((2, 256, 512), BF16),
        in_specs=[smem, smem] + [anywhere] * len(operands),
        out_specs=anywhere,
        scratch_shapes=[pltpu.VMEM(x.shape, x.dtype) for x in operands] + [
            vmem(BF16, 2, 256, 512),
            vmem(BF16, 2, 2, 256, 256), vmem(BF16, 2, 2, 256, 256),
            vmem(BF16, 2, 3, 512, 512),
            vmem(F32, 2, 256, 512),
            vmem(F32, 2, 512, 256),
            vmem(BF16, 1024, 1024),
            vmem(BF16, 512, 512), vmem(BF16, 256, 256), vmem(BF16, 256, 256),
            vmem(F32, 2, NC, 16, 512),
            vmem(BF16, NR, 16, 512),
            vmem(BF16, NR, 32, 512),
            vmem(BF16, NC, 32, 512),
            vmem(F32, 2, NC, 32, 512),
            vmem(BF16, NC, 16, 1024),
            vmem(BF16, 128, 1024),
            vmem(F32, NC, 16, 1024),
            vmem(BF16, 2, 256, 512),
            vmem(BF16, *halves), vmem(BF16, *halves),
            vmem(BF16, 2, NC, NR, 8, 128), vmem(BF16, 2, NC, NR, 8, 128),
            vmem(BF16, 2, NC, NR, 8, 128), vmem(BF16, 2, NC, NR, 8, 128),
            vmem(BF16, *halves), vmem(BF16, *halves),
            vmem(BF16, *halves), vmem(BF16, *halves),
            vmem(BF16, *halves), vmem(BF16, *halves),
            vmem(BF16, 2, NC, NR, 8, 128), vmem(BF16, 2, NC, NR, 8, 128),
            vmem(BF16, 2, NC, 16, 1024), vmem(BF16, 2, NC, 16, 1024),
            vmem(BF16, NC, 2, 16, 512), vmem(BF16, NC, 2, 16, 512),
            pltpu.SemaphoreType.DMA((11,)),
            pltpu.SemaphoreType.DMA((15,)),
            pltpu.SemaphoreType.DMA((15,)),
            pltpu.SemaphoreType.DMA((4, 4)),
            pltpu.SemaphoreType.REGULAR((6,)),
        ],
        compiler_params=pltpu.CompilerParams(
            collective_id=0, has_side_effects=True, vmem_limit_bytes=60 * 1024 * 1024
        ),
    )(shifts, order_mask, *operands)
    return space.astype(F32) * transmission[None]


def solution(mesh):
    placed = (
        P(None, "rows", "cols"),
        P(None, "rows", None, None, None),
        P("rows", None),
        P(None, "rows", "cols"),
        P("rows", "cols"),
        P(),
    )
    return jax.shard_map(
        on_device, mesh=mesh, in_specs=placed, out_specs=P(None, "rows", "cols"), check_vma=False
    )
```

```python
import math

import jax
import jax.numpy as jnp
import numpy as np
from jax import lax
from jax.experimental import pallas as pl
from jax.experimental.pallas import tpu as pltpu
from jax.sharding import PartitionSpec as P

F32 = jnp.float32
BF16 = jnp.bfloat16
NR = 16
NC = 8
FULL = 4096


def ring(step):
    return min(step, 4 - step)


def depth(high, low):
    return (0, 1, 2, 1)[2 * high + low]


ROW_STEPS = sorted(
    ((z, x, c) for z in range(2) for x in range(4) for c in range(2)),
    key=lambda o: -(8 * (o[0] + ring(o[1])) + o[2]),
)
COL_STEPS = sorted(
    ((z, y) for z in range(2) for y in range(4)), key=lambda o: -(2 * o[0] + ring(o[1]))
)
PAIR_STEPS = sorted(
    ((r, c) for r in ROW_STEPS for c in COL_STEPS),
    key=lambda p: -(8 * (depth(p[1][0], p[0][0]) + ring(p[0][1]) + ring(p[1][1])) + p[0][2]),
)


def tables():
    def circle(count, left, right):
        angle = 2.0 * np.pi * ((left[:, None] * right[None, :]) % count) / count
        return np.cos(angle), np.sin(angle)

    at = np.arange(512)
    row = 16 * (at // 8 % 16) + 8 * (at // 256) + at % 8
    imaginary = at // 128 % 2 == 1
    c, s = circle(256, np.arange(256), row)
    base_rows = np.concatenate([np.where(imaginary, s, c), np.where(imaginary, c, -s)]) / 64.0
    c, s = circle(256, np.arange(256), np.arange(256))
    base_cols = np.block([[c, s], [-s, c]]) / 64.0
    turn_rows = np.stack(circle(FULL, np.arange(NR), np.arange(256)))[:, :, None, :]
    return (
        jnp.asarray(base_rows, BF16),
        jnp.asarray(base_cols, BF16),
        jnp.asarray(turn_rows, F32),
    )


def times_unit(value, numerator, count, sign):
    real, imag = value
    step = (numerator * 8) % (count * 8)
    eighth, rest = divmod(step, count)
    if rest == 0 and eighth % 2 == 0:
        quarter = (eighth // 2) % 4
        if quarter == 0:
            return real, imag
        if quarter == 2:
            return -real, -imag
        if (quarter == 1) == (sign > 0):
            return -imag, real
        return imag, -real
    angle = 2.0 * math.pi * numerator / count
    cosine, sine = math.cos(angle), sign * math.sin(angle)
    if rest == 0:
        half = abs(cosine)
        a = (real - imag) if cosine * sine > 0 else (real + imag)
        b = (real + imag) if cosine * sine > 0 else (imag - real)
        if cosine < 0:
            return a * (-half), b * (-half)
        return a * half, b * half
    return real * cosine - imag * sine, real * sine + imag * cosine


def butterfly(values, sign):
    count = len(values)
    if count == 1:
        return values
    even = butterfly(values[0::2], sign)
    odd = butterfly(values[1::2], sign)
    low, high = [], []
    for at in range(count // 2):
        er, ei = even[at]
        tr, ti = times_unit(odd[at], at, count, sign)
        low.append((er + tr, ei + ti))
        high.append((er - tr, ei - ti))
    return low + high


def cos_sin(angle):
    half = angle * 0.5
    square = half * half
    sine = -2.5052108e-08
    for factor in (2.7557319e-06, -1.9841270e-04, 8.3333333e-03, -1.6666667e-01, 1.0):
        sine = sine * square + factor
    sine = sine * half
    cosine = 2.0876757e-09
    for factor in (-2.7557319e-07, 2.4801587e-05, -1.3888889e-03, 4.1666667e-02, -0.5, 1.0):
        cosine = cosine * square + factor
    return 1.0 - 2.0 * (sine * sine), 2.0 * (sine * cosine)


def dot(a, b):
    return jnp.dot(a, b, preferred_element_type=F32)


def dot_nt(a, b):
    return lax.dot_general(a, b, (((1,), (1,)), ((), ())), preferred_element_type=F32)


def kernel(
    shifts, mask, spec_h, diff_h, phases_h, trans_h, base_rows_h, base_cols_h, turn_rows_h, out_h,
    spec, diff, phases, trans, wr, wc, turn_rows, out,
    low0, high0, dw, trig0, trig1, pick_cols, pick_rows, back_rows, tspace,
    work_b, work_z, work_y, work_r, work_d, work_s, work_x, work_o,
    sa1, rb1, sm1, rd1, sm2, rb2, sb2, ra3, low1, high1, sa3, rb3, sm3, rd3, fs, rf, ts, tr,
    in_sem, send_sem, recv_sem, halo_sem, ready_sem,
):
    rp = lax.axis_index("rows")
    cp = lax.axis_index("cols")

    z_lo, x, core = lax.div(rp, 8), lax.rem(lax.div(rp, 2), 4), lax.rem(rp, 2)
    z_hi, y = lax.div(cp, 4), lax.rem(cp, 4)

    def row_at(step):
        return lax.rem(rp + step, NR)

    def col_at(step):
        return lax.rem(cp + step, NC)

    row_peer = {
        o: lax.rem(z_lo + o[0], 2) * 8 + lax.rem(x + o[1], 4) * 2 + lax.rem(core + o[2], 2) for o in ROW_STEPS
    }
    col_peer = {o: lax.rem(z_hi + o[0], 2) * 4 + lax.rem(y + o[1], 4) for o in COL_STEPS}

    waits = []

    def finish():
        for wait in waits:
            wait()

    barrier = pltpu.get_barrier_semaphore()
    for step in (1, NR - 1):
        pl.semaphore_signal(barrier, inc=1, device_id={"rows": row_at(step)})
    for step in (1, NC - 1):
        pl.semaphore_signal(barrier, inc=1, device_id={"cols": col_at(step)})

    rounds = (("rows", 1), ("rows", 2), ("rows", 4), ("cols", 1), ("cols", 2), ("cols", 4))

    def tell(which):
        axis, reach = rounds[which]
        count, at = (NR, row_at) if axis == "rows" else (NC, col_at)
        for step in sorted({reach, count - reach}):
            pl.semaphore_signal(ready_sem.at[which], inc=1, device_id={axis: at(step)})

    def told(which):
        axis, reach = rounds[which]
        pl.semaphore_wait(ready_sem.at[which], 1 if 2 * reach == NC and axis == "cols" else 2)

    loads = {}
    for at, (name, src, dst) in enumerate((
        ("diff", diff_h, diff), ("phases", phases_h, phases), ("spec", spec_h, spec),
        ("wr", base_rows_h, wr), ("turn_rows", turn_rows_h, turn_rows), ("trans", trans_h, trans),
        ("wc", base_cols_h, wc),
    )):
        loads[name] = pltpu.make_async_copy(src, dst, in_sem.at[at])
        loads[name].start()

    def remote(src, dst, at, device):
        return pltpu.make_async_remote_copy(
            src_ref=src, dst_ref=dst, send_sem=send_sem.at[at], recv_sem=recv_sem.at[at], device_id=device
        )

    def rows_exchange(src, dst, at):
        for step in ROW_STEPS[:-1]:
            peer = row_peer[step]
            remote(src.at[peer], dst.at[rp], at, {"rows": peer}).start()
        pltpu.make_async_copy(src.at[rp], dst.at[rp], recv_sem.at[at]).start()
        waits.append(lambda: sent(src.at[pl.ds(0, NR - 1)], at))

    def cols_exchange(src, dst, at):
        for step in COL_STEPS[:-1]:
            peer = col_peer[step]
            remote(src.at[peer], dst.at[cp], at, {"cols": peer}).start()
        pltpu.make_async_copy(src.at[cp], dst.at[cp], recv_sem.at[at]).start()
        waits.append(lambda: sent(src.at[pl.ds(0, NC - 1)], at))

    def tiles_exchange(src, dst, at):
        for row_step, col_step in PAIR_STEPS[:-1]:
            d, g = row_peer[row_step], col_peer[col_step]
            remote(src.at[g, d], dst.at[cp, rp], at, {"rows": d, "cols": g}).start()
        pltpu.make_async_copy(src.at[cp, rp], dst.at[cp, rp], recv_sem.at[at]).start()
        waits.append(lambda: sent(src.at[pl.ds(0, NC - 1)], at))
        waits.append(lambda: sent(src.at[0, pl.ds(0, NR - 1)], at))

    def arrived(dst, at):
        pltpu.make_async_copy(dst, dst, recv_sem.at[at]).wait()

    def sent(src, at):
        pltpu.make_async_copy(src, src, send_sem.at[at]).wait()

    def halo_start(src, low, high, at):
        @pl.when(rp < NR - 1)
        def _():
            pltpu.make_async_remote_copy(
                src_ref=src, dst_ref=low, send_sem=halo_sem.at[at, 0], recv_sem=halo_sem.at[at, 1],
                device_id={"rows": rp + 1},
            ).start()

        @pl.when(rp > 0)
        def _():
            pltpu.make_async_remote_copy(
                src_ref=src, dst_ref=high, send_sem=halo_sem.at[at, 2], recv_sem=halo_sem.at[at, 3],
                device_id={"rows": rp - 1},
            ).start()

        waits.append(lambda: halo_sent(src, at))

    def halo_wait(low, high, at):
        @pl.when(rp < NR - 1)
        def _():
            pltpu.make_async_copy(high, high, halo_sem.at[at, 3]).wait()

        @pl.when(rp > 0)
        def _():
            pltpu.make_async_copy(low, low, halo_sem.at[at, 1]).wait()

    def halo_sent(src, at):
        @pl.when(rp < NR - 1)
        def _():
            pltpu.make_async_copy(src, src, halo_sem.at[at, 0]).wait()

        @pl.when(rp > 0)
        def _():
            pltpu.make_async_copy(src, src, halo_sem.at[at, 2]).wait()

    def iota(shape, axis):
        return lax.broadcasted_iota(jnp.int32, shape, axis)

    def one_hot(test):
        return jnp.where(test, 1.0, 0.0).astype(BF16)

    at_j, to_j = iota((128, 256), 0), iota((128, 256), 1)

    def banded(bounce):
        g = shifts[bounce]
        below = one_hot(to_j == at_j + 256 - g)
        above = one_hot(to_j == at_j + g - 128)
        for block in range(2):
            weights = [mask[block, m].astype(F32) for m in range(3)]
            for plane in range(2):
                left = (dot(diff[plane, block, 0], below) * weights[0]).astype(BF16)
                own = (diff[plane, block, 1].astype(F32) * weights[1]).astype(BF16)
                right = (dot(diff[plane, block, 2], above) * weights[2]).astype(BF16)
                nothing = jnp.zeros((128, 128), BF16)
                units = [left[:, :128], left[:, 128:], own, right[:, :128], right[:, 128:]]
                units = units + [nothing] if block == 0 else [nothing] + units
                for at, unit in enumerate(units):
                    which, col = at // 2, 128 * (at % 2)
                    row = 128 * block
                    if plane == 0:
                        dw[bounce, which, row:row + 128, col:col + 128] = unit
                        dw[bounce, which, 256 + row:384 + row, 256 + col:384 + col] = unit
                    else:
                        dw[bounce, which, 256 + row:384 + row, col:col + 128] = unit
                        dw[bounce, which, row:row + 128, 256 + col:384 + col] = -unit

    loads["diff"].wait()
    banded(0)

    @pl.when(rp == 0)
    def _():
        low0[...] = jnp.zeros_like(low0)
        low1[...] = jnp.zeros_like(low1)

    @pl.when(rp == NR - 1)
    def _():
        high0[...] = jnp.zeros_like(high0)
        high1[...] = jnp.zeros_like(high1)

    pl.semaphore_wait(barrier, 4)
    for h in range(2):
        halo_start(spec_h.at[:, :, pl.ds(256 * h, 256)], low0.at[h], high0.at[h], h)
    tell(0)
    loads["phases"].wait()

    def phase0(at, _):
        rows = pl.ds(pl.multiple_of(at * 32, 32), 32)
        cosine, sine = cos_sin(phases[0, rows, :])
        trig0[0, rows, :] = cosine
        trig0[1, rows, :] = sine
        return 0

    lax.fori_loop(0, 3, phase0, 0)
    told(0)
    tell(1)
    lax.fori_loop(3, 6, phase0, 0)
    told(1)
    tell(2)
    lax.fori_loop(6, 8, phase0, 0)
    loads["spec"].wait()

    for h in range(2):
        halo_wait(low0.at[h], high0.at[h], h)
        for part in range(2):
            cols = slice(256 * h + 128 * part, 256 * h + 128 * part + 128)
            here = slice(128 * part, 128 * part + 128)
            total = dot(dw[0, 1], spec[:, :, cols].reshape(512, 128))
            total = total + dot(dw[0, 0], low0[h, :, :, here].reshape(512, 128))
            total = total + dot(dw[0, 2], high0[h, :, :, here].reshape(512, 128))
            cosine, sine = trig0[0, :, cols], trig0[1, :, cols]
            real, imag = total[:256], total[256:]
            wave_re = (real * cosine - imag * sine).astype(BF16)
            wave_im = (real * sine + imag * cosine).astype(BF16)
            sa1[h, 8 * part:8 * part + 8, :, 0:256] = wave_re.T.reshape(8, 16, 256)
            sa1[h, 8 * part:8 * part + 8, :, 256:512] = wave_im.T.reshape(8, 16, 256)
        if h == 0:
            told(2)
            tell(3)
        rows_exchange(sa1.at[h], rb1.at[h], 1 + h)

    told(3)
    tell(4)

    lane = iota((512, 512), 1)
    pick_cols[...] = one_hot(iota((512, 512), 0) == (lane & 31) * 16 + (lane >> 5))
    a, b = iota((256, 256), 0), iota((256, 256), 1)
    pick_rows[...] = one_hot(b == (a & 15) * 16 + (a >> 4))
    back_rows[...] = one_hot(b == (a & 1) * 128 + ((a & 15) >> 1) * 16 + (a >> 4))

    told(4)
    tell(5)
    loads["trans"].wait()
    for half in range(2):
        cols = pl.ds(half * 256, 256)
        picked = dot(trans[...].astype(BF16), pick_cols[:, cols]).astype(BF16)
        ts[:, :, :, cols] = dot(pick_rows[...], picked).astype(BF16).reshape(NC, 2, 16, 256)
    told(5)
    cols_exchange(ts, tr, 0)

    for name in ("wr", "wc", "turn_rows"):
        loads[name].wait()

    lane128 = iota((1, 128), 1)

    def swap(first, second, size):
        even = (lane128 & size) == 0
        return (
            jnp.where(even, first, pltpu.roll(second, size, 1)),
            jnp.where(even, pltpu.roll(first, 128 - size, 1), second),
        )

    def crossed(values):
        reach = len(values) // 2
        while reach:
            size = reach * (128 // len(values))
            result = list(values)
            for at in range(len(values)):
                if at & reach == 0:
                    result[at], result[at + reach] = swap(values[at], values[at + reach], size)
            values = result
            reach //= 2
        return values

    def forward_rows(src, h):
        def first(at, _):
            half = pl.multiple_of(at * 128, 128)
            re, im = pl.ds(half, 128), pl.ds(half + 256, 128)
            values = [(src[p, :, re].astype(F32), src[p, :, im].astype(F32)) for p in range(NR)]
            values = butterfly(values, 1)
            for r in range(NR):
                real, imag = values[r]
                cosine, sine = turn_rows[0, r, :, re], turn_rows[1, r, :, re]
                work_b[r, :, re] = (real * cosine - imag * sine).astype(BF16)
                work_b[r, :, im] = (real * sine + imag * cosine).astype(BF16)
            return 0

        lax.fori_loop(0, 2, first, 0)
        for part in range(2):
            lanes = slice(256 * part, 256 * part + 256)
            got = dot(work_b[...].reshape(256, 512), wr[:, lanes])
            work_z[:, 16 * h:16 * h + 16, lanes] = got.astype(BF16).reshape(NR, 16, 256)

    def to_cols(send, recv, at):
        for half in range(2):
            def turn(g, _):
                block = work_z[2 * g + half]
                block = jnp.concatenate([block[:, 128 * u:128 * u + 128] for u in range(4)], axis=0)
                send[half, g] = block.T.reshape(NR, 8, 128)
                return 0

            lax.fori_loop(0, NC, turn, 0)
            tiles_exchange(send.at[half], recv.at[half], at + half)

    def forward_cols(src):
        def first(at, _):
            lanes = pl.ds(pl.multiple_of(at * 128, 128), 128)
            lanes2 = pl.ds(pl.multiple_of(at * 128 + 256, 128), 128)
            for p in range(NC):
                parts = crossed([src[p, at * 8 + low].astype(F32) for low in range(8)])
                for k in range(8):
                    work_x[k // 4, k // 2 % 2, 2 * p + k % 2] = parts[k]
            for u in range(2):
                values = butterfly([(work_x[u, 0, p], work_x[u, 1, p]) for p in range(NR)], 1)
                for r in range(NR):
                    real, imag = values[r]
                    cosine, sine = turn_rows[0, r, :, lanes], turn_rows[1, r, :, lanes]
                    rows = slice(8 * u, 8 * u + 8)
                    work_d[r, rows, lanes] = real * cosine - imag * sine
                    work_d[r, rows, lanes2] = real * sine + imag * cosine
            return 0

        lax.fori_loop(0, 2, first, 0)

    def phase1(at, _):
        cols = pl.ds(pl.multiple_of(at * 128, 128), 128)
        cosine, sine = cos_sin(phases[1, :, cols])
        trig1[0, cols, :] = cosine.T
        trig1[1, cols, :] = sine.T
        return 0

    for h in range(2):
        arrived(rb1.at[h], 1 + h)
        forward_rows(rb1.at[h], h)
    to_cols(sm1, rd1, 3)

    lax.fori_loop(0, 4, phase1, 0)
    banded(1)

    arrived(tr, 0)
    for e in range(2):
        for q in range(4):
            src = slice(128 * q, 128 * q + 128)
            got = crossed([tr[4 * e + k, :, :, src].reshape(32, 128).astype(F32) for k in range(4)])
            for k in range(4):
                tspace[:, 4 * q + k, :, 128 * e:128 * e + 128] = got[k].reshape(2, 16, 128)

    for half in range(2):
        arrived(rd1.at[half], 3 + half)
        forward_cols(rd1.at[half])
        rows = work_d[...].astype(BF16).reshape(256, 512)
        for part in range(2):
            lanes = slice(256 * part, 256 * part + 256)
            space = dot(rows, wc[:, lanes])
            work_s[:, lanes] = (space * tspace[half].reshape(256, 256)).astype(BF16)
        for part in range(2):
            lanes = slice(256 * part, 256 * part + 256)
            work_d[:, :, lanes] = dot_nt(work_s[...], wc[lanes, :]).reshape(NR, 16, 256)

        def last_cols(at, _):
            re = pl.ds(pl.multiple_of(at * 128, 128), 128)
            im = pl.ds(pl.multiple_of(at * 128 + 256, 128), 128)
            for u in range(2):
                values = []
                for r in range(NR):
                    real, imag = work_d[r, 8 * u:8 * u + 8, re], work_d[r, 8 * u:8 * u + 8, im]
                    cosine, sine = turn_rows[0, r, :, re], turn_rows[1, r, :, re]
                    values.append((real * cosine + imag * sine, imag * cosine - real * sine))
                values = butterfly(values, -1)
                for r in range(NR):
                    work_x[u, 0, r], work_x[u, 1, r] = values[r]
            for q in range(NC):
                tiles = crossed([work_x[k // 4, k // 2 % 2, 2 * q + k % 2] for k in range(8)])
                for low in range(8):
                    sm2[half, q, at * 8 + low] = tiles[low].astype(BF16)
            return 0

        lax.fori_loop(0, 2, last_cols, 0)
        tiles_exchange(sm2.at[half], rb2.at[half], 11 + half)

    for half in range(2):
        arrived(rb2.at[half], 11 + half)

        def untile(g, _):
            block = rb2[half, g].reshape(128, 128).T
            for u in range(4):
                work_y[g, :, 128 * u:128 * u + 128] = block[32 * u:32 * u + 32]
            return 0

        lax.fori_loop(0, NC, untile, 0)
        for part in range(2):
            lanes = slice(256 * part, 256 * part + 256)
            got = dot_nt(work_y[...].reshape(256, 512), wr[lanes, :])
            work_r[half, :, :, lanes] = got.reshape(NC, 32, 256)
    for h in range(2):
        crow = slice(16 * h, 16 * h + 16)

        def sources(at, _):
            half = pl.multiple_of(at * 128, 128)
            re, im = pl.ds(half, 128), pl.ds(half + 256, 128)
            values = []
            for r in range(NR):
                real, imag = work_r[r % 2, r // 2, crow, re], work_r[r % 2, r // 2, crow, im]
                cosine, sine = turn_rows[0, r, :, re], turn_rows[1, r, :, re]
                values.append((real * cosine + imag * sine, imag * cosine - real * sine))
            values = butterfly(values, -1)
            for r in range(NR):
                sb2[h, r, :, re] = values[r][0].astype(BF16)
                sb2[h, r, :, im] = values[r][1].astype(BF16)
            return 0

        lax.fori_loop(0, 2, sources, 0)
        rows_exchange(sb2.at[h], ra3.at[h], 5 + h)

    for h in range(2):
        arrived(ra3.at[h], 5 + h)
        halo_start(ra3.at[h], low1.at[h], high1.at[h], 2 + h)

    for h in range(2):
        halo_wait(low1.at[h], high1.at[h], 2 + h)
        total = dot_nt(ra3[h].reshape(256, 512), dw[1, 1])
        total = total + dot_nt(low1[h].reshape(256, 512), dw[1, 0])
        total = total + dot_nt(high1[h].reshape(256, 512), dw[1, 2])
        rows = slice(256 * h, 256 * h + 256)
        cosine, sine = trig1[0, rows, :], trig1[1, rows, :]
        real, imag = total[:, :256], total[:, 256:]
        sa3[h, :, :, 0:256] = (real * cosine - imag * sine).astype(BF16).reshape(NR, 16, 256)
        sa3[h, :, :, 256:512] = (real * sine + imag * cosine).astype(BF16).reshape(NR, 16, 256)
        rows_exchange(sa3.at[h], rb3.at[h], 7 + h)
    for h in range(2):
        arrived(rb3.at[h], 7 + h)
        forward_rows(rb3.at[h], h)
    to_cols(sm3, rd3, 9)
    for half in range(2):
        arrived(rd3.at[half], 9 + half)
        forward_cols(rd3.at[half])
        rows = work_d[...].astype(BF16).reshape(256, 512)
        for plane in range(2):
            lanes = slice(256 * plane, 256 * plane + 256)
            work_d[:, :, lanes] = dot(rows, wc[:, lanes]).reshape(NR, 16, 256)
            for q in range(4):
                for e in range(2):
                    src = slice(256 * plane + 128 * e, 256 * plane + 128 * e + 128)
                    lanes_to = slice(512 * plane + 128 * q, 512 * plane + 128 * q + 128)
                    got = crossed([work_d[4 * q + k, :, src] for k in range(4)])
                    for k in range(4):
                        fs[half, 4 * e + k, :, lanes_to] = got[k].astype(BF16)
        cols_exchange(fs.at[half], rf.at[half], 13 + half)
    for half in range(2):
        arrived(rf.at[half], 13 + half)
        for plane in range(2):
            lanes = slice(512 * plane, 512 * plane + 512)
            ordered = dot_nt(rf[half, :, :, lanes].reshape(128, 512), pick_cols[...])
            work_o[plane, 128 * half:128 * half + 128, :] = ordered.astype(BF16)
    for plane in range(2):
        out[plane] = dot(back_rows[...], work_o[plane]).astype(BF16)
        result = pltpu.make_async_copy(out.at[plane], out_h.at[plane], in_sem.at[9 + plane])
        result.start()
        waits.append(result.wait)

    finish()


def on_device(spectrum, diffraction, order_mask, phases, transmission, shifts):
    anywhere = pl.BlockSpec(memory_space=pl.ANY)
    smem = pl.BlockSpec(memory_space=pltpu.SMEM)
    constants = tables()
    operands = (spectrum, diffraction, phases, transmission) + constants

    def vmem(kind, *shape):
        return pltpu.VMEM(shape, kind)

    halves = (2, NR, 16, 512)
    space = pl.pallas_call(
        kernel,
        out_shape=jax.ShapeDtypeStruct((2, 256, 512), BF16),
        in_specs=[smem, smem] + [anywhere] * len(operands),
        out_specs=anywhere,
        scratch_shapes=[pltpu.VMEM(x.shape, x.dtype) for x in operands] + [
            vmem(BF16, 2, 256, 512),
            vmem(BF16, 2, 2, 256, 256), vmem(BF16, 2, 2, 256, 256),
            vmem(BF16, 2, 3, 512, 512),
            vmem(F32, 2, 256, 512),
            vmem(F32, 2, 512, 256),
            vmem(BF16, 512, 512), vmem(BF16, 256, 256), vmem(BF16, 256, 256),
            vmem(F32, 2, NR, 16, 256),
            vmem(BF16, NR, 16, 512),
            vmem(BF16, NR, 32, 512),
            vmem(BF16, NC, 32, 512),
            vmem(F32, 2, NC, 32, 512),
            vmem(F32, NR, 16, 512),
            vmem(BF16, 256, 512),
            vmem(F32, 2, 2, NR, 8, 128),
            vmem(BF16, 2, 256, 512),
            vmem(BF16, *halves), vmem(BF16, *halves),
            vmem(BF16, 2, NC, NR, 8, 128), vmem(BF16, 2, NC, NR, 8, 128),
            vmem(BF16, 2, NC, NR, 8, 128), vmem(BF16, 2, NC, NR, 8, 128),
            vmem(BF16, *halves), vmem(BF16, *halves),
            vmem(BF16, *halves), vmem(BF16, *halves),
            vmem(BF16, *halves), vmem(BF16, *halves),
            vmem(BF16, 2, NC, NR, 8, 128), vmem(BF16, 2, NC, NR, 8, 128),
            vmem(BF16, 2, NC, 16, 1024), vmem(BF16, 2, NC, 16, 1024),
            vmem(BF16, NC, 2, 16, 512), vmem(BF16, NC, 2, 16, 512),
            pltpu.SemaphoreType.DMA((11,)),
            pltpu.SemaphoreType.DMA((15,)),
            pltpu.SemaphoreType.DMA((15,)),
            pltpu.SemaphoreType.DMA((4, 4)),
            pltpu.SemaphoreType.REGULAR((6,)),
        ],
        compiler_params=pltpu.CompilerParams(
            collective_id=0, has_side_effects=True, vmem_limit_bytes=60 * 1024 * 1024
        ),
    )(shifts, order_mask, *operands)
    return space.astype(F32) * transmission[None]


def solution(mesh):
    placed = (
        P(None, "rows", "cols"),
        P(None, "rows", None, None, None),
        P("rows", None),
        P(None, "rows", "cols"),
        P("rows", "cols"),
        P(),
    )
    return jax.shard_map(
        on_device, mesh=mesh, in_specs=placed, out_specs=P(None, "rows", "cols"), check_vma=False
    )
```

```python
import math

import jax
import jax.numpy as jnp
import numpy as np
from jax import lax
from jax.experimental import pallas as pl
from jax.experimental.pallas import tpu as pltpu
from jax.sharding import PartitionSpec as P

F32 = jnp.float32
BF16 = jnp.bfloat16
NR = 16
NC = 8
FULL = 4096
CHUNKS = 4


def ring(step):
    return min(step, 4 - step)


def depth(high, low):
    return (0, 1, 2, 1)[2 * high + low]


ROW_STEPS = sorted(
    ((z, x, c) for z in range(2) for x in range(4) for c in range(2)),
    key=lambda o: -(8 * (o[0] + ring(o[1])) + o[2]),
)
COL_STEPS = sorted(
    ((z, y) for z in range(2) for y in range(4)), key=lambda o: -(2 * o[0] + ring(o[1]))
)
PAIR_STEPS = sorted(
    ((r, c) for r in ROW_STEPS for c in COL_STEPS),
    key=lambda p: -(8 * (depth(p[1][0], p[0][0]) + ring(p[0][1]) + ring(p[1][1])) + p[0][2]),
)


def tables():
    def circle(count, left, right):
        angle = 2.0 * np.pi * ((left[:, None] * right[None, :]) % count) / count
        return np.cos(angle), np.sin(angle)

    at = np.arange(512)
    row = 16 * (at // 8 % 16) + 8 * (at // 256) + at % 8
    imaginary = at // 128 % 2 == 1
    c, s = circle(256, np.arange(256), row)
    base_rows = np.concatenate([np.where(imaginary, s, c), np.where(imaginary, c, -s)]) / 64.0
    at = np.arange(256)
    col = 128 * (at // 8 % 2) + 64 * (at // 128) + 8 * (at // 16 % 8) + at % 8
    c, s = circle(256, col, np.arange(256))
    base_cols = np.block([[c, s], [-s, c]]) / 64.0
    turn_rows = np.stack(circle(FULL, np.arange(NR), np.arange(256)))[:, :, None, :]
    turn_cols = np.stack(circle(FULL, np.arange(NR), col))[:, :, None, :]
    return (
        jnp.asarray(base_rows, BF16),
        jnp.asarray(base_cols, BF16),
        jnp.asarray(turn_rows, F32),
        jnp.asarray(turn_cols, F32),
    )


def times_unit(value, numerator, count, sign):
    real, imag = value
    step = (numerator * 8) % (count * 8)
    eighth, rest = divmod(step, count)
    if rest == 0 and eighth % 2 == 0:
        quarter = (eighth // 2) % 4
        if quarter == 0:
            return real, imag
        if quarter == 2:
            return -real, -imag
        if (quarter == 1) == (sign > 0):
            return -imag, real
        return imag, -real
    angle = 2.0 * math.pi * numerator / count
    cosine, sine = math.cos(angle), sign * math.sin(angle)
    if rest == 0:
        half = abs(cosine)
        a = (real - imag) if cosine * sine > 0 else (real + imag)
        b = (real + imag) if cosine * sine > 0 else (imag - real)
        if cosine < 0:
            return a * (-half), b * (-half)
        return a * half, b * half
    return real * cosine - imag * sine, real * sine + imag * cosine


def butterfly(values, sign):
    count = len(values)
    if count == 1:
        return values
    even = butterfly(values[0::2], sign)
    odd = butterfly(values[1::2], sign)
    low, high = [], []
    for at in range(count // 2):
        er, ei = even[at]
        tr, ti = times_unit(odd[at], at, count, sign)
        low.append((er + tr, ei + ti))
        high.append((er - tr, ei - ti))
    return low + high


def cos_sin(angle):
    half = angle * 0.5
    square = half * half
    sine = -2.5052108e-08
    for factor in (2.7557319e-06, -1.9841270e-04, 8.3333333e-03, -1.6666667e-01, 1.0):
        sine = sine * square + factor
    sine = sine * half
    cosine = 2.0876757e-09
    for factor in (-2.7557319e-07, 2.4801587e-05, -1.3888889e-03, 4.1666667e-02, -0.5, 1.0):
        cosine = cosine * square + factor
    return 1.0 - 2.0 * (sine * sine), 2.0 * (sine * cosine)


def dot(a, b):
    return jnp.dot(a, b, preferred_element_type=F32)


def dot_nt(a, b):
    return lax.dot_general(a, b, (((1,), (1,)), ((), ())), preferred_element_type=F32)


def kernel(
    shifts, mask, spec_h, diff_h, phases_h, trans_h, base_rows_h, base_cols_h, turn_rows_h, turn_cols_h, out_h,
    spec, diff, phases, trans, wr, wc, turn_rows, turn_cols, out,
    low0, high0, dw, trig0, trig1, pick_cols, pick_rows, back_rows, tspace,
    work_b, work_z, work_y, work_r, work_d, work_s, work_x, work_o,
    sa1, rb1, sm1, rd1, sm2, rb2, sb2, ra3, low1, high1, sa3, rb3, sm3, rd3, fs, rf, ts, tr,
    in_sem, send_sem, recv_sem, halo_sem, ready_sem,
):
    rp = lax.axis_index("rows")
    cp = lax.axis_index("cols")

    z_lo, x, core = lax.div(rp, 8), lax.rem(lax.div(rp, 2), 4), lax.rem(rp, 2)
    z_hi, y = lax.div(cp, 4), lax.rem(cp, 4)

    def row_at(step):
        return lax.rem(rp + step, NR)

    def col_at(step):
        return lax.rem(cp + step, NC)

    row_peer = {
        o: lax.rem(z_lo + o[0], 2) * 8 + lax.rem(x + o[1], 4) * 2 + lax.rem(core + o[2], 2) for o in ROW_STEPS
    }
    col_peer = {o: lax.rem(z_hi + o[0], 2) * 4 + lax.rem(y + o[1], 4) for o in COL_STEPS}

    waits = []

    def finish():
        for wait in waits:
            wait()

    barrier = pltpu.get_barrier_semaphore()
    for step in (1, NR - 1):
        pl.semaphore_signal(barrier, inc=1, device_id={"rows": row_at(step)})
    for step in (1, NC - 1):
        pl.semaphore_signal(barrier, inc=1, device_id={"cols": col_at(step)})

    rounds = (("rows", 1), ("rows", 2), ("rows", 4), ("cols", 1), ("cols", 2), ("cols", 4))

    def tell(which):
        axis, reach = rounds[which]
        count, at = (NR, row_at) if axis == "rows" else (NC, col_at)
        for step in sorted({reach, count - reach}):
            pl.semaphore_signal(ready_sem.at[which], inc=1, device_id={axis: at(step)})

    def told(which):
        axis, reach = rounds[which]
        pl.semaphore_wait(ready_sem.at[which], 1 if 2 * reach == NC and axis == "cols" else 2)

    loads = {}
    for at, (name, src, dst) in enumerate((
        ("diff", diff_h, diff), ("phases", phases_h, phases), ("spec", spec_h, spec),
        ("wr", base_rows_h, wr), ("turn_rows", turn_rows_h, turn_rows), ("trans", trans_h, trans),
        ("wc", base_cols_h, wc), ("turn_cols", turn_cols_h, turn_cols),
    )):
        loads[name] = pltpu.make_async_copy(src, dst, in_sem.at[at])
        loads[name].start()

    def remote(src, dst, at, device):
        return pltpu.make_async_remote_copy(
            src_ref=src, dst_ref=dst, send_sem=send_sem.at[at], recv_sem=recv_sem.at[at], device_id=device
        )

    def rows_exchange(src, dst, at):
        for step in ROW_STEPS[:-1]:
            peer = row_peer[step]
            remote(src.at[peer], dst.at[rp], at, {"rows": peer}).start()
        pltpu.make_async_copy(src.at[rp], dst.at[rp], recv_sem.at[at]).start()
        waits.append(lambda: sent(src.at[pl.ds(0, NR - 1)], at))

    def cols_exchange(src, dst, at):
        for step in COL_STEPS[:-1]:
            peer = col_peer[step]
            remote(src.at[peer], dst.at[cp], at, {"cols": peer}).start()
        pltpu.make_async_copy(src.at[cp], dst.at[cp], recv_sem.at[at]).start()
        waits.append(lambda: sent(src.at[pl.ds(0, NC - 1)], at))

    def tiles_exchange(src, dst, at):
        for row_step, col_step in PAIR_STEPS[:-1]:
            d, g = row_peer[row_step], col_peer[col_step]
            remote(src.at[g, d], dst.at[cp, rp], at, {"rows": d, "cols": g}).start()
        pltpu.make_async_copy(src.at[cp, rp], dst.at[cp, rp], recv_sem.at[at]).start()
        waits.append(lambda: sent(src.at[pl.ds(0, NC - 1)], at))
        waits.append(lambda: sent(src.at[0, pl.ds(0, NR - 1)], at))

    def arrived(dst, at):
        pltpu.make_async_copy(dst, dst, recv_sem.at[at]).wait()

    def sent(src, at):
        pltpu.make_async_copy(src, src, send_sem.at[at]).wait()

    def halo_start(src, low, high, at):
        @pl.when(rp < NR - 1)
        def _():
            pltpu.make_async_remote_copy(
                src_ref=src, dst_ref=low, send_sem=halo_sem.at[at, 0], recv_sem=halo_sem.at[at, 1],
                device_id={"rows": rp + 1},
            ).start()

        @pl.when(rp > 0)
        def _():
            pltpu.make_async_remote_copy(
                src_ref=src, dst_ref=high, send_sem=halo_sem.at[at, 2], recv_sem=halo_sem.at[at, 3],
                device_id={"rows": rp - 1},
            ).start()

        waits.append(lambda: halo_sent(src, at))

    def halo_wait(low, high, at):
        @pl.when(rp < NR - 1)
        def _():
            pltpu.make_async_copy(high, high, halo_sem.at[at, 3]).wait()

        @pl.when(rp > 0)
        def _():
            pltpu.make_async_copy(low, low, halo_sem.at[at, 1]).wait()

    def halo_sent(src, at):
        @pl.when(rp < NR - 1)
        def _():
            pltpu.make_async_copy(src, src, halo_sem.at[at, 0]).wait()

        @pl.when(rp > 0)
        def _():
            pltpu.make_async_copy(src, src, halo_sem.at[at, 2]).wait()

    def iota(shape, axis):
        return lax.broadcasted_iota(jnp.int32, shape, axis)

    def one_hot(test):
        return jnp.where(test, 1.0, 0.0).astype(BF16)

    at_j, to_j = iota((128, 256), 0), iota((128, 256), 1)

    def banded(bounce):
        g = shifts[bounce]
        below = one_hot(to_j == at_j + 256 - g)
        above = one_hot(to_j == at_j + g - 128)
        for block in range(2):
            weights = [mask[block, m].astype(F32) for m in range(3)]
            for plane in range(2):
                left = (dot(diff[plane, block, 0], below) * weights[0]).astype(BF16)
                own = (diff[plane, block, 1].astype(F32) * weights[1]).astype(BF16)
                right = (dot(diff[plane, block, 2], above) * weights[2]).astype(BF16)
                nothing = jnp.zeros((128, 128), BF16)
                units = [left[:, :128], left[:, 128:], own, right[:, :128], right[:, 128:]]
                units = units + [nothing] if block == 0 else [nothing] + units
                for at, unit in enumerate(units):
                    which, col = at // 2, 128 * (at % 2)
                    row = 128 * block
                    if plane == 0:
                        dw[bounce, which, row:row + 128, col:col + 128] = unit
                        dw[bounce, which, 256 + row:384 + row, 256 + col:384 + col] = unit
                    else:
                        dw[bounce, which, 256 + row:384 + row, col:col + 128] = unit
                        dw[bounce, which, row:row + 128, 256 + col:384 + col] = -unit

    loads["diff"].wait()
    banded(0)

    @pl.when(rp == 0)
    def _():
        low0[...] = jnp.zeros_like(low0)
        low1[...] = jnp.zeros_like(low1)

    @pl.when(rp == NR - 1)
    def _():
        high0[...] = jnp.zeros_like(high0)
        high1[...] = jnp.zeros_like(high1)

    pl.semaphore_wait(barrier, 4)
    for h in range(CHUNKS):
        halo_start(spec_h.at[:, :, pl.ds(128 * h, 128)], low0.at[h], high0.at[h], h)
    tell(0)
    loads["phases"].wait()

    def phase0(at, _):
        rows = pl.ds(pl.multiple_of(at * 32, 32), 32)
        cosine, sine = cos_sin(phases[0, rows, :])
        trig0[0, rows, :] = cosine
        trig0[1, rows, :] = sine
        return 0

    lax.fori_loop(0, 3, phase0, 0)
    told(0)
    tell(1)
    lax.fori_loop(3, 6, phase0, 0)
    told(1)
    tell(2)
    lax.fori_loop(6, 8, phase0, 0)
    loads["spec"].wait()

    for h in range(CHUNKS):
        halo_wait(low0.at[h], high0.at[h], h)
        cols = slice(128 * h, 128 * h + 128)
        total = dot(dw[0, 1], spec[:, :, cols].reshape(512, 128))
        total = total + dot(dw[0, 0], low0[h].reshape(512, 128))
        total = total + dot(dw[0, 2], high0[h].reshape(512, 128))
        cosine, sine = trig0[0, :, cols], trig0[1, :, cols]
        real, imag = total[:256], total[256:]
        wave_re = (real * cosine - imag * sine).astype(BF16)
        wave_im = (real * sine + imag * cosine).astype(BF16)
        sa1[h, :, :, 0:256] = wave_re.T.reshape(NR, 8, 256)
        sa1[h, :, :, 256:512] = wave_im.T.reshape(NR, 8, 256)
        if h == 0:
            told(2)
            tell(3)
        rows_exchange(sa1.at[h], rb1.at[h], 1 + h)

    told(3)
    tell(4)

    lane = iota((512, 512), 1)
    pick_cols[...] = one_hot(iota((512, 512), 0) == (lane & 31) * 16 + (lane >> 5))
    a, b = iota((256, 256), 0), iota((256, 256), 1)
    pick_rows[...] = one_hot(b == (a & 15) * 16 + (a >> 4))
    back_rows[...] = one_hot(b == (a & 1) * 128 + ((a & 15) >> 1) * 16 + (a >> 4))

    told(4)
    tell(5)
    loads["trans"].wait()
    for half in range(2):
        cols = pl.ds(half * 256, 256)
        picked = dot(trans[...].astype(BF16), pick_cols[:, cols]).astype(BF16)
        ts[:, :, :, cols] = dot(pick_rows[...], picked).astype(BF16).reshape(NC, 2, 16, 256)
    told(5)
    cols_exchange(ts, tr, 0)

    for name in ("wr", "wc", "turn_rows", "turn_cols"):
        loads[name].wait()

    lane128 = iota((1, 128), 1)

    def swap(first, second, size):
        even = (lane128 & size) == 0
        return (
            jnp.where(even, first, pltpu.roll(second, size, 1)),
            jnp.where(even, pltpu.roll(first, 128 - size, 1), second),
        )

    def crossed(values):
        reach = len(values) // 2
        while reach:
            size = reach * (128 // len(values))
            result = list(values)
            for at in range(len(values)):
                if at & reach == 0:
                    result[at], result[at + reach] = swap(values[at], values[at + reach], size)
            values = result
            reach //= 2
        return values

    def forward_rows(src, h):
        def first(at, _):
            half = pl.multiple_of(at * 128, 128)
            re, im = pl.ds(half, 128), pl.ds(half + 256, 128)
            values = [(src[p, :, re].astype(F32), src[p, :, im].astype(F32)) for p in range(NR)]
            values = butterfly(values, 1)
            for r in range(NR):
                real, imag = values[r]
                cosine, sine = turn_rows[0, r, :, re], turn_rows[1, r, :, re]
                work_b[r, :, re] = real * cosine - imag * sine
                work_b[r, :, im] = real * sine + imag * cosine
            return 0

        lax.fori_loop(0, 2, first, 0)
        rows = work_b[...].astype(BF16).reshape(128, 512)
        for part in range(2):
            lanes = slice(256 * part, 256 * part + 256)
            got = dot(rows, wr[:, lanes])
            work_z[:, 8 * h:8 * h + 8, lanes] = got.reshape(NR, 8, 256)

    def to_cols(send, recv, at):
        for half in range(2):
            def turn(g, _):
                block = work_z[2 * g + half].astype(BF16)
                block = jnp.concatenate([block[:, 128 * u:128 * u + 128] for u in range(4)], axis=0)
                send[half, g] = block.T.reshape(NR, 8, 128)
                return 0

            lax.fori_loop(0, NC, turn, 0)
            tiles_exchange(send.at[half], recv.at[half], at + half)

    def forward_cols(src):
        def first(at, _):
            lanes = pl.ds(pl.multiple_of(at * 128, 128), 128)
            lanes2 = pl.ds(pl.multiple_of(at * 128 + 256, 128), 128)
            for p in range(NC):
                parts = crossed([src[p, at * 8 + low].astype(F32) for low in range(8)])
                for k in range(8):
                    work_x[k // 4, k // 2 % 2, 2 * p + k % 2] = parts[k]
            for u in range(2):
                values = butterfly([(work_x[u, 0, p], work_x[u, 1, p]) for p in range(NR)], 1)
                for r in range(NR):
                    real, imag = values[r]
                    cosine, sine = turn_cols[0, r, :, lanes], turn_cols[1, r, :, lanes]
                    rows = slice(8 * u, 8 * u + 8)
                    work_d[r, rows, lanes] = real * cosine - imag * sine
                    work_d[r, rows, lanes2] = real * sine + imag * cosine
            return 0

        lax.fori_loop(0, 2, first, 0)

    def phase1(at, _):
        cols = pl.ds(pl.multiple_of(at * 128, 128), 128)
        cosine, sine = cos_sin(phases[1, :, cols])
        trig1[0, cols, :] = cosine.T
        trig1[1, cols, :] = sine.T
        return 0

    for h in range(CHUNKS):
        arrived(rb1.at[h], 1 + h)
        forward_rows(rb1.at[h], h)
    to_cols(sm1, rd1, 5)

    lax.fori_loop(0, 4, phase1, 0)
    banded(1)

    arrived(tr, 0)
    for e in range(2):
        for q in range(4):
            src = slice(128 * q, 128 * q + 128)
            got = crossed([tr[4 * e + k, :, :, src].reshape(32, 128).astype(F32) for k in range(4)])
            for k in range(4):
                tspace[:, 4 * q + k, :, 128 * e:128 * e + 128] = got[k].reshape(2, 16, 128)

    for half in range(2):
        arrived(rd1.at[half], 5 + half)
        forward_cols(rd1.at[half])
        rows = work_d[...].astype(BF16).reshape(256, 512)
        for part in range(2):
            lanes = slice(256 * part, 256 * part + 256)
            space = dot(rows, wc[:, lanes])
            work_s[:, lanes] = (space * tspace[half].reshape(256, 256)).astype(BF16)
        for part in range(2):
            lanes = slice(256 * part, 256 * part + 256)
            work_d[:, :, lanes] = dot_nt(work_s[...], wc[lanes, :]).reshape(NR, 16, 256)

        def last_cols(at, _):
            re = pl.ds(pl.multiple_of(at * 128, 128), 128)
            im = pl.ds(pl.multiple_of(at * 128 + 256, 128), 128)
            for u in range(2):
                values = []
                for r in range(NR):
                    real, imag = work_d[r, 8 * u:8 * u + 8, re], work_d[r, 8 * u:8 * u + 8, im]
                    cosine, sine = turn_cols[0, r, :, re], turn_cols[1, r, :, re]
                    values.append((real * cosine + imag * sine, imag * cosine - real * sine))
                values = butterfly(values, -1)
                for r in range(NR):
                    work_x[u, 0, r], work_x[u, 1, r] = values[r]
            for q in range(NC):
                tiles = crossed([work_x[k // 4, k // 2 % 2, 2 * q + k % 2] for k in range(8)])
                for low in range(8):
                    sm2[half, q, at * 8 + low] = tiles[low].astype(BF16)
            return 0

        lax.fori_loop(0, 2, last_cols, 0)
        tiles_exchange(sm2.at[half], rb2.at[half], 7 + half)

    for half in range(2):
        arrived(rb2.at[half], 7 + half)

        def untile(g, _):
            block = rb2[half, g].reshape(128, 128).T
            for u in range(4):
                work_y[g, :, 128 * u:128 * u + 128] = block[32 * u:32 * u + 32]
            return 0

        lax.fori_loop(0, NC, untile, 0)
        for part in range(2):
            lanes = slice(256 * part, 256 * part + 256)
            got = dot_nt(work_y[...].reshape(256, 512), wr[lanes, :])
            work_r[half, :, :, lanes] = got.reshape(NC, 32, 256)
    for h in range(CHUNKS):
        crow = slice(8 * h, 8 * h + 8)

        def sources(at, _):
            half = pl.multiple_of(at * 128, 128)
            re, im = pl.ds(half, 128), pl.ds(half + 256, 128)
            values = []
            for r in range(NR):
                real, imag = work_r[r % 2, r // 2, crow, re], work_r[r % 2, r // 2, crow, im]
                cosine, sine = turn_rows[0, r, :, re], turn_rows[1, r, :, re]
                values.append((real * cosine + imag * sine, imag * cosine - real * sine))
            values = butterfly(values, -1)
            for r in range(NR):
                sb2[h, r, :, re] = values[r][0].astype(BF16)
                sb2[h, r, :, im] = values[r][1].astype(BF16)
            return 0

        lax.fori_loop(0, 2, sources, 0)
        rows_exchange(sb2.at[h], ra3.at[h], 9 + h)

    for h in range(CHUNKS):
        arrived(ra3.at[h], 9 + h)
        halo_start(ra3.at[h], low1.at[h], high1.at[h], CHUNKS + h)

    for h in range(CHUNKS):
        halo_wait(low1.at[h], high1.at[h], CHUNKS + h)
        total = dot_nt(ra3[h].reshape(128, 512), dw[1, 1])
        total = total + dot_nt(low1[h].reshape(128, 512), dw[1, 0])
        total = total + dot_nt(high1[h].reshape(128, 512), dw[1, 2])
        rows = slice(128 * h, 128 * h + 128)
        cosine, sine = trig1[0, rows, :], trig1[1, rows, :]
        real, imag = total[:, :256], total[:, 256:]
        sa3[h, :, :, 0:256] = (real * cosine - imag * sine).astype(BF16).reshape(NR, 8, 256)
        sa3[h, :, :, 256:512] = (real * sine + imag * cosine).astype(BF16).reshape(NR, 8, 256)
        rows_exchange(sa3.at[h], rb3.at[h], 13 + h)
    for h in range(CHUNKS):
        arrived(rb3.at[h], 13 + h)
        forward_rows(rb3.at[h], h)
    to_cols(sm3, rd3, 17)
    for half in range(2):
        arrived(rd3.at[half], 17 + half)
        forward_cols(rd3.at[half])
        rows = work_d[...].astype(BF16).reshape(256, 512)
        for plane in range(2):
            lanes = slice(256 * plane, 256 * plane + 256)
            work_d[:, :, lanes] = dot(rows, wc[:, lanes]).reshape(NR, 16, 256)
            for q in range(4):
                for e in range(2):
                    src = slice(256 * plane + 128 * e, 256 * plane + 128 * e + 128)
                    lanes_to = slice(512 * plane + 128 * q, 512 * plane + 128 * q + 128)
                    got = crossed([work_d[4 * q + k, :, src] for k in range(4)])
                    for k in range(4):
                        fs[half, 4 * e + k, :, lanes_to] = got[k].astype(BF16)
        cols_exchange(fs.at[half], rf.at[half], 19 + half)
    for half in range(2):
        arrived(rf.at[half], 19 + half)
        for plane in range(2):
            lanes = slice(512 * plane, 512 * plane + 512)
            ordered = dot_nt(rf[half, :, :, lanes].reshape(128, 512), pick_cols[...])
            work_o[plane, 128 * half:128 * half + 128, :] = ordered.astype(BF16)
    for plane in range(2):
        out[plane] = dot(back_rows[...], work_o[plane]).astype(BF16)
        result = pltpu.make_async_copy(out.at[plane], out_h.at[plane], in_sem.at[9 + plane])
        result.start()
        waits.append(result.wait)

    finish()


def on_device(spectrum, diffraction, order_mask, phases, transmission, shifts):
    anywhere = pl.BlockSpec(memory_space=pl.ANY)
    smem = pl.BlockSpec(memory_space=pltpu.SMEM)
    constants = tables()
    operands = (spectrum, diffraction, phases, transmission) + constants

    def vmem(kind, *shape):
        return pltpu.VMEM(shape, kind)

    halves = (CHUNKS, NR, 8, 512)
    space = pl.pallas_call(
        kernel,
        out_shape=jax.ShapeDtypeStruct((2, 256, 512), BF16),
        in_specs=[smem, smem] + [anywhere] * len(operands),
        out_specs=anywhere,
        scratch_shapes=[pltpu.VMEM(x.shape, x.dtype) for x in operands] + [
            vmem(BF16, 2, 256, 512),
            vmem(BF16, CHUNKS, 2, 256, 128), vmem(BF16, CHUNKS, 2, 256, 128),
            vmem(BF16, 2, 3, 512, 512),
            vmem(F32, 2, 256, 512),
            vmem(F32, 2, 512, 256),
            vmem(BF16, 512, 512), vmem(BF16, 256, 256), vmem(BF16, 256, 256),
            vmem(F32, 2, NR, 16, 256),
            vmem(F32, NR, 8, 512),
            vmem(F32, NR, 32, 512),
            vmem(BF16, NC, 32, 512),
            vmem(F32, 2, NC, 32, 512),
            vmem(F32, NR, 16, 512),
            vmem(BF16, 256, 512),
            vmem(F32, 2, 2, NR, 8, 128),
            vmem(BF16, 2, 256, 512),
            vmem(BF16, *halves), vmem(BF16, *halves),
            vmem(BF16, 2, NC, NR, 8, 128), vmem(BF16, 2, NC, NR, 8, 128),
            vmem(BF16, 2, NC, NR, 8, 128), vmem(BF16, 2, NC, NR, 8, 128),
            vmem(BF16, *halves), vmem(BF16, *halves),
            vmem(BF16, *halves), vmem(BF16, *halves),
            vmem(BF16, *halves), vmem(BF16, *halves),
            vmem(BF16, 2, NC, NR, 8, 128), vmem(BF16, 2, NC, NR, 8, 128),
            vmem(BF16, 2, NC, 16, 1024), vmem(BF16, 2, NC, 16, 1024),
            vmem(BF16, NC, 2, 16, 512), vmem(BF16, NC, 2, 16, 512),
            pltpu.SemaphoreType.DMA((11,)),
            pltpu.SemaphoreType.DMA((21,)),
            pltpu.SemaphoreType.DMA((21,)),
            pltpu.SemaphoreType.DMA((2 * CHUNKS, 4)),
            pltpu.SemaphoreType.REGULAR((6,)),
        ],
        compiler_params=pltpu.CompilerParams(
            collective_id=0, has_side_effects=True, vmem_limit_bytes=60 * 1024 * 1024
        ),
    )(shifts, order_mask, *operands)
    return space.astype(F32) * transmission[None]


def solution(mesh):
    placed = (
        P(None, "rows", "cols"),
        P(None, "rows", None, None, None),
        P("rows", None),
        P(None, "rows", "cols"),
        P("rows", "cols"),
        P(),
    )
    return jax.shard_map(
        on_device, mesh=mesh, in_specs=placed, out_specs=P(None, "rows", "cols"), check_vma=False
    )
```

```python
import math

import jax
import jax.numpy as jnp
import numpy as np
from jax import lax
from jax.experimental import pallas as pl
from jax.experimental.pallas import tpu as pltpu
from jax.sharding import PartitionSpec as P

F32 = jnp.float32
BF16 = jnp.bfloat16
NR = 16
NC = 8
FULL = 4096
CHUNKS = 4


def ring(step):
    return min(step, 4 - step)


def depth(high, low):
    return (0, 1, 2, 1)[2 * high + low]


ROW_STEPS = sorted(
    ((z, x, c) for z in range(2) for x in range(4) for c in range(2)),
    key=lambda o: -(8 * (o[0] + ring(o[1])) + o[2]),
)
COL_STEPS = sorted(
    ((z, y) for z in range(2) for y in range(4)), key=lambda o: -(2 * o[0] + ring(o[1]))
)
PAIR_STEPS = sorted(
    ((r, c) for r in ROW_STEPS for c in COL_STEPS),
    key=lambda p: -(8 * (depth(p[1][0], p[0][0]) + ring(p[0][1]) + ring(p[1][1])) + p[0][2]),
)


def tables():
    def circle(count, left, right):
        angle = 2.0 * np.pi * ((left[:, None] * right[None, :]) % count) / count
        return np.cos(angle), np.sin(angle)

    at = np.arange(512)
    row = 16 * (at // 8 % 16) + 8 * (at // 256) + at % 8
    imaginary = at // 128 % 2 == 1
    c, s = circle(256, np.arange(256), row)
    base_rows = np.concatenate([np.where(imaginary, s, c), np.where(imaginary, c, -s)]) / 64.0
    at = np.arange(256)
    col = 128 * (at // 8 % 2) + 64 * (at // 128) + 8 * (at // 16 % 8) + at % 8
    c, s = circle(256, col, np.arange(256))
    base_cols = np.block([[c, s], [-s, c]]) / 64.0
    turn_rows = np.stack(circle(FULL, np.arange(NR), np.arange(256)))[:, :, None, :]
    turn_cols = np.stack(circle(FULL, np.arange(NR), col))[:, :, None, :]
    return (
        jnp.asarray(base_rows, BF16),
        jnp.asarray(base_cols, BF16),
        jnp.asarray(turn_rows, F32),
        jnp.asarray(turn_cols, F32),
    )


def times_unit(value, numerator, count, sign):
    real, imag = value
    step = (numerator * 8) % (count * 8)
    eighth, rest = divmod(step, count)
    if rest == 0 and eighth % 2 == 0:
        quarter = (eighth // 2) % 4
        if quarter == 0:
            return real, imag
        if quarter == 2:
            return -real, -imag
        if (quarter == 1) == (sign > 0):
            return -imag, real
        return imag, -real
    angle = 2.0 * math.pi * numerator / count
    cosine, sine = math.cos(angle), sign * math.sin(angle)
    if rest == 0:
        half = abs(cosine)
        a = (real - imag) if cosine * sine > 0 else (real + imag)
        b = (real + imag) if cosine * sine > 0 else (imag - real)
        if cosine < 0:
            return a * (-half), b * (-half)
        return a * half, b * half
    return real * cosine - imag * sine, real * sine + imag * cosine


def butterfly(values, sign):
    count = len(values)
    if count == 1:
        return values
    even = butterfly(values[0::2], sign)
    odd = butterfly(values[1::2], sign)
    low, high = [], []
    for at in range(count // 2):
        er, ei = even[at]
        tr, ti = times_unit(odd[at], at, count, sign)
        low.append((er + tr, ei + ti))
        high.append((er - tr, ei - ti))
    return low + high


def cos_sin(angle):
    half = angle * 0.5
    square = half * half
    sine = -2.5052108e-08
    for factor in (2.7557319e-06, -1.9841270e-04, 8.3333333e-03, -1.6666667e-01, 1.0):
        sine = sine * square + factor
    sine = sine * half
    cosine = 2.0876757e-09
    for factor in (-2.7557319e-07, 2.4801587e-05, -1.3888889e-03, 4.1666667e-02, -0.5, 1.0):
        cosine = cosine * square + factor
    return 1.0 - 2.0 * (sine * sine), 2.0 * (sine * cosine)


def dot(a, b):
    return jnp.dot(a, b, preferred_element_type=F32)


def dot_nt(a, b):
    return lax.dot_general(a, b, (((1,), (1,)), ((), ())), preferred_element_type=F32)


def kernel(
    shifts, mask, spec_h, diff_h, phases_h, trans_h, base_rows_h, base_cols_h, turn_rows_h, turn_cols_h, out_h,
    spec, diff, phases, trans, wr, wc, turn_rows, turn_cols, out,
    low0, high0, dw, trig0, trig1, pick_cols, pick_rows, back_rows, tspace,
    work_b, work_z, work_y, work_r, work_d, work_s, work_x, work_o, own0, own1,
    sa1, rb1, sm1, rd1, sm2, rb2, sb2, ra3, low1, high1, sa3, rb3, sm3, rd3, fs, rf, ts, tr,
    in_sem, send_sem, recv_sem, halo_sem, ready_sem,
):
    rp = lax.axis_index("rows")
    cp = lax.axis_index("cols")

    z_lo, x, core = lax.div(rp, 8), lax.rem(lax.div(rp, 2), 4), lax.rem(rp, 2)
    z_hi, y = lax.div(cp, 4), lax.rem(cp, 4)

    def row_at(step):
        return lax.rem(rp + step, NR)

    def col_at(step):
        return lax.rem(cp + step, NC)

    row_peer = {
        o: lax.rem(z_lo + o[0], 2) * 8 + lax.rem(x + o[1], 4) * 2 + lax.rem(core + o[2], 2) for o in ROW_STEPS
    }
    col_peer = {o: lax.rem(z_hi + o[0], 2) * 4 + lax.rem(y + o[1], 4) for o in COL_STEPS}

    waits = []

    def finish():
        for wait in waits:
            wait()

    barrier = pltpu.get_barrier_semaphore()
    for step in (1, NR - 1):
        pl.semaphore_signal(barrier, inc=1, device_id={"rows": row_at(step)})
    for step in (1, NC - 1):
        pl.semaphore_signal(barrier, inc=1, device_id={"cols": col_at(step)})

    rounds = (("rows", 1), ("rows", 2), ("rows", 4), ("cols", 1), ("cols", 2), ("cols", 4))

    def tell(which):
        axis, reach = rounds[which]
        count, at = (NR, row_at) if axis == "rows" else (NC, col_at)
        for step in sorted({reach, count - reach}):
            pl.semaphore_signal(ready_sem.at[which], inc=1, device_id={axis: at(step)})

    def told(which):
        axis, reach = rounds[which]
        pl.semaphore_wait(ready_sem.at[which], 1 if 2 * reach == NC and axis == "cols" else 2)

    loads = {}
    for at, (name, src, dst) in enumerate((
        ("diff", diff_h, diff), ("phases", phases_h, phases), ("spec", spec_h, spec),
        ("wr", base_rows_h, wr), ("turn_rows", turn_rows_h, turn_rows), ("trans", trans_h, trans),
        ("wc", base_cols_h, wc), ("turn_cols", turn_cols_h, turn_cols),
    )):
        loads[name] = pltpu.make_async_copy(src, dst, in_sem.at[at])
        loads[name].start()

    def remote(src, dst, at, device):
        return pltpu.make_async_remote_copy(
            src_ref=src, dst_ref=dst, send_sem=send_sem.at[at], recv_sem=recv_sem.at[at], device_id=device
        )

    def rows_exchange(src, dst, at):
        for step in ROW_STEPS[:-1]:
            peer = row_peer[step]
            remote(src.at[peer], dst.at[rp], at, {"rows": peer}).start()
        pltpu.make_async_copy(src.at[rp], dst.at[rp], recv_sem.at[at]).start()
        waits.append(lambda: sent(src.at[pl.ds(0, NR - 1)], at))

    def cols_exchange(src, dst, at):
        for step in COL_STEPS[:-1]:
            peer = col_peer[step]
            remote(src.at[peer], dst.at[cp], at, {"cols": peer}).start()
        pltpu.make_async_copy(src.at[cp], dst.at[cp], recv_sem.at[at]).start()
        waits.append(lambda: sent(src.at[pl.ds(0, NC - 1)], at))

    def tiles_exchange(src, dst, at):
        for row_step, col_step in PAIR_STEPS[:-1]:
            d, g = row_peer[row_step], col_peer[col_step]
            remote(src.at[g, d], dst.at[cp, rp], at, {"rows": d, "cols": g}).start()
        tiles_kept(src, dst, at)

    def tiles_kept(src, dst, at):
        pltpu.make_async_copy(src.at[cp, rp], dst.at[cp, rp], recv_sem.at[at]).start()
        waits.append(lambda: sent(src.at[pl.ds(0, NC - 1)], at))
        waits.append(lambda: sent(src.at[0, pl.ds(0, NR - 1)], at))

    def arrived(dst, at):
        pltpu.make_async_copy(dst, dst, recv_sem.at[at]).wait()

    def sent(src, at):
        pltpu.make_async_copy(src, src, send_sem.at[at]).wait()

    def halo_start(src, low, high, at):
        @pl.when(rp < NR - 1)
        def _():
            pltpu.make_async_remote_copy(
                src_ref=src, dst_ref=low, send_sem=halo_sem.at[at, 0], recv_sem=halo_sem.at[at, 1],
                device_id={"rows": rp + 1},
            ).start()

        @pl.when(rp > 0)
        def _():
            pltpu.make_async_remote_copy(
                src_ref=src, dst_ref=high, send_sem=halo_sem.at[at, 2], recv_sem=halo_sem.at[at, 3],
                device_id={"rows": rp - 1},
            ).start()

        waits.append(lambda: halo_sent(src, at))

    def halo_wait(low, high, at):
        @pl.when(rp < NR - 1)
        def _():
            pltpu.make_async_copy(high, high, halo_sem.at[at, 3]).wait()

        @pl.when(rp > 0)
        def _():
            pltpu.make_async_copy(low, low, halo_sem.at[at, 1]).wait()

    def halo_sent(src, at):
        @pl.when(rp < NR - 1)
        def _():
            pltpu.make_async_copy(src, src, halo_sem.at[at, 0]).wait()

        @pl.when(rp > 0)
        def _():
            pltpu.make_async_copy(src, src, halo_sem.at[at, 2]).wait()

    def iota(shape, axis):
        return lax.broadcasted_iota(jnp.int32, shape, axis)

    def one_hot(test):
        return jnp.where(test, 1.0, 0.0).astype(BF16)

    at_j, to_j = iota((128, 256), 0), iota((128, 256), 1)

    def banded(bounce):
        g = shifts[bounce]
        below = one_hot(to_j == at_j + 256 - g)
        above = one_hot(to_j == at_j + g - 128)
        for block in range(2):
            weights = [mask[block, m].astype(F32) for m in range(3)]
            for plane in range(2):
                left = (dot(diff[plane, block, 0], below) * weights[0]).astype(BF16)
                own = (diff[plane, block, 1].astype(F32) * weights[1]).astype(BF16)
                right = (dot(diff[plane, block, 2], above) * weights[2]).astype(BF16)
                nothing = jnp.zeros((128, 128), BF16)
                units = [left[:, :128], left[:, 128:], own, right[:, :128], right[:, 128:]]
                units = units + [nothing] if block == 0 else [nothing] + units
                for at, unit in enumerate(units):
                    which, col = at // 2, 128 * (at % 2)
                    row = 128 * block
                    if plane == 0:
                        dw[bounce, which, row:row + 128, col:col + 128] = unit
                        dw[bounce, which, 256 + row:384 + row, 256 + col:384 + col] = unit
                    else:
                        dw[bounce, which, 256 + row:384 + row, col:col + 128] = unit
                        dw[bounce, which, row:row + 128, 256 + col:384 + col] = -unit

    loads["diff"].wait()
    banded(0)

    @pl.when(rp == 0)
    def _():
        low0[...] = jnp.zeros_like(low0)
        low1[...] = jnp.zeros_like(low1)

    @pl.when(rp == NR - 1)
    def _():
        high0[...] = jnp.zeros_like(high0)
        high1[...] = jnp.zeros_like(high1)

    pl.semaphore_wait(barrier, 4)
    for h in range(CHUNKS):
        halo_start(spec_h.at[:, :, pl.ds(128 * h, 128)], low0.at[h], high0.at[h], h)
    tell(0)
    loads["phases"].wait()

    def phase0(at, _):
        rows = pl.ds(pl.multiple_of(at * 32, 32), 32)
        cosine, sine = cos_sin(phases[0, rows, :])
        trig0[0, rows, :] = cosine
        trig0[1, rows, :] = sine
        return 0

    lax.fori_loop(0, 3, phase0, 0)
    told(0)
    tell(1)
    lax.fori_loop(3, 6, phase0, 0)
    told(1)
    tell(2)
    lax.fori_loop(6, 8, phase0, 0)
    loads["spec"].wait()

    for h in range(CHUNKS):
        own0[h] = dot(dw[0, 1], spec[:, :, 128 * h:128 * h + 128].reshape(512, 128))
    for h in range(CHUNKS):
        halo_wait(low0.at[h], high0.at[h], h)
        cols = slice(128 * h, 128 * h + 128)
        total = own0[h] + dot(dw[0, 0], low0[h].reshape(512, 128))
        total = total + dot(dw[0, 2], high0[h].reshape(512, 128))
        cosine, sine = trig0[0, :, cols], trig0[1, :, cols]
        real, imag = total[:256], total[256:]
        wave_re = (real * cosine - imag * sine).astype(BF16)
        wave_im = (real * sine + imag * cosine).astype(BF16)
        sa1[h, :, :, 0:256] = wave_re.T.reshape(NR, 8, 256)
        sa1[h, :, :, 256:512] = wave_im.T.reshape(NR, 8, 256)
        if h == 0:
            told(2)
            tell(3)
        rows_exchange(sa1.at[h], rb1.at[h], 1 + h)

    told(3)
    tell(4)

    lane = iota((512, 512), 1)
    pick_cols[...] = one_hot(iota((512, 512), 0) == (lane & 31) * 16 + (lane >> 5))
    a, b = iota((256, 256), 0), iota((256, 256), 1)
    pick_rows[...] = one_hot(b == (a & 15) * 16 + (a >> 4))
    back_rows[...] = one_hot(b == (a & 1) * 128 + ((a & 15) >> 1) * 16 + (a >> 4))

    told(4)
    tell(5)
    loads["trans"].wait()
    for half in range(2):
        cols = pl.ds(half * 256, 256)
        picked = dot(trans[...].astype(BF16), pick_cols[:, cols]).astype(BF16)
        ts[:, :, :, cols] = dot(pick_rows[...], picked).astype(BF16).reshape(NC, 2, 16, 256)
    told(5)
    cols_exchange(ts, tr, 0)

    for name in ("wr", "wc", "turn_rows", "turn_cols"):
        loads[name].wait()

    lane128 = iota((1, 128), 1)

    def swap(first, second, size):
        even = (lane128 & size) == 0
        return (
            jnp.where(even, first, pltpu.roll(second, size, 1)),
            jnp.where(even, pltpu.roll(first, 128 - size, 1), second),
        )

    def crossed(values):
        reach = len(values) // 2
        while reach:
            size = reach * (128 // len(values))
            result = list(values)
            for at in range(len(values)):
                if at & reach == 0:
                    result[at], result[at + reach] = swap(values[at], values[at + reach], size)
            values = result
            reach //= 2
        return values

    def forward_rows(src, h):
        def first(at, _):
            half = pl.multiple_of(at * 128, 128)
            re, im = pl.ds(half, 128), pl.ds(half + 256, 128)
            values = [(src[p, :, re].astype(F32), src[p, :, im].astype(F32)) for p in range(NR)]
            values = butterfly(values, 1)
            for r in range(NR):
                real, imag = values[r]
                cosine, sine = turn_rows[0, r, :, re], turn_rows[1, r, :, re]
                work_b[r, :, re] = real * cosine - imag * sine
                work_b[r, :, im] = real * sine + imag * cosine
            return 0

        lax.fori_loop(0, 2, first, 0)
        rows = work_b[...].astype(BF16).reshape(128, 512)
        for part in range(2):
            lanes = slice(256 * part, 256 * part + 256)
            got = dot(rows, wr[:, lanes])
            work_z[:, 8 * h:8 * h + 8, lanes] = got.reshape(NR, 8, 256)

    def to_cols(send, recv, at):
        for half in range(2):
            def turn(g):
                block = work_z[2 * g + half].astype(BF16)
                block = jnp.concatenate([block[:, 128 * u:128 * u + 128] for u in range(4)], axis=0)
                send[half, g] = block.T.reshape(NR, 8, 128)

            turn(col_peer[COL_STEPS[0]])
            for number, col_step in enumerate(COL_STEPS):
                if number < NC - 1:
                    turn(col_peer[COL_STEPS[number + 1]])
                g = col_peer[col_step]
                for row_step in ROW_STEPS:
                    d = row_peer[row_step]
                    if any(row_step) or any(col_step):
                        device = {"rows": d, "cols": g}
                        remote(send.at[half, g, d], recv.at[half, cp, rp], at + half, device).start()
            tiles_kept(send.at[half], recv.at[half], at + half)

    def forward_cols(src):
        def first(at, _):
            lanes = pl.ds(pl.multiple_of(at * 128, 128), 128)
            lanes2 = pl.ds(pl.multiple_of(at * 128 + 256, 128), 128)
            for p in range(NC):
                parts = crossed([src[p, at * 8 + low].astype(F32) for low in range(8)])
                for k in range(8):
                    work_x[k // 4, k // 2 % 2, 2 * p + k % 2] = parts[k]
            for u in range(2):
                values = butterfly([(work_x[u, 0, p], work_x[u, 1, p]) for p in range(NR)], 1)
                for r in range(NR):
                    real, imag = values[r]
                    cosine, sine = turn_cols[0, r, :, lanes], turn_cols[1, r, :, lanes]
                    rows = slice(8 * u, 8 * u + 8)
                    work_d[r, rows, lanes] = real * cosine - imag * sine
                    work_d[r, rows, lanes2] = real * sine + imag * cosine
            return 0

        lax.fori_loop(0, 2, first, 0)

    def phase1(at, _):
        cols = pl.ds(pl.multiple_of(at * 128, 128), 128)
        cosine, sine = cos_sin(phases[1, :, cols])
        trig1[0, cols, :] = cosine.T
        trig1[1, cols, :] = sine.T
        return 0

    for h in range(CHUNKS):
        arrived(rb1.at[h], 1 + h)
        forward_rows(rb1.at[h], h)
    to_cols(sm1, rd1, 5)

    lax.fori_loop(0, 4, phase1, 0)
    banded(1)

    arrived(tr, 0)
    for e in range(2):
        for q in range(4):
            src = slice(128 * q, 128 * q + 128)
            got = crossed([tr[4 * e + k, :, :, src].reshape(32, 128).astype(F32) for k in range(4)])
            for k in range(4):
                tspace[:, 4 * q + k, :, 128 * e:128 * e + 128] = got[k].reshape(2, 16, 128)

    for half in range(2):
        arrived(rd1.at[half], 5 + half)
        forward_cols(rd1.at[half])
        rows = work_d[...].astype(BF16).reshape(256, 512)
        for part in range(2):
            lanes = slice(256 * part, 256 * part + 256)
            space = dot(rows, wc[:, lanes])
            work_s[:, lanes] = (space * tspace[half].reshape(256, 256)).astype(BF16)
        for part in range(2):
            lanes = slice(256 * part, 256 * part + 256)
            work_d[:, :, lanes] = dot_nt(work_s[...], wc[lanes, :]).reshape(NR, 16, 256)

        def last_cols(at, _):
            re = pl.ds(pl.multiple_of(at * 128, 128), 128)
            im = pl.ds(pl.multiple_of(at * 128 + 256, 128), 128)
            for u in range(2):
                values = []
                for r in range(NR):
                    real, imag = work_d[r, 8 * u:8 * u + 8, re], work_d[r, 8 * u:8 * u + 8, im]
                    cosine, sine = turn_cols[0, r, :, re], turn_cols[1, r, :, re]
                    values.append((real * cosine + imag * sine, imag * cosine - real * sine))
                values = butterfly(values, -1)
                for r in range(NR):
                    work_x[u, 0, r], work_x[u, 1, r] = values[r]
            for q in range(NC):
                tiles = crossed([work_x[k // 4, k // 2 % 2, 2 * q + k % 2] for k in range(8)])
                for low in range(8):
                    sm2[half, q, at * 8 + low] = tiles[low].astype(BF16)
            return 0

        lax.fori_loop(0, 2, last_cols, 0)
        tiles_exchange(sm2.at[half], rb2.at[half], 7 + half)

    for half in range(2):
        arrived(rb2.at[half], 7 + half)

        def untile(g, _):
            block = rb2[half, g].reshape(128, 128).T
            for u in range(4):
                work_y[g, :, 128 * u:128 * u + 128] = block[32 * u:32 * u + 32]
            return 0

        lax.fori_loop(0, NC, untile, 0)
        for part in range(2):
            lanes = slice(256 * part, 256 * part + 256)
            got = dot_nt(work_y[...].reshape(256, 512), wr[lanes, :])
            work_r[half, :, :, lanes] = got.reshape(NC, 32, 256)
    for h in range(CHUNKS):
        crow = slice(8 * h, 8 * h + 8)

        def sources(at, _):
            half = pl.multiple_of(at * 128, 128)
            re, im = pl.ds(half, 128), pl.ds(half + 256, 128)
            values = []
            for r in range(NR):
                real, imag = work_r[r % 2, r // 2, crow, re], work_r[r % 2, r // 2, crow, im]
                cosine, sine = turn_rows[0, r, :, re], turn_rows[1, r, :, re]
                values.append((real * cosine + imag * sine, imag * cosine - real * sine))
            values = butterfly(values, -1)
            for r in range(NR):
                sb2[h, r, :, re] = values[r][0].astype(BF16)
                sb2[h, r, :, im] = values[r][1].astype(BF16)
            return 0

        lax.fori_loop(0, 2, sources, 0)
        rows_exchange(sb2.at[h], ra3.at[h], 9 + h)

    for h in range(CHUNKS):
        arrived(ra3.at[h], 9 + h)
        halo_start(ra3.at[h], low1.at[h], high1.at[h], CHUNKS + h)
        own1[h] = dot_nt(ra3[h].reshape(128, 512), dw[1, 1])

    for h in range(CHUNKS):
        halo_wait(low1.at[h], high1.at[h], CHUNKS + h)
        total = own1[h] + dot_nt(low1[h].reshape(128, 512), dw[1, 0])
        total = total + dot_nt(high1[h].reshape(128, 512), dw[1, 2])
        rows = slice(128 * h, 128 * h + 128)
        cosine, sine = trig1[0, rows, :], trig1[1, rows, :]
        real, imag = total[:, :256], total[:, 256:]
        sa3[h, :, :, 0:256] = (real * cosine - imag * sine).astype(BF16).reshape(NR, 8, 256)
        sa3[h, :, :, 256:512] = (real * sine + imag * cosine).astype(BF16).reshape(NR, 8, 256)
        rows_exchange(sa3.at[h], rb3.at[h], 13 + h)
    for h in range(CHUNKS):
        arrived(rb3.at[h], 13 + h)
        forward_rows(rb3.at[h], h)
    to_cols(sm3, rd3, 17)
    for half in range(2):
        arrived(rd3.at[half], 17 + half)
        forward_cols(rd3.at[half])
        rows = work_d[...].astype(BF16).reshape(256, 512)
        for plane in range(2):
            lanes = slice(256 * plane, 256 * plane + 256)
            work_d[:, :, lanes] = dot(rows, wc[:, lanes]).reshape(NR, 16, 256)
            for q in range(4):
                for e in range(2):
                    src = slice(256 * plane + 128 * e, 256 * plane + 128 * e + 128)
                    lanes_to = slice(512 * plane + 128 * q, 512 * plane + 128 * q + 128)
                    got = crossed([work_d[4 * q + k, :, src] for k in range(4)])
                    for k in range(4):
                        fs[half, 4 * e + k, :, lanes_to] = got[k].astype(BF16)
        cols_exchange(fs.at[half], rf.at[half], 19 + half)
    for half in range(2):
        arrived(rf.at[half], 19 + half)
        for plane in range(2):
            lanes = slice(512 * plane, 512 * plane + 512)
            ordered = dot_nt(rf[half, :, :, lanes].reshape(128, 512), pick_cols[...])
            work_o[plane, 128 * half:128 * half + 128, :] = ordered.astype(BF16)
    for plane in range(2):
        out[plane] = dot(back_rows[...], work_o[plane]).astype(BF16)
        result = pltpu.make_async_copy(out.at[plane], out_h.at[plane], in_sem.at[9 + plane])
        result.start()
        waits.append(result.wait)

    finish()


def on_device(spectrum, diffraction, order_mask, phases, transmission, shifts):
    anywhere = pl.BlockSpec(memory_space=pl.ANY)
    smem = pl.BlockSpec(memory_space=pltpu.SMEM)
    constants = tables()
    operands = (spectrum, diffraction, phases, transmission) + constants

    def vmem(kind, *shape):
        return pltpu.VMEM(shape, kind)

    halves = (CHUNKS, NR, 8, 512)
    space = pl.pallas_call(
        kernel,
        out_shape=jax.ShapeDtypeStruct((2, 256, 512), BF16),
        in_specs=[smem, smem] + [anywhere] * len(operands),
        out_specs=anywhere,
        scratch_shapes=[pltpu.VMEM(x.shape, x.dtype) for x in operands] + [
            vmem(BF16, 2, 256, 512),
            vmem(BF16, CHUNKS, 2, 256, 128), vmem(BF16, CHUNKS, 2, 256, 128),
            vmem(BF16, 2, 3, 512, 512),
            vmem(F32, 2, 256, 512),
            vmem(F32, 2, 512, 256),
            vmem(BF16, 512, 512), vmem(BF16, 256, 256), vmem(BF16, 256, 256),
            vmem(F32, 2, NR, 16, 256),
            vmem(F32, NR, 8, 512),
            vmem(F32, NR, 32, 512),
            vmem(BF16, NC, 32, 512),
            vmem(F32, 2, NC, 32, 512),
            vmem(F32, NR, 16, 512),
            vmem(BF16, 256, 512),
            vmem(F32, 2, 2, NR, 8, 128),
            vmem(BF16, 2, 256, 512),
            vmem(F32, CHUNKS, 512, 128), vmem(F32, CHUNKS, 128, 512),
            vmem(BF16, *halves), vmem(BF16, *halves),
            vmem(BF16, 2, NC, NR, 8, 128), vmem(BF16, 2, NC, NR, 8, 128),
            vmem(BF16, 2, NC, NR, 8, 128), vmem(BF16, 2, NC, NR, 8, 128),
            vmem(BF16, *halves), vmem(BF16, *halves),
            vmem(BF16, *halves), vmem(BF16, *halves),
            vmem(BF16, *halves), vmem(BF16, *halves),
            vmem(BF16, 2, NC, NR, 8, 128), vmem(BF16, 2, NC, NR, 8, 128),
            vmem(BF16, 2, NC, 16, 1024), vmem(BF16, 2, NC, 16, 1024),
            vmem(BF16, NC, 2, 16, 512), vmem(BF16, NC, 2, 16, 512),
            pltpu.SemaphoreType.DMA((11,)),
            pltpu.SemaphoreType.DMA((21,)),
            pltpu.SemaphoreType.DMA((21,)),
            pltpu.SemaphoreType.DMA((2 * CHUNKS, 4)),
            pltpu.SemaphoreType.REGULAR((6,)),
        ],
        compiler_params=pltpu.CompilerParams(
            collective_id=0, has_side_effects=True, vmem_limit_bytes=60 * 1024 * 1024
        ),
    )(shifts, order_mask, *operands)
    return space.astype(F32) * transmission[None]


def solution(mesh):
    placed = (
        P(None, "rows", "cols"),
        P(None, "rows", None, None, None),
        P("rows", None),
        P(None, "rows", "cols"),
        P("rows", "cols"),
        P(),
    )
    return jax.shard_map(
        on_device, mesh=mesh, in_specs=placed, out_specs=P(None, "rows", "cols"), check_vma=False
    )
```

```python
import math

import jax
import jax.numpy as jnp
import numpy as np
from jax import lax
from jax.experimental import pallas as pl
from jax.experimental.pallas import tpu as pltpu
from jax.sharding import PartitionSpec as P

F32 = jnp.float32
BF16 = jnp.bfloat16
NR = 16
NC = 8
FULL = 4096
CHUNKS = 4


def ring(step):
    return min(step, 4 - step)


def depth(high, low):
    return (0, 1, 2, 1)[2 * high + low]


ROW_STEPS = sorted(
    ((z, x, c) for z in range(2) for x in range(4) for c in range(2)),
    key=lambda o: -(8 * (o[0] + ring(o[1])) + o[2]),
)
COL_STEPS = sorted(
    ((z, y) for z in range(2) for y in range(4)), key=lambda o: -(2 * o[0] + ring(o[1]))
)
PAIR_STEPS = sorted(
    ((r, c) for r in ROW_STEPS for c in COL_STEPS),
    key=lambda p: -(8 * (depth(p[1][0], p[0][0]) + ring(p[0][1]) + ring(p[1][1])) + p[0][2]),
)


def tables():
    def circle(count, left, right):
        angle = 2.0 * np.pi * ((left[:, None] * right[None, :]) % count) / count
        return np.cos(angle), np.sin(angle)

    at = np.arange(512)
    row = 16 * (at // 8 % 16) + 8 * (at // 256) + at % 8
    imaginary = at // 128 % 2 == 1
    c, s = circle(256, np.arange(256), row)
    base_rows = np.concatenate([np.where(imaginary, s, c), np.where(imaginary, c, -s)]) / 64.0
    at = np.arange(256)
    col = 128 * (at // 8 % 2) + 64 * (at // 128) + 8 * (at // 16 % 8) + at % 8
    c, s = circle(256, col, np.arange(256))
    base_cols = np.block([[c, s], [-s, c]]) / 64.0
    turn_rows = np.stack(circle(FULL, np.arange(NR), np.arange(256)))[:, :, None, :]
    turn_cols = np.stack(circle(FULL, np.arange(NR), col))[:, :, None, :]
    return (
        jnp.asarray(base_rows, BF16),
        jnp.asarray(base_cols, BF16),
        jnp.asarray(turn_rows, F32),
        jnp.asarray(turn_cols, F32),
    )


def times_unit(value, numerator, count, sign):
    real, imag = value
    step = (numerator * 8) % (count * 8)
    eighth, rest = divmod(step, count)
    if rest == 0 and eighth % 2 == 0:
        quarter = (eighth // 2) % 4
        if quarter == 0:
            return real, imag
        if quarter == 2:
            return -real, -imag
        if (quarter == 1) == (sign > 0):
            return -imag, real
        return imag, -real
    angle = 2.0 * math.pi * numerator / count
    cosine, sine = math.cos(angle), sign * math.sin(angle)
    if rest == 0:
        half = abs(cosine)
        a = (real - imag) if cosine * sine > 0 else (real + imag)
        b = (real + imag) if cosine * sine > 0 else (imag - real)
        if cosine < 0:
            return a * (-half), b * (-half)
        return a * half, b * half
    return real * cosine - imag * sine, real * sine + imag * cosine


def butterfly(values, sign):
    count = len(values)
    if count == 1:
        return values
    even = butterfly(values[0::2], sign)
    odd = butterfly(values[1::2], sign)
    low, high = [], []
    for at in range(count // 2):
        er, ei = even[at]
        tr, ti = times_unit(odd[at], at, count, sign)
        low.append((er + tr, ei + ti))
        high.append((er - tr, ei - ti))
    return low + high


def cos_sin(angle):
    half = angle * 0.5
    square = half * half
    sine = -2.5052108e-08
    for factor in (2.7557319e-06, -1.9841270e-04, 8.3333333e-03, -1.6666667e-01, 1.0):
        sine = sine * square + factor
    sine = sine * half
    cosine = 2.0876757e-09
    for factor in (-2.7557319e-07, 2.4801587e-05, -1.3888889e-03, 4.1666667e-02, -0.5, 1.0):
        cosine = cosine * square + factor
    return 1.0 - 2.0 * (sine * sine), 2.0 * (sine * cosine)


def dot(a, b):
    return jnp.dot(a, b, preferred_element_type=F32)


def dot_nt(a, b):
    return lax.dot_general(a, b, (((1,), (1,)), ((), ())), preferred_element_type=F32)


def kernel(
    shifts, mask, spec_h, diff_h, phases_h, trans_h, base_rows_h, base_cols_h, turn_rows_h, turn_cols_h, out_h,
    spec, diff, phases, trans, wr, wc, turn_rows, turn_cols, out,
    low0, high0, dw, trig0, trig1, pick_cols, pick_rows, back_rows, tspace,
    work_b, work_z, work_y, work_r, work_d, work_s, work_x, work_o, own0, own1,
    sa1, rb1, sm1, rd1, sm2, rb2, sb2, ra3, low1, high1, sa3, rb3, sm3, rd3, fs, rf, ts, tr,
    in_sem, send_sem, recv_sem, halo_sem, ready_sem,
):
    rp = lax.axis_index("rows")
    cp = lax.axis_index("cols")

    z_lo, x, core = lax.div(rp, 8), lax.rem(lax.div(rp, 2), 4), lax.rem(rp, 2)
    z_hi, y = lax.div(cp, 4), lax.rem(cp, 4)

    def row_at(step):
        return lax.rem(rp + step, NR)

    def col_at(step):
        return lax.rem(cp + step, NC)

    row_peer = {
        o: lax.rem(z_lo + o[0], 2) * 8 + lax.rem(x + o[1], 4) * 2 + lax.rem(core + o[2], 2) for o in ROW_STEPS
    }
    col_peer = {o: lax.rem(z_hi + o[0], 2) * 4 + lax.rem(y + o[1], 4) for o in COL_STEPS}

    waits = []

    def finish():
        for wait in waits:
            wait()

    barrier = pltpu.get_barrier_semaphore()
    for step in (1, NR - 1):
        pl.semaphore_signal(barrier, inc=1, device_id={"rows": row_at(step)})
    for step in (1, NC - 1):
        pl.semaphore_signal(barrier, inc=1, device_id={"cols": col_at(step)})

    rounds = (("rows", 1), ("rows", 2), ("rows", 4), ("cols", 1), ("cols", 2), ("cols", 4))

    def tell(which):
        axis, reach = rounds[which]
        count, at = (NR, row_at) if axis == "rows" else (NC, col_at)
        for step in sorted({reach, count - reach}):
            pl.semaphore_signal(ready_sem.at[which], inc=1, device_id={axis: at(step)})

    def told(which):
        axis, reach = rounds[which]
        pl.semaphore_wait(ready_sem.at[which], 1 if 2 * reach == NC and axis == "cols" else 2)

    loads = {}
    for at, (name, src, dst) in enumerate((
        ("diff", diff_h, diff), ("phases", phases_h, phases), ("spec", spec_h, spec),
        ("wr", base_rows_h, wr), ("turn_rows", turn_rows_h, turn_rows), ("trans", trans_h, trans),
        ("wc", base_cols_h, wc), ("turn_cols", turn_cols_h, turn_cols),
    )):
        loads[name] = pltpu.make_async_copy(src, dst, in_sem.at[at])
        loads[name].start()

    def remote(src, dst, at, device):
        return pltpu.make_async_remote_copy(
            src_ref=src, dst_ref=dst, send_sem=send_sem.at[at], recv_sem=recv_sem.at[at], device_id=device
        )

    def rows_exchange(src, dst, at):
        for step in ROW_STEPS[:-1]:
            peer = row_peer[step]
            remote(src.at[peer], dst.at[rp], at, {"rows": peer}).start()
        pltpu.make_async_copy(src.at[rp], dst.at[rp], recv_sem.at[at]).start()
        waits.append(lambda: sent(src.at[pl.ds(0, NR - 1)], at))

    def cols_exchange(src, dst, at):
        for step in COL_STEPS[:-1]:
            peer = col_peer[step]
            remote(src.at[peer], dst.at[cp], at, {"cols": peer}).start()
        pltpu.make_async_copy(src.at[cp], dst.at[cp], recv_sem.at[at]).start()
        waits.append(lambda: sent(src.at[pl.ds(0, NC - 1)], at))

    def tiles_kept(src, dst, at):
        pltpu.make_async_copy(src.at[cp, rp], dst.at[cp, rp], recv_sem.at[at]).start()
        waits.append(lambda: sent(src.at[pl.ds(0, NC - 1)], at))
        waits.append(lambda: sent(src.at[0, pl.ds(0, NR - 1)], at))

    def arrived(dst, at):
        pltpu.make_async_copy(dst, dst, recv_sem.at[at]).wait()

    def sent(src, at):
        pltpu.make_async_copy(src, src, send_sem.at[at]).wait()

    def halo_start(src, low, high, at):
        @pl.when(rp < NR - 1)
        def _():
            pltpu.make_async_remote_copy(
                src_ref=src, dst_ref=low, send_sem=halo_sem.at[at, 0], recv_sem=halo_sem.at[at, 1],
                device_id={"rows": rp + 1},
            ).start()

        @pl.when(rp > 0)
        def _():
            pltpu.make_async_remote_copy(
                src_ref=src, dst_ref=high, send_sem=halo_sem.at[at, 2], recv_sem=halo_sem.at[at, 3],
                device_id={"rows": rp - 1},
            ).start()

        waits.append(lambda: halo_sent(src, at))

    def halo_wait(low, high, at):
        @pl.when(rp < NR - 1)
        def _():
            pltpu.make_async_copy(high, high, halo_sem.at[at, 3]).wait()

        @pl.when(rp > 0)
        def _():
            pltpu.make_async_copy(low, low, halo_sem.at[at, 1]).wait()

    def halo_sent(src, at):
        @pl.when(rp < NR - 1)
        def _():
            pltpu.make_async_copy(src, src, halo_sem.at[at, 0]).wait()

        @pl.when(rp > 0)
        def _():
            pltpu.make_async_copy(src, src, halo_sem.at[at, 2]).wait()

    def iota(shape, axis):
        return lax.broadcasted_iota(jnp.int32, shape, axis)

    def one_hot(test):
        return jnp.where(test, 1.0, 0.0).astype(BF16)

    at_j, to_j = iota((128, 256), 0), iota((128, 256), 1)

    def banded(bounce):
        g = shifts[bounce]
        below = one_hot(to_j == at_j + 256 - g)
        above = one_hot(to_j == at_j + g - 128)
        for block in range(2):
            weights = [mask[block, m].astype(F32) for m in range(3)]
            for plane in range(2):
                left = (dot(diff[plane, block, 0], below) * weights[0]).astype(BF16)
                own = (diff[plane, block, 1].astype(F32) * weights[1]).astype(BF16)
                right = (dot(diff[plane, block, 2], above) * weights[2]).astype(BF16)
                nothing = jnp.zeros((128, 128), BF16)
                units = [left[:, :128], left[:, 128:], own, right[:, :128], right[:, 128:]]
                units = units + [nothing] if block == 0 else [nothing] + units
                for at, unit in enumerate(units):
                    which, col = at // 2, 128 * (at % 2)
                    row = 128 * block
                    if plane == 0:
                        dw[bounce, which, row:row + 128, col:col + 128] = unit
                        dw[bounce, which, 256 + row:384 + row, 256 + col:384 + col] = unit
                    else:
                        dw[bounce, which, 256 + row:384 + row, col:col + 128] = unit
                        dw[bounce, which, row:row + 128, 256 + col:384 + col] = -unit

    loads["diff"].wait()
    banded(0)

    @pl.when(rp == 0)
    def _():
        low0[...] = jnp.zeros_like(low0)
        low1[...] = jnp.zeros_like(low1)

    @pl.when(rp == NR - 1)
    def _():
        high0[...] = jnp.zeros_like(high0)
        high1[...] = jnp.zeros_like(high1)

    pl.semaphore_wait(barrier, 4)
    for h in range(CHUNKS):
        halo_start(spec_h.at[:, :, pl.ds(128 * h, 128)], low0.at[h], high0.at[h], h)
    tell(0)
    loads["phases"].wait()

    def phase0(at, _):
        rows = pl.ds(pl.multiple_of(at * 32, 32), 32)
        cosine, sine = cos_sin(phases[0, rows, :])
        trig0[0, rows, :] = cosine
        trig0[1, rows, :] = sine
        return 0

    lax.fori_loop(0, 3, phase0, 0)
    told(0)
    tell(1)
    lax.fori_loop(3, 6, phase0, 0)
    told(1)
    tell(2)
    lax.fori_loop(6, 8, phase0, 0)
    loads["spec"].wait()

    for h in range(CHUNKS):
        own0[h] = dot(dw[0, 1], spec[:, :, 128 * h:128 * h + 128].reshape(512, 128))
    for h in range(CHUNKS):
        halo_wait(low0.at[h], high0.at[h], h)
        cols = slice(128 * h, 128 * h + 128)
        total = own0[h] + dot(dw[0, 0], low0[h].reshape(512, 128))
        total = total + dot(dw[0, 2], high0[h].reshape(512, 128))
        cosine, sine = trig0[0, :, cols], trig0[1, :, cols]
        real, imag = total[:256], total[256:]
        wave_re = (real * cosine - imag * sine).astype(BF16)
        wave_im = (real * sine + imag * cosine).astype(BF16)
        sa1[h, :, :, 0:256] = wave_re.T.reshape(NR, 8, 256)
        sa1[h, :, :, 256:512] = wave_im.T.reshape(NR, 8, 256)
        if h == 0:
            told(2)
            tell(3)
        rows_exchange(sa1.at[h], rb1.at[h], 1 + h)

    told(3)
    tell(4)

    lane = iota((512, 512), 1)
    pick_cols[...] = one_hot(iota((512, 512), 0) == (lane & 31) * 16 + (lane >> 5))
    a, b = iota((256, 256), 0), iota((256, 256), 1)
    pick_rows[...] = one_hot(b == (a & 15) * 16 + (a >> 4))
    back_rows[...] = one_hot(b == (a & 1) * 128 + ((a & 15) >> 1) * 16 + (a >> 4))

    told(4)
    tell(5)
    loads["trans"].wait()
    for half in range(2):
        cols = pl.ds(half * 256, 256)
        picked = dot(trans[...].astype(BF16), pick_cols[:, cols]).astype(BF16)
        ts[:, :, :, cols] = dot(pick_rows[...], picked).astype(BF16).reshape(NC, 2, 16, 256)
    told(5)
    cols_exchange(ts, tr, 0)

    for name in ("wr", "wc", "turn_rows", "turn_cols"):
        loads[name].wait()

    lane128 = iota((1, 128), 1)

    def swap(first, second, size):
        even = (lane128 & size) == 0
        return (
            jnp.where(even, first, pltpu.roll(second, size, 1)),
            jnp.where(even, pltpu.roll(first, 128 - size, 1), second),
        )

    def crossed(values):
        reach = len(values) // 2
        while reach:
            size = reach * (128 // len(values))
            result = list(values)
            for at in range(len(values)):
                if at & reach == 0:
                    result[at], result[at + reach] = swap(values[at], values[at + reach], size)
            values = result
            reach //= 2
        return values

    def forward_rows(src, h):
        def first(at, _):
            half = pl.multiple_of(at * 128, 128)
            re, im = pl.ds(half, 128), pl.ds(half + 256, 128)
            values = [(src[p, :, re].astype(F32), src[p, :, im].astype(F32)) for p in range(NR)]
            values = butterfly(values, 1)
            for r in range(NR):
                real, imag = values[r]
                cosine, sine = turn_rows[0, r, :, re], turn_rows[1, r, :, re]
                work_b[r, :, re] = real * cosine - imag * sine
                work_b[r, :, im] = real * sine + imag * cosine
            return 0

        lax.fori_loop(0, 2, first, 0)
        rows = work_b[...].astype(BF16).reshape(128, 512)
        for part in range(2):
            lanes = slice(256 * part, 256 * part + 256)
            got = dot(rows, wr[:, lanes])
            work_z[:, 8 * h:8 * h + 8, lanes] = got.reshape(NR, 8, 256)

    def to_cols(send, recv, at):
        for half in range(2):
            def turn(g):
                block = work_z[2 * g + half].astype(BF16)
                block = jnp.concatenate([block[:, 128 * u:128 * u + 128] for u in range(4)], axis=0)
                send[half, g] = block.T.reshape(NR, 8, 128)

            turn(col_peer[COL_STEPS[0]])
            for number, col_step in enumerate(COL_STEPS):
                if number < NC - 1:
                    turn(col_peer[COL_STEPS[number + 1]])
                g = col_peer[col_step]
                for row_step in ROW_STEPS:
                    d = row_peer[row_step]
                    if any(row_step) or any(col_step):
                        device = {"rows": d, "cols": g}
                        remote(send.at[half, g, d], recv.at[half, cp, rp], at + half, device).start()
            tiles_kept(send.at[half], recv.at[half], at + half)

    def forward_cols(src):
        def first(at, _):
            lanes = pl.ds(pl.multiple_of(at * 128, 128), 128)
            lanes2 = pl.ds(pl.multiple_of(at * 128 + 256, 128), 128)
            for p in range(NC):
                parts = crossed([src[p, at * 8 + low].astype(F32) for low in range(8)])
                for k in range(8):
                    work_x[k // 4, k // 2 % 2, 2 * p + k % 2] = parts[k]
            for u in range(2):
                values = butterfly([(work_x[u, 0, p], work_x[u, 1, p]) for p in range(NR)], 1)
                for r in range(NR):
                    real, imag = values[r]
                    cosine, sine = turn_cols[0, r, :, lanes], turn_cols[1, r, :, lanes]
                    rows = slice(8 * u, 8 * u + 8)
                    work_d[r, rows, lanes] = real * cosine - imag * sine
                    work_d[r, rows, lanes2] = real * sine + imag * cosine
            return 0

        lax.fori_loop(0, 2, first, 0)

    def phase1(at, _):
        cols = pl.ds(pl.multiple_of(at * 128, 128), 128)
        cosine, sine = cos_sin(phases[1, :, cols])
        trig1[0, cols, :] = cosine.T
        trig1[1, cols, :] = sine.T
        return 0

    for h in range(CHUNKS):
        arrived(rb1.at[h], 1 + h)
        forward_rows(rb1.at[h], h)
    to_cols(sm1, rd1, 5)

    lax.fori_loop(0, 4, phase1, 0)
    banded(1)

    arrived(tr, 0)
    for e in range(2):
        for q in range(4):
            src = slice(128 * q, 128 * q + 128)
            got = crossed([tr[4 * e + k, :, :, src].reshape(32, 128).astype(F32) for k in range(4)])
            for k in range(4):
                tspace[:, 4 * q + k, :, 128 * e:128 * e + 128] = got[k].reshape(2, 16, 128)

    for half in range(2):
        arrived(rd1.at[half], 5 + half)
        forward_cols(rd1.at[half])
        rows = work_d[...].astype(BF16).reshape(256, 512)
        for part in range(2):
            lanes = slice(256 * part, 256 * part + 256)
            space = dot(rows, wc[:, lanes])
            work_s[:, lanes] = (space * tspace[half].reshape(256, 256)).astype(BF16)
        for part in range(2):
            lanes = slice(256 * part, 256 * part + 256)
            work_d[:, :, lanes] = dot_nt(work_s[...], wc[lanes, :]).reshape(NR, 16, 256)

        def last_cols(at):
            re = pl.ds(pl.multiple_of(at * 128, 128), 128)
            im = pl.ds(pl.multiple_of(at * 128 + 256, 128), 128)
            for u in range(2):
                values = []
                for r in range(NR):
                    real, imag = work_d[r, 8 * u:8 * u + 8, re], work_d[r, 8 * u:8 * u + 8, im]
                    cosine, sine = turn_cols[0, r, :, re], turn_cols[1, r, :, re]
                    values.append((real * cosine + imag * sine, imag * cosine - real * sine))
                values = butterfly(values, -1)
                for r in range(NR):
                    work_x[u, 0, r], work_x[u, 1, r] = values[r]
            for q in range(NC):
                tiles = crossed([work_x[k // 4, k // 2 % 2, 2 * q + k % 2] for k in range(8)])
                for low in range(8):
                    sm2[half, q, at * 8 + low] = tiles[low].astype(BF16)

        for other in (1, 0):
            last_cols(lax.rem(z_lo + other, 2))
            for row_step, col_step in PAIR_STEPS[:-1]:
                if row_step[0] == other:
                    d, g = row_peer[row_step], col_peer[col_step]
                    device = {"rows": d, "cols": g}
                    remote(sm2.at[half, g, d], rb2.at[half, cp, rp], 7 + half, device).start()
        tiles_kept(sm2.at[half], rb2.at[half], 7 + half)

    for half in range(2):
        arrived(rb2.at[half], 7 + half)

        def untile(g, _):
            block = rb2[half, g].reshape(128, 128).T
            for u in range(4):
                work_y[g, :, 128 * u:128 * u + 128] = block[32 * u:32 * u + 32]
            return 0

        lax.fori_loop(0, NC, untile, 0)
        for part in range(2):
            lanes = slice(256 * part, 256 * part + 256)
            got = dot_nt(work_y[...].reshape(256, 512), wr[lanes, :])
            work_r[half, :, :, lanes] = got.reshape(NC, 32, 256)
    for h in range(CHUNKS):
        crow = slice(8 * h, 8 * h + 8)

        def sources(at, _):
            half = pl.multiple_of(at * 128, 128)
            re, im = pl.ds(half, 128), pl.ds(half + 256, 128)
            values = []
            for r in range(NR):
                real, imag = work_r[r % 2, r // 2, crow, re], work_r[r % 2, r // 2, crow, im]
                cosine, sine = turn_rows[0, r, :, re], turn_rows[1, r, :, re]
                values.append((real * cosine + imag * sine, imag * cosine - real * sine))
            values = butterfly(values, -1)
            for r in range(NR):
                sb2[h, r, :, re] = values[r][0].astype(BF16)
                sb2[h, r, :, im] = values[r][1].astype(BF16)
            return 0

        lax.fori_loop(0, 2, sources, 0)
        rows_exchange(sb2.at[h], ra3.at[h], 9 + h)

    for h in range(CHUNKS):
        arrived(ra3.at[h], 9 + h)
        halo_start(ra3.at[h], low1.at[h], high1.at[h], CHUNKS + h)
        own1[h] = dot_nt(ra3[h].reshape(128, 512), dw[1, 1])

    for h in range(CHUNKS):
        halo_wait(low1.at[h], high1.at[h], CHUNKS + h)
        total = own1[h] + dot_nt(low1[h].reshape(128, 512), dw[1, 0])
        total = total + dot_nt(high1[h].reshape(128, 512), dw[1, 2])
        rows = slice(128 * h, 128 * h + 128)
        cosine, sine = trig1[0, rows, :], trig1[1, rows, :]
        real, imag = total[:, :256], total[:, 256:]
        sa3[h, :, :, 0:256] = (real * cosine - imag * sine).astype(BF16).reshape(NR, 8, 256)
        sa3[h, :, :, 256:512] = (real * sine + imag * cosine).astype(BF16).reshape(NR, 8, 256)
        rows_exchange(sa3.at[h], rb3.at[h], 13 + h)
    for h in range(CHUNKS):
        arrived(rb3.at[h], 13 + h)
        forward_rows(rb3.at[h], h)
    to_cols(sm3, rd3, 17)
    for half in range(2):
        arrived(rd3.at[half], 17 + half)
        forward_cols(rd3.at[half])
        rows = work_d[...].astype(BF16).reshape(256, 512)
        for plane in range(2):
            lanes = slice(256 * plane, 256 * plane + 256)
            work_d[:, :, lanes] = dot(rows, wc[:, lanes]).reshape(NR, 16, 256)
            for q in range(4):
                for e in range(2):
                    src = slice(256 * plane + 128 * e, 256 * plane + 128 * e + 128)
                    lanes_to = slice(512 * plane + 128 * q, 512 * plane + 128 * q + 128)
                    got = crossed([work_d[4 * q + k, :, src] for k in range(4)])
                    for k in range(4):
                        fs[half, 4 * e + k, :, lanes_to] = got[k].astype(BF16)
        cols_exchange(fs.at[half], rf.at[half], 19 + half)
    for half in range(2):
        arrived(rf.at[half], 19 + half)
        for plane in range(2):
            lanes = slice(512 * plane, 512 * plane + 512)
            ordered = dot_nt(rf[half, :, :, lanes].reshape(128, 512), pick_cols[...])
            work_o[plane, 128 * half:128 * half + 128, :] = ordered.astype(BF16)
            if half == 1:
                out[plane] = dot(back_rows[...], work_o[plane]).astype(BF16)
                result = pltpu.make_async_copy(out.at[plane], out_h.at[plane], in_sem.at[9 + plane])
                result.start()
                waits.append(result.wait)

    finish()


def on_device(spectrum, diffraction, order_mask, phases, transmission, shifts):
    anywhere = pl.BlockSpec(memory_space=pl.ANY)
    smem = pl.BlockSpec(memory_space=pltpu.SMEM)
    constants = tables()
    operands = (spectrum, diffraction, phases, transmission) + constants

    def vmem(kind, *shape):
        return pltpu.VMEM(shape, kind)

    halves = (CHUNKS, NR, 8, 512)
    space = pl.pallas_call(
        kernel,
        out_shape=jax.ShapeDtypeStruct((2, 256, 512), BF16),
        in_specs=[smem, smem] + [anywhere] * len(operands),
        out_specs=anywhere,
        scratch_shapes=[pltpu.VMEM(x.shape, x.dtype) for x in operands] + [
            vmem(BF16, 2, 256, 512),
            vmem(BF16, CHUNKS, 2, 256, 128), vmem(BF16, CHUNKS, 2, 256, 128),
            vmem(BF16, 2, 3, 512, 512),
            vmem(F32, 2, 256, 512),
            vmem(F32, 2, 512, 256),
            vmem(BF16, 512, 512), vmem(BF16, 256, 256), vmem(BF16, 256, 256),
            vmem(F32, 2, NR, 16, 256),
            vmem(F32, NR, 8, 512),
            vmem(F32, NR, 32, 512),
            vmem(BF16, NC, 32, 512),
            vmem(F32, 2, NC, 32, 512),
            vmem(F32, NR, 16, 512),
            vmem(BF16, 256, 512),
            vmem(F32, 2, 2, NR, 8, 128),
            vmem(BF16, 2, 256, 512),
            vmem(F32, CHUNKS, 512, 128), vmem(F32, CHUNKS, 128, 512),
            vmem(BF16, *halves), vmem(BF16, *halves),
            vmem(BF16, 2, NC, NR, 8, 128), vmem(BF16, 2, NC, NR, 8, 128),
            vmem(BF16, 2, NC, NR, 8, 128), vmem(BF16, 2, NC, NR, 8, 128),
            vmem(BF16, *halves), vmem(BF16, *halves),
            vmem(BF16, *halves), vmem(BF16, *halves),
            vmem(BF16, *halves), vmem(BF16, *halves),
            vmem(BF16, 2, NC, NR, 8, 128), vmem(BF16, 2, NC, NR, 8, 128),
            vmem(BF16, 2, NC, 16, 1024), vmem(BF16, 2, NC, 16, 1024),
            vmem(BF16, NC, 2, 16, 512), vmem(BF16, NC, 2, 16, 512),
            pltpu.SemaphoreType.DMA((11,)),
            pltpu.SemaphoreType.DMA((21,)),
            pltpu.SemaphoreType.DMA((21,)),
            pltpu.SemaphoreType.DMA((2 * CHUNKS, 4)),
            pltpu.SemaphoreType.REGULAR((6,)),
        ],
        compiler_params=pltpu.CompilerParams(
            collective_id=0, has_side_effects=True, vmem_limit_bytes=40 * 1024 * 1024
        ),
    )(shifts, order_mask, *operands)
    return space.astype(F32) * transmission[None]


def solution(mesh):
    placed = (
        P(None, "rows", "cols"),
        P(None, "rows", None, None, None),
        P("rows", None),
        P(None, "rows", "cols"),
        P("rows", "cols"),
        P(),
    )
    return jax.shard_map(
        on_device, mesh=mesh, in_specs=placed, out_specs=P(None, "rows", "cols"), check_vma=False
    )
```

```python
import math

import jax
import jax.numpy as jnp
import numpy as np
from jax import lax
from jax.experimental import pallas as pl
from jax.experimental.pallas import tpu as pltpu
from jax.sharding import PartitionSpec as P

F32 = jnp.float32
BF16 = jnp.bfloat16
NR = 16
NC = 8
FULL = 4096
CHUNKS = 4


def ring(step):
    return min(step, 4 - step)


def depth(high, low):
    return (0, 1, 2, 1)[2 * high + low]


ROW_STEPS = sorted(
    ((z, x, c) for z in range(2) for x in range(4) for c in range(2)),
    key=lambda o: -(8 * (o[0] + ring(o[1])) + o[2]),
)
COL_STEPS = sorted(
    ((z, y) for z in range(2) for y in range(4)), key=lambda o: -(2 * o[0] + ring(o[1]))
)
PAIR_STEPS = sorted(
    ((r, c) for r in ROW_STEPS for c in COL_STEPS),
    key=lambda p: -(8 * (depth(p[1][0], p[0][0]) + ring(p[0][1]) + ring(p[1][1])) + p[0][2]),
)


def tables():
    def circle(count, left, right):
        angle = 2.0 * np.pi * ((left[:, None] * right[None, :]) % count) / count
        return np.cos(angle), np.sin(angle)

    at = np.arange(512)
    row = 16 * (at // 8 % 16) + 8 * (at // 256) + at % 8
    imaginary = at // 128 % 2 == 1
    c, s = circle(256, np.arange(256), row)
    base_rows = np.concatenate([np.where(imaginary, s, c), np.where(imaginary, c, -s)]) / 64.0
    at = np.arange(256)
    col = 128 * (at // 8 % 2) + 64 * (at // 128) + 8 * (at // 16 % 8) + at % 8
    c, s = circle(256, col, np.arange(256))
    base_cols = np.block([[c, s], [-s, c]]) / 64.0
    turn_rows = np.stack(circle(FULL, np.arange(NR), np.arange(256)))[:, :, None, :]
    turn_cols = np.stack(circle(FULL, np.arange(NR), col))[:, :, None, :]
    return (
        jnp.asarray(base_rows, BF16),
        jnp.asarray(base_cols, BF16),
        jnp.asarray(turn_rows, F32),
        jnp.asarray(turn_cols, F32),
    )


def times_unit(value, numerator, count, sign):
    real, imag = value
    step = (numerator * 8) % (count * 8)
    eighth, rest = divmod(step, count)
    if rest == 0 and eighth % 2 == 0:
        quarter = (eighth // 2) % 4
        if quarter == 0:
            return real, imag
        if quarter == 2:
            return -real, -imag
        if (quarter == 1) == (sign > 0):
            return -imag, real
        return imag, -real
    angle = 2.0 * math.pi * numerator / count
    cosine, sine = math.cos(angle), sign * math.sin(angle)
    if rest == 0:
        half = abs(cosine)
        a = (real - imag) if cosine * sine > 0 else (real + imag)
        b = (real + imag) if cosine * sine > 0 else (imag - real)
        if cosine < 0:
            return a * (-half), b * (-half)
        return a * half, b * half
    return real * cosine - imag * sine, real * sine + imag * cosine


def butterfly(values, sign):
    count = len(values)
    if count == 1:
        return values
    even = butterfly(values[0::2], sign)
    odd = butterfly(values[1::2], sign)
    low, high = [], []
    for at in range(count // 2):
        er, ei = even[at]
        tr, ti = times_unit(odd[at], at, count, sign)
        low.append((er + tr, ei + ti))
        high.append((er - tr, ei - ti))
    return low + high


def cos_sin(angle):
    half = angle * 0.5
    square = half * half
    sine = -2.5052108e-08
    for factor in (2.7557319e-06, -1.9841270e-04, 8.3333333e-03, -1.6666667e-01, 1.0):
        sine = sine * square + factor
    sine = sine * half
    cosine = 2.0876757e-09
    for factor in (-2.7557319e-07, 2.4801587e-05, -1.3888889e-03, 4.1666667e-02, -0.5, 1.0):
        cosine = cosine * square + factor
    return 1.0 - 2.0 * (sine * sine), 2.0 * (sine * cosine)


def dot(a, b):
    return jnp.dot(a, b, preferred_element_type=F32)


def dot_nt(a, b):
    return lax.dot_general(a, b, (((1,), (1,)), ((), ())), preferred_element_type=F32)


def kernel(
    shifts, mask, spec_h, diff_h, phases_h, trans_h, base_rows_h, base_cols_h, turn_rows_h, turn_cols_h, out_h,
    spec, diff, phases, trans, wr, wc, turn_rows, turn_cols, out,
    low0, high0, dw, trig0, trig1, pick_cols, pick_rows, back_rows, tspace,
    work_b, work_z, work_y, work_r, work_d, work_s, work_x, work_o, own0, own1,
    sa1, rb1, sm1, rd1, sm2, rb2, sb2, ra3, low1, high1, sa3, rb3, sm3, rd3, fs, rf, ts, tr,
    in_sem, send_sem, recv_sem, halo_sem, ready_sem,
):
    rp = lax.axis_index("rows")
    cp = lax.axis_index("cols")

    z_lo, x, core = lax.div(rp, 8), lax.rem(lax.div(rp, 2), 4), lax.rem(rp, 2)
    z_hi, y = lax.div(cp, 4), lax.rem(cp, 4)

    def row_at(step):
        return lax.rem(rp + step, NR)

    def col_at(step):
        return lax.rem(cp + step, NC)

    row_peer = {
        o: lax.rem(z_lo + o[0], 2) * 8 + lax.rem(x + o[1], 4) * 2 + lax.rem(core + o[2], 2) for o in ROW_STEPS
    }
    col_peer = {o: lax.rem(z_hi + o[0], 2) * 4 + lax.rem(y + o[1], 4) for o in COL_STEPS}

    waits = []

    def finish():
        for wait in waits:
            wait()

    barrier = pltpu.get_barrier_semaphore()
    for step in (1, NR - 1):
        pl.semaphore_signal(barrier, inc=1, device_id={"rows": row_at(step)})
    for step in (1, NC - 1):
        pl.semaphore_signal(barrier, inc=1, device_id={"cols": col_at(step)})

    rounds = (("rows", 1), ("rows", 2), ("rows", 4), ("cols", 1), ("cols", 2), ("cols", 4))

    def tell(which):
        axis, reach = rounds[which]
        count, at = (NR, row_at) if axis == "rows" else (NC, col_at)
        for step in sorted({reach, count - reach}):
            pl.semaphore_signal(ready_sem.at[which], inc=1, device_id={axis: at(step)})

    def told(which):
        axis, reach = rounds[which]
        pl.semaphore_wait(ready_sem.at[which], 1 if 2 * reach == NC and axis == "cols" else 2)

    loads = {}
    for at, (name, src, dst) in enumerate((
        ("diff", diff_h, diff), ("phases", phases_h, phases), ("spec", spec_h, spec),
        ("wr", base_rows_h, wr), ("turn_rows", turn_rows_h, turn_rows), ("trans", trans_h, trans),
        ("wc", base_cols_h, wc), ("turn_cols", turn_cols_h, turn_cols),
    )):
        loads[name] = pltpu.make_async_copy(src, dst, in_sem.at[at])
        loads[name].start()

    def remote(src, dst, at, device):
        return pltpu.make_async_remote_copy(
            src_ref=src, dst_ref=dst, send_sem=send_sem.at[at], recv_sem=recv_sem.at[at], device_id=device
        )

    def rows_exchange(src, dst, at):
        for step in ROW_STEPS[:-1]:
            peer = row_peer[step]
            remote(src.at[peer], dst.at[rp], at, {"rows": peer}).start()
        pltpu.make_async_copy(src.at[rp], dst.at[rp], recv_sem.at[at]).start()
        waits.append(lambda: sent(src.at[pl.ds(0, NR - 1)], at))

    def cols_exchange(src, dst, at):
        for step in COL_STEPS[:-1]:
            peer = col_peer[step]
            remote(src.at[peer], dst.at[cp], at, {"cols": peer}).start()
        pltpu.make_async_copy(src.at[cp], dst.at[cp], recv_sem.at[at]).start()
        waits.append(lambda: sent(src.at[pl.ds(0, NC - 1)], at))

    def tiles_kept(src, dst, at):
        pltpu.make_async_copy(src.at[cp, rp], dst.at[cp, rp], recv_sem.at[at]).start()
        waits.append(lambda: sent(src.at[pl.ds(0, NC - 1)], at))
        waits.append(lambda: sent(src.at[0, pl.ds(0, NR - 1)], at))

    def arrived(dst, at):
        pltpu.make_async_copy(dst, dst, recv_sem.at[at]).wait()

    def sent(src, at):
        pltpu.make_async_copy(src, src, send_sem.at[at]).wait()

    def halo_start(src, low, high, at):
        @pl.when(rp < NR - 1)
        def _():
            pltpu.make_async_remote_copy(
                src_ref=src, dst_ref=low, send_sem=halo_sem.at[at, 0], recv_sem=halo_sem.at[at, 1],
                device_id={"rows": rp + 1},
            ).start()

        @pl.when(rp > 0)
        def _():
            pltpu.make_async_remote_copy(
                src_ref=src, dst_ref=high, send_sem=halo_sem.at[at, 2], recv_sem=halo_sem.at[at, 3],
                device_id={"rows": rp - 1},
            ).start()

        waits.append(lambda: halo_sent(src, at))

    def halo_wait(low, high, at):
        @pl.when(rp < NR - 1)
        def _():
            pltpu.make_async_copy(high, high, halo_sem.at[at, 3]).wait()

        @pl.when(rp > 0)
        def _():
            pltpu.make_async_copy(low, low, halo_sem.at[at, 1]).wait()

    def halo_sent(src, at):
        @pl.when(rp < NR - 1)
        def _():
            pltpu.make_async_copy(src, src, halo_sem.at[at, 0]).wait()

        @pl.when(rp > 0)
        def _():
            pltpu.make_async_copy(src, src, halo_sem.at[at, 2]).wait()

    def iota(shape, axis):
        return lax.broadcasted_iota(jnp.int32, shape, axis)

    def one_hot(test):
        return jnp.where(test, 1.0, 0.0).astype(BF16)

    at_j, to_j = iota((128, 256), 0), iota((128, 256), 1)

    def banded(bounce):
        g = shifts[bounce]
        below = one_hot(to_j == at_j + 256 - g)
        above = one_hot(to_j == at_j + g - 128)
        for block in range(2):
            weights = [mask[block, m].astype(F32) for m in range(3)]
            for plane in range(2):
                left = (dot(diff[plane, block, 0], below) * weights[0]).astype(BF16)
                own = (diff[plane, block, 1].astype(F32) * weights[1]).astype(BF16)
                right = (dot(diff[plane, block, 2], above) * weights[2]).astype(BF16)
                nothing = jnp.zeros((128, 128), BF16)
                units = [left[:, :128], left[:, 128:], own, right[:, :128], right[:, 128:]]
                units = units + [nothing] if block == 0 else [nothing] + units
                for at, unit in enumerate(units):
                    which, col = at // 2, 128 * (at % 2)
                    row = 128 * block
                    if plane == 0:
                        dw[bounce, which, row:row + 128, col:col + 128] = unit
                        dw[bounce, which, 256 + row:384 + row, 256 + col:384 + col] = unit
                    else:
                        dw[bounce, which, 256 + row:384 + row, col:col + 128] = unit
                        dw[bounce, which, row:row + 128, 256 + col:384 + col] = -unit

    loads["diff"].wait()
    banded(0)

    @pl.when(rp == 0)
    def _():
        low0[...] = jnp.zeros_like(low0)
        low1[...] = jnp.zeros_like(low1)

    @pl.when(rp == NR - 1)
    def _():
        high0[...] = jnp.zeros_like(high0)
        high1[...] = jnp.zeros_like(high1)

    pl.semaphore_wait(barrier, 4)
    for h in range(CHUNKS):
        halo_start(spec_h.at[:, :, pl.ds(128 * h, 128)], low0.at[h], high0.at[h], h)
    tell(0)
    loads["phases"].wait()

    def phase0(at, _):
        rows = pl.ds(pl.multiple_of(at * 32, 32), 32)
        cosine, sine = cos_sin(phases[0, rows, :])
        trig0[0, rows, :] = cosine
        trig0[1, rows, :] = sine
        return 0

    lax.fori_loop(0, 3, phase0, 0)
    told(0)
    tell(1)
    lax.fori_loop(3, 6, phase0, 0)
    told(1)
    tell(2)
    lax.fori_loop(6, 8, phase0, 0)
    loads["spec"].wait()

    for h in range(CHUNKS):
        own0[h] = dot(dw[0, 1], spec[:, :, 128 * h:128 * h + 128].reshape(512, 128))
    for h in range(CHUNKS):
        halo_wait(low0.at[h], high0.at[h], h)
        cols = slice(128 * h, 128 * h + 128)
        total = own0[h] + dot(dw[0, 0], low0[h].reshape(512, 128))
        total = total + dot(dw[0, 2], high0[h].reshape(512, 128))
        cosine, sine = trig0[0, :, cols], trig0[1, :, cols]
        real, imag = total[:256], total[256:]
        wave_re = (real * cosine - imag * sine).astype(BF16)
        wave_im = (real * sine + imag * cosine).astype(BF16)
        sa1[h, :, :, 0:256] = wave_re.T.reshape(NR, 8, 256)
        sa1[h, :, :, 256:512] = wave_im.T.reshape(NR, 8, 256)
        if h == 0:
            told(2)
            tell(3)
        rows_exchange(sa1.at[h], rb1.at[h], 1 + h)

    told(3)
    tell(4)

    lane = iota((512, 512), 1)
    pick_cols[...] = one_hot(iota((512, 512), 0) == (lane & 31) * 16 + (lane >> 5))
    a, b = iota((256, 256), 0), iota((256, 256), 1)
    pick_rows[...] = one_hot(b == (a & 15) * 16 + (a >> 4))
    back_rows[...] = one_hot(b == (a & 1) * 128 + ((a & 15) >> 1) * 16 + (a >> 4))

    told(4)
    tell(5)
    loads["trans"].wait()
    for half in range(2):
        cols = pl.ds(half * 256, 256)
        picked = dot(trans[...].astype(BF16), pick_cols[:, cols]).astype(BF16)
        ts[:, :, :, cols] = dot(pick_rows[...], picked).astype(BF16).reshape(NC, 2, 16, 256)
    told(5)
    cols_exchange(ts, tr, 0)

    for name in ("wr", "wc", "turn_rows", "turn_cols"):
        loads[name].wait()

    lane128 = iota((1, 128), 1)

    def swap(first, second, size):
        even = (lane128 & size) == 0
        return (
            jnp.where(even, first, pltpu.roll(second, size, 1)),
            jnp.where(even, pltpu.roll(first, 128 - size, 1), second),
        )

    def crossed(values):
        reach = len(values) // 2
        while reach:
            size = reach * (128 // len(values))
            result = list(values)
            for at in range(len(values)):
                if at & reach == 0:
                    result[at], result[at + reach] = swap(values[at], values[at + reach], size)
            values = result
            reach //= 2
        return values

    def forward_rows(src, h):
        def first(at, _):
            half = pl.multiple_of(at * 128, 128)
            re, im = pl.ds(half, 128), pl.ds(half + 256, 128)
            values = [(src[p, :, re].astype(F32), src[p, :, im].astype(F32)) for p in range(NR)]
            values = butterfly(values, 1)
            for r in range(NR):
                real, imag = values[r]
                cosine, sine = turn_rows[0, r, :, re], turn_rows[1, r, :, re]
                work_b[r, :, re] = real * cosine - imag * sine
                work_b[r, :, im] = real * sine + imag * cosine
            return 0

        lax.fori_loop(0, 2, first, 0)
        rows = work_b[...].astype(BF16).reshape(128, 512)
        for part in range(2):
            lanes = slice(256 * part, 256 * part + 256)
            got = dot(rows, wr[:, lanes])
            work_z[:, 8 * h:8 * h + 8, lanes] = got.reshape(NR, 8, 256)

    def to_cols(send, recv, at):
        for half in range(2):
            def turn(g):
                block = work_z[2 * g + half].astype(BF16)
                block = jnp.concatenate([block[:, 128 * u:128 * u + 128] for u in range(4)], axis=0)
                send[half, g] = block.T.reshape(NR, 8, 128)

            turn(col_peer[COL_STEPS[0]])
            for number, col_step in enumerate(COL_STEPS):
                if number < NC - 1:
                    turn(col_peer[COL_STEPS[number + 1]])
                g = col_peer[col_step]
                for row_step in ROW_STEPS:
                    d = row_peer[row_step]
                    if any(row_step) or any(col_step):
                        device = {"rows": d, "cols": g}
                        remote(send.at[half, g, d], recv.at[half, cp, rp], at + half, device).start()
            tiles_kept(send.at[half], recv.at[half], at + half)

    def forward_cols(src):
        def first(at, _):
            lanes = pl.ds(pl.multiple_of(at * 128, 128), 128)
            lanes2 = pl.ds(pl.multiple_of(at * 128 + 256, 128), 128)
            for p in range(NC):
                parts = crossed([src[p, at * 8 + low].astype(F32) for low in range(8)])
                for k in range(8):
                    work_x[k // 4, k // 2 % 2, 2 * p + k % 2] = parts[k]
            for u in range(2):
                values = butterfly([(work_x[u, 0, p], work_x[u, 1, p]) for p in range(NR)], 1)
                for r in range(NR):
                    real, imag = values[r]
                    cosine, sine = turn_cols[0, r, :, lanes], turn_cols[1, r, :, lanes]
                    rows = slice(8 * u, 8 * u + 8)
                    work_d[r, rows, lanes] = real * cosine - imag * sine
                    work_d[r, rows, lanes2] = real * sine + imag * cosine
            return 0

        lax.fori_loop(0, 2, first, 0)

    def phase1(at, _):
        cols = pl.ds(pl.multiple_of(at * 128, 128), 128)
        cosine, sine = cos_sin(phases[1, :, cols])
        trig1[0, cols, :] = cosine.T
        trig1[1, cols, :] = sine.T
        return 0

    for h in range(CHUNKS):
        arrived(rb1.at[h], 1 + h)
        forward_rows(rb1.at[h], h)
    to_cols(sm1, rd1, 5)

    lax.fori_loop(0, 4, phase1, 0)
    banded(1)

    arrived(tr, 0)
    for e in range(2):
        for q in range(4):
            src = slice(128 * q, 128 * q + 128)
            got = crossed([tr[4 * e + k, :, :, src].reshape(32, 128).astype(F32) for k in range(4)])
            for k in range(4):
                tspace[:, 4 * q + k, :, 128 * e:128 * e + 128] = got[k].reshape(2, 16, 128)

    for half in range(2):
        arrived(rd1.at[half], 5 + half)
        forward_cols(rd1.at[half])
        rows = work_d[...].astype(BF16).reshape(256, 512)
        for part in range(2):
            lanes = slice(256 * part, 256 * part + 256)
            space = dot(rows, wc[:, lanes])
            work_s[:, lanes] = (space * tspace[half].reshape(256, 256)).astype(BF16)
        for part in range(2):
            lanes = slice(256 * part, 256 * part + 256)
            work_d[:, :, lanes] = dot_nt(work_s[...], wc[lanes, :]).reshape(NR, 16, 256)

        def last_cols(at):
            re, im = slice(128 * at, 128 * at + 128), slice(128 * at + 256, 128 * at + 384)
            for u in range(2):
                values = []
                for r in range(NR):
                    real, imag = work_d[r, 8 * u:8 * u + 8, re], work_d[r, 8 * u:8 * u + 8, im]
                    cosine, sine = turn_cols[0, r, :, re], turn_cols[1, r, :, re]
                    values.append((real * cosine + imag * sine, imag * cosine - real * sine))
                values = butterfly(values, -1)
                for r in range(NR):
                    work_x[u, 0, r], work_x[u, 1, r] = values[r]
            for q in range(NC):
                tiles = crossed([work_x[k // 4, k // 2 % 2, 2 * q + k % 2] for k in range(8)])
                for low in range(8):
                    sm2[half, q, at * 8 + low] = tiles[low].astype(BF16)

        for at in range(2):
            last_cols(at)
        for row_step, col_step in PAIR_STEPS[:-1]:
            d, g = row_peer[row_step], col_peer[col_step]
            remote(sm2.at[half, g, d], rb2.at[half, cp, rp], 7 + half, {"rows": d, "cols": g}).start()
        tiles_kept(sm2.at[half], rb2.at[half], 7 + half)

    for half in range(2):
        arrived(rb2.at[half], 7 + half)

        def untile(g, _):
            block = rb2[half, g].reshape(128, 128).T
            for u in range(4):
                work_y[g, :, 128 * u:128 * u + 128] = block[32 * u:32 * u + 32]
            return 0

        lax.fori_loop(0, NC, untile, 0)
        for part in range(2):
            lanes = slice(256 * part, 256 * part + 256)
            got = dot_nt(work_y[...].reshape(256, 512), wr[lanes, :])
            work_r[half, :, :, lanes] = got.reshape(NC, 32, 256)
    for h in range(CHUNKS):
        crow = slice(8 * h, 8 * h + 8)

        def sources(at, _):
            half = pl.multiple_of(at * 128, 128)
            re, im = pl.ds(half, 128), pl.ds(half + 256, 128)
            values = []
            for r in range(NR):
                real, imag = work_r[r % 2, r // 2, crow, re], work_r[r % 2, r // 2, crow, im]
                cosine, sine = turn_rows[0, r, :, re], turn_rows[1, r, :, re]
                values.append((real * cosine + imag * sine, imag * cosine - real * sine))
            values = butterfly(values, -1)
            for r in range(NR):
                sb2[h, r, :, re] = values[r][0].astype(BF16)
                sb2[h, r, :, im] = values[r][1].astype(BF16)
            return 0

        lax.fori_loop(0, 2, sources, 0)
        rows_exchange(sb2.at[h], ra3.at[h], 9 + h)

    for h in range(CHUNKS):
        arrived(ra3.at[h], 9 + h)
        halo_start(ra3.at[h], low1.at[h], high1.at[h], CHUNKS + h)
        own1[h] = dot_nt(ra3[h].reshape(128, 512), dw[1, 1])

    for h in range(CHUNKS):
        halo_wait(low1.at[h], high1.at[h], CHUNKS + h)
        total = own1[h] + dot_nt(low1[h].reshape(128, 512), dw[1, 0])
        total = total + dot_nt(high1[h].reshape(128, 512), dw[1, 2])
        rows = slice(128 * h, 128 * h + 128)
        cosine, sine = trig1[0, rows, :], trig1[1, rows, :]
        real, imag = total[:, :256], total[:, 256:]
        sa3[h, :, :, 0:256] = (real * cosine - imag * sine).astype(BF16).reshape(NR, 8, 256)
        sa3[h, :, :, 256:512] = (real * sine + imag * cosine).astype(BF16).reshape(NR, 8, 256)
        rows_exchange(sa3.at[h], rb3.at[h], 13 + h)
    for h in range(CHUNKS):
        arrived(rb3.at[h], 13 + h)
        forward_rows(rb3.at[h], h)
    to_cols(sm3, rd3, 17)
    for half in range(2):
        arrived(rd3.at[half], 17 + half)
        forward_cols(rd3.at[half])
        rows = work_d[...].astype(BF16).reshape(256, 512)
        for plane in range(2):
            lanes = slice(256 * plane, 256 * plane + 256)
            work_d[:, :, lanes] = dot(rows, wc[:, lanes]).reshape(NR, 16, 256)
            for q in range(4):
                for e in range(2):
                    src = slice(256 * plane + 128 * e, 256 * plane + 128 * e + 128)
                    lanes_to = slice(512 * plane + 128 * q, 512 * plane + 128 * q + 128)
                    got = crossed([work_d[4 * q + k, :, src] for k in range(4)])
                    for k in range(4):
                        fs[half, 4 * e + k, :, lanes_to] = got[k].astype(BF16)
        cols_exchange(fs.at[half], rf.at[half], 19 + half)
    for half in range(2):
        arrived(rf.at[half], 19 + half)
        for plane in range(2):
            lanes = slice(512 * plane, 512 * plane + 512)
            ordered = dot_nt(rf[half, :, :, lanes].reshape(128, 512), pick_cols[...])
            work_o[plane, 128 * half:128 * half + 128, :] = ordered.astype(BF16)
            if half == 1:
                out[plane] = dot(back_rows[...], work_o[plane]).astype(BF16)
                result = pltpu.make_async_copy(out.at[plane], out_h.at[plane], in_sem.at[9 + plane])
                result.start()
                waits.append(result.wait)

    finish()


def on_device(spectrum, diffraction, order_mask, phases, transmission, shifts):
    anywhere = pl.BlockSpec(memory_space=pl.ANY)
    smem = pl.BlockSpec(memory_space=pltpu.SMEM)
    constants = tables()
    operands = (spectrum, diffraction, phases, transmission) + constants

    def vmem(kind, *shape):
        return pltpu.VMEM(shape, kind)

    halves = (CHUNKS, NR, 8, 512)
    space = pl.pallas_call(
        kernel,
        out_shape=jax.ShapeDtypeStruct((2, 256, 512), BF16),
        in_specs=[smem, smem] + [anywhere] * len(operands),
        out_specs=anywhere,
        scratch_shapes=[pltpu.VMEM(x.shape, x.dtype) for x in operands] + [
            vmem(BF16, 2, 256, 512),
            vmem(BF16, CHUNKS, 2, 256, 128), vmem(BF16, CHUNKS, 2, 256, 128),
            vmem(BF16, 2, 3, 512, 512),
            vmem(F32, 2, 256, 512),
            vmem(F32, 2, 512, 256),
            vmem(BF16, 512, 512), vmem(BF16, 256, 256), vmem(BF16, 256, 256),
            vmem(F32, 2, NR, 16, 256),
            vmem(F32, NR, 8, 512),
            vmem(F32, NR, 32, 512),
            vmem(BF16, NC, 32, 512),
            vmem(F32, 2, NC, 32, 512),
            vmem(F32, NR, 16, 512),
            vmem(BF16, 256, 512),
            vmem(F32, 2, 2, NR, 8, 128),
            vmem(BF16, 2, 256, 512),
            vmem(F32, CHUNKS, 512, 128), vmem(F32, CHUNKS, 128, 512),
            vmem(BF16, *halves), vmem(BF16, *halves),
            vmem(BF16, 2, NC, NR, 8, 128), vmem(BF16, 2, NC, NR, 8, 128),
            vmem(BF16, 2, NC, NR, 8, 128), vmem(BF16, 2, NC, NR, 8, 128),
            vmem(BF16, *halves), vmem(BF16, *halves),
            vmem(BF16, *halves), vmem(BF16, *halves),
            vmem(BF16, *halves), vmem(BF16, *halves),
            vmem(BF16, 2, NC, NR, 8, 128), vmem(BF16, 2, NC, NR, 8, 128),
            vmem(BF16, 2, NC, 16, 1024), vmem(BF16, 2, NC, 16, 1024),
            vmem(BF16, NC, 2, 16, 512), vmem(BF16, NC, 2, 16, 512),
            pltpu.SemaphoreType.DMA((11,)),
            pltpu.SemaphoreType.DMA((21,)),
            pltpu.SemaphoreType.DMA((21,)),
            pltpu.SemaphoreType.DMA((2 * CHUNKS, 4)),
            pltpu.SemaphoreType.REGULAR((6,)),
        ],
        compiler_params=pltpu.CompilerParams(
            collective_id=0, has_side_effects=True, vmem_limit_bytes=40 * 1024 * 1024
        ),
    )(shifts, order_mask, *operands)
    return space.astype(F32) * transmission[None]


def solution(mesh):
    placed = (
        P(None, "rows", "cols"),
        P(None, "rows", None, None, None),
        P("rows", None),
        P(None, "rows", "cols"),
        P("rows", "cols"),
        P(),
    )
    return jax.shard_map(
        on_device, mesh=mesh, in_specs=placed, out_specs=P(None, "rows", "cols"), check_vma=False
    )
```
